32 devices in a mesh: gx: 4 (over z), gy: 4 (over y, x), gz: 2 (over core).
Axes of the slice: x: 2, y: 2, z: 4, core: 2. Of those that a mesh axis runs over, the one named last changes fastest.
Arguments:
- old_state: float32 [5, 64, 16384], P(None, None, ('gx', 'gy', 'gz')), may hold values from -0.5 to 3.5, as said below
- element_size: float32 [8192], P(('gx', 'gy', 'gz')), may hold values from 0.5 to 2
- old_start: int32 [33], replicated, may hold values from 0 to 8192, as said below
- neighbour: int32 [6, 8192], P(None, ('gx', 'gy', 'gz')), may hold values from 0 to 8191, as said below
- orientation: int32 [6, 8192], P(None, ('gx', 'gy', 'gz')), may hold values from 0 to 7
Outputs:
- final_state: float32 [5, 64, 8192], P(None, None, ('gx', 'gy', 'gz'))
The draws below stay inside these ranges and needn't reach their ends.
Inputs may be any that keep to these rules, and one draw needn't show every extreme that they name: `old_state`: A gas with density and pressure between 0.85 and 1.15 and each velocity component below 0.3 in magnitude at every node, in conserved form. old_start[0] is 0 and old_start[32] is 8192; old_start[d] differs from d * 256 by at most 128, so a device's old range holds at most 512 elements. `neighbour`: after repartitioning, the element behind a face is owned by the owner of the element itself or by the device just before or just after it along the curve, counted cyclically; of the 1536 faces of each device's elements exactly 32 lead to the device before and exactly 32 to the device after.
All inputs are finite; a program needn't handle non-finite values.
Results may differ from the reference program's by a relative error of at most 0.0001.
Values sent between devices are 32-bit elements; how exact they have to be, the bound alone decides.
No kernel may reach another device: no remote copies, remote signals or barrier semaphores. Data moves between devices by JAX's collectives and lax.ppermute only.
A program may use at most 128 MiB of HBM per device.

```python
import math
import jax
import jax.numpy as jnp
import numpy as np
from jax import lax

NODES = 64
E_DEV = 256
HALF = 128
REMOTE = 32
OLD_CAP = 512
RANKS = 32
TOTAL = 8192


def draw_old_state(key, part):
    slots = RANKS * OLD_CAP
    shape = (NODES, slots)
    streams = jax.random.split(key, 6)
    mean_density = jax.random.uniform(streams[0], (slots,), jnp.float32, 0.9, 1.1)
    mean_speed = jax.random.uniform(streams[1], (3, slots), jnp.float32, -0.2, 0.2)
    mean_pressure = jax.random.uniform(streams[2], (slots,), jnp.float32, 0.9, 1.1)
    density = mean_density[None] * jax.random.uniform(streams[3], shape, jnp.float32, 0.96, 1.04)
    speeds = mean_speed[:, None, :] + jax.random.uniform(streams[4], (3,) + shape, jnp.float32, -0.05, 0.05)
    pressure = mean_pressure[None] * jax.random.uniform(streams[5], shape, jnp.float32, 0.96, 1.04)
    momenta = density[None] * speeds
    energy = pressure / 0.4 + 0.5 * density * jnp.sum(speeds * speeds, axis=0)
    return jnp.concatenate([density[None], momenta, energy[None]], axis=0)


def draw_old_start(key, part):
    streams = jax.random.split(key, 2)
    drift = jax.random.randint(streams[0], (RANKS + 1,), -HALF, HALF + 1)
    pivot = jax.random.randint(streams[1], (), 1, RANKS - 1)
    places = jnp.arange(RANKS + 1, dtype=jnp.int32)
    drift = jnp.where(places == pivot, -HALF, drift)
    drift = jnp.where(places == pivot + 1, HALF, drift)
    drift = jnp.where((places == 0) | (places == RANKS), 0, drift)
    return (places * E_DEV + drift).astype(jnp.int32)


def draw_neighbour(key, part):
    streams = jax.random.split(key, 2)
    face_count = 6 * E_DEV

    def device_offsets(device):
        order = jax.random.permutation(jax.random.fold_in(streams[0], device), face_count)
        offset = jnp.zeros((face_count,), jnp.int32)
        offset = offset.at[order[:REMOTE]].set(-1)
        offset = offset.at[order[REMOTE:2 * REMOTE]].set(1)
        return offset.reshape(6, E_DEV)
    offsets = jax.vmap(device_offsets)(jnp.arange(RANKS, dtype=jnp.int32))
    offsets = offsets.transpose(1, 0, 2).reshape(6, TOTAL)
    curve_index = jnp.arange(TOTAL, dtype=jnp.int32)
    owners = (curve_index // E_DEV)[None, :]
    target = (owners + offsets + RANKS) % RANKS
    slots = jax.random.randint(streams[1], (6, TOTAL), 0, E_DEV)
    return (target * E_DEV + slots).astype(jnp.int32)


def plant(values, own_key, low, top_value):
    shape = values.shape
    spot = [jax.random.randint(jax.random.fold_in(own_key, axis), (), 0, shape[axis]) for axis in range(len(shape))]
    values = values.at[tuple(spot)].set(low)
    longest = shape.index(max(shape))
    spot[longest] = (spot[longest] + 1) % shape[longest]
    return values.at[tuple(spot)].set(top_value)


def steps_of(own_key, extent, cuts, low, largest):
    level = 1.0
    for dim, parts in cuts:
        draws = jax.random.uniform(jax.random.fold_in(jax.random.fold_in(own_key, 6), dim), (parts,), jnp.float32, low / len(cuts), largest / len(cuts))
        level = level * jnp.repeat(jnp.exp(draws), extent[dim] // parts).reshape((-1,) + (1,) * (len(extent) - 1 - dim))
    return level


def setup_inputs(seed: int = 0) -> dict:
    key_of = jax.random.split(jax.random.key(seed), 6)
    return {
        "old_state": draw_old_state(jax.random.fold_in(key_of[5], 71), 0),
        "element_size": jnp.clip(jnp.exp(math.log(2.0) - 1.3862944 * jax.random.uniform(key_of[1], (TOTAL,), jnp.float32) ** steps_of(key_of[1], (TOTAL,), ((0, 32),), -0.2, 0.2)), 0.5, 2.0),
        "old_start": draw_old_start(jax.random.fold_in(key_of[5], 71), 0),
        "neighbour": draw_neighbour(jax.random.fold_in(key_of[5], 71), 0),
        "orientation": plant(jax.random.randint(key_of[4], (6, TOTAL), 0, 8), jax.random.fold_in(key_of[4], 1), 0, 7).astype(jnp.int32),
    }


GAMMA = 1.4
TIME_STEP = 0.03
LIFT = 6.0
HIGHEST = lax.Precision.HIGHEST

def gll_derivative():
    points = np.array([-1.0, -1.0 / np.sqrt(5.0), 1.0 / np.sqrt(5.0), 1.0])
    barycentric = np.array([1.0 / np.prod([points[column] - points[partner] for partner in range(4) if partner != column]) for column in range(4)])
    matrix = np.zeros((4, 4))
    for target in range(4):
        for column in range(4):
            if target != column:
                matrix[target, column] = barycentric[column] / barycentric[target] / (points[target] - points[column])
        matrix[target, target] = -np.sum(matrix[target])
    return matrix

def orient_table():
    lookup_table = np.zeros((8, 16), dtype=np.int32)
    for orient_code in range(8):
        for lead_node in range(4):
            for next_node in range(4):
                along_node, cross_node = (next_node, lead_node) if orient_code & 1 else (lead_node, next_node)
                if orient_code & 2:
                    along_node = 3 - along_node
                if orient_code & 4:
                    cross_node = 3 - cross_node
                lookup_table[orient_code, lead_node * 4 + next_node] = along_node * 4 + cross_node
    return lookup_table

def primitives(fields):
    velocity = fields[1:4] / fields[0]
    pressure = (GAMMA - 1.0) * (fields[4] - 0.5 * lax.optimization_barrier(jnp.sum(fields[1:4] * velocity, axis=0)))
    return (velocity, pressure)

def directed_flux(fields, velocity, pressure, direction):
    normal_speed = velocity[direction]
    components = [fields[member] * normal_speed for member in range(4)]
    components.append((fields[4] + pressure) * normal_speed)
    components[1 + direction] = components[1 + direction] + pressure
    return jnp.stack(components)

def face_traces(nodal_cube):
    elements = nodal_cube.shape[-1]
    face_slices = [nodal_cube[:, 0], nodal_cube[:, 3], nodal_cube[:, :, 0], nodal_cube[:, :, 3], nodal_cube[:, :, :, 0], nodal_cube[:, :, :, 3]]
    return jnp.stack([side_nodes.reshape(5, 16, elements) for side_nodes in face_slices])

def orient_faces(gathered, orient_codes):
    lookup_table = orient_table()
    combined = jnp.zeros_like(gathered)
    for orient_code in range(8):
        combined = jnp.where(orient_codes == orient_code, gathered[:, lookup_table[orient_code], :], combined)
    return combined

def residual_of(fields, element_size, own_faces, outside):
    elements = fields.shape[-1]
    nodal_cube = fields.reshape(5, 4, 4, 4, elements)
    velocity, pressure = primitives(nodal_cube)
    derivative = jnp.asarray(gll_derivative(), dtype=jnp.float32)
    volume = jnp.einsum('ai,vijke->vajke', derivative, directed_flux(nodal_cube, velocity, pressure, 0), precision=HIGHEST)
    volume = volume + jnp.einsum('bj,vijke->vibke', derivative, directed_flux(nodal_cube, velocity, pressure, 1), precision=HIGHEST)
    volume = volume + jnp.einsum('ck,vijke->vijce', derivative, directed_flux(nodal_cube, velocity, pressure, 2), precision=HIGHEST)
    surface = jnp.zeros_like(nodal_cube)
    for face_number in range(6):
        direction = face_number // 2
        outward = 1.0 if face_number % 2 else -1.0
        position = 3 if face_number % 2 else 0
        inside_trace = own_faces[face_number]
        outside_trace = outside[face_number]
        inside_velocity, inside_pressure = primitives(inside_trace)
        outside_velocity, outside_pressure = primitives(outside_trace)
        wave_speed = jnp.maximum(jnp.abs(inside_velocity[direction]) + jnp.sqrt(GAMMA * inside_pressure / inside_trace[0]), jnp.abs(outside_velocity[direction]) + jnp.sqrt(GAMMA * outside_pressure / outside_trace[0]))
        correction = 0.5 * outward * (directed_flux(outside_trace, outside_velocity, outside_pressure, direction) - directed_flux(inside_trace, inside_velocity, inside_pressure, direction)) - 0.5 * wave_speed * (outside_trace - inside_trace)
        correction = correction.reshape(5, 4, 4, elements)
        if direction == 0:
            surface = surface.at[:, position].add(correction)
        elif direction == 1:
            surface = surface.at[:, :, position].add(correction)
        else:
            surface = surface.at[:, :, :, position].add(correction)
    return (-(2.0 / element_size) * (volume + LIFT * surface)).reshape(5, 64, elements)

def section_rate(fields, element_size, neighbour, orientation):
    own_faces = face_traces(fields.reshape(5, 4, 4, 4, TOTAL))
    outside = jnp.stack([orient_faces(jnp.take(own_faces[face_number ^ 1], neighbour[face_number], axis=2), orientation[face_number]) for face_number in range(6)])
    blocks = (fields.reshape(5, 64, RANKS, E_DEV).transpose(2, 0, 1, 3), element_size.reshape(RANKS, E_DEV), own_faces.reshape(6, 5, 16, RANKS, E_DEV).transpose(3, 0, 1, 2, 4), outside.reshape(6, 5, 16, RANKS, E_DEV).transpose(3, 0, 1, 2, 4))
    rates = lax.map(lambda pieces: residual_of(pieces[0], pieces[1], pieces[2], pieces[3]), blocks)
    return rates.transpose(1, 2, 0, 3).reshape(5, 64, TOTAL)

def reference(old_state, element_size, old_start, neighbour, orientation):
    curve_index = jnp.arange(TOTAL, dtype=jnp.int32)
    old_owner = (jnp.searchsorted(old_start, curve_index, side='right') - 1).astype(jnp.int32)
    source = old_owner * OLD_CAP + curve_index - jnp.take(old_start, old_owner)
    fields = jnp.take(old_state, source, axis=2)
    first_section = fields + TIME_STEP * section_rate(fields, element_size, neighbour, orientation)
    return 0.5 * fields + 0.5 * (first_section + TIME_STEP * section_rate(first_section, element_size, neighbour, orientation))
```

```python
import functools

import jax
import jax.numpy as jnp
import numpy as np
from jax import lax
from jax.experimental import pallas as pl
from jax.experimental.pallas import tpu as pltpu
from jax.sharding import PartitionSpec as P

AXES = ("gx", "gy", "gz")
TIME_STEP = 0.03
LIFT = 6.0
VARS = 5
NODES = 64
EL = 256
LANES = 128
REMOTE = 32
FACES = 6
ROWS = VARS * NODES
BF = jnp.bfloat16
F32 = jnp.float32
I32 = jnp.int32


def gll_derivative():
    points = np.array([-1.0, -1.0 / np.sqrt(5.0), 1.0 / np.sqrt(5.0), 1.0])
    weights = np.array(
        [1.0 / np.prod([points[c] - points[p] for p in range(4) if p != c]) for c in range(4)]
    )
    matrix = np.zeros((4, 4))
    for row in range(4):
        for col in range(4):
            if row != col:
                matrix[row, col] = weights[col] / weights[row] / (points[row] - points[col])
        matrix[row, row] = -np.sum(matrix[row])
    return matrix


def node_derivatives():
    d, one = gll_derivative(), np.eye(4)
    parts = [
        np.kron(np.kron(d, one), one),
        np.kron(np.kron(one, d), one),
        np.kron(np.kron(one, one), d),
    ]
    return np.concatenate(parts, axis=1).astype(np.float32)


def iota(shape, dim):
    return lax.broadcasted_iota(I32, shape, dim)


def split(x):
    hi = x.astype(BF)
    return hi, (x - hi.astype(F32)).astype(BF)


def mm(a, b):
    return jnp.dot(a, b, preferred_element_type=F32)


def face_rows(ref, h, v, f):
    base = v * NODES
    if f < 2:
        return ref[h, base + 48 * f : base + 48 * f + 16, :]
    if f < 4:
        first = base + 12 * (f - 2)
        return jnp.concatenate([ref[h, first + 16 * i : first + 16 * i + 4, :] for i in range(4)], 0)
    return ref[h, pl.ds(base + 3 * (f - 4), 16, stride=4), :]


def add_face_rows(ref, lead, base, f, val):
    at = (lambda r: (lead, r)) if lead is not None else (lambda r: (r,))
    if f < 2:
        r = at(pl.ds(base + 48 * f, 16)) + (slice(None),)
        ref[r] = ref[r] + val
    elif f < 4:
        for i in range(4):
            r = at(pl.ds(base + 12 * (f - 2) + 16 * i, 4)) + (slice(None),)
            ref[r] = ref[r] + val[4 * i : 4 * i + 4, :]
    else:
        r = at(pl.ds(base + 3 * (f - 4), 16, stride=4)) + (slice(None),)
        ref[r] = ref[r] + val


def rank_of(sizes):
    return (lax.axis_index("gx") * sizes[1] + lax.axis_index("gy")) * sizes[2] + lax.axis_index("gz")


def send_kernel(sizes, start, old, nb_ref, ori_ref, s_a, s_b, rows_ref, col_ref, mk):
    n = sizes[0] * sizes[1] * sizes[2]
    d = rank_of(sizes)
    even = (d & 1) == 0
    up = jnp.where(d + 1 == n, 0, d + 1) * EL
    down = jnp.where(d == 0, n - 1, d - 1) * EL
    base_a = jnp.where(even, up, down)
    base_b = jnp.where(even, down, up)
    nb = nb_ref[...]
    rel = [nb - base_a, nb - base_b]
    mk[...] = jnp.zeros((16, EL), F32)
    for k in range(2):
        mk[8 * k : 8 * k + FACES, :] = jnp.where((rel[k] >= 0) & (rel[k] < EL), 1.0, 0.0)
    mask = mk[...]
    upper = jnp.where(iota((EL, EL), 0) <= iota((EL, EL), 1), 1.0, 0.0).astype(BF)
    inclusive = mm(mask.astype(BF), upper)
    total = jnp.broadcast_to(inclusive[:, EL - 1 : EL], (16, LANES)).astype(BF)
    r, c = iota((16, 16), 0), iota((16, 16), 1)
    lower = jnp.where((c < r) & ((c >> 3) == (r >> 3)), 1.0, 0.0).astype(BF)
    offset = mm(lower, total)[:, 0:1]
    place = jnp.where(mask > 0.5, inclusive + offset - 1.0, -1.0)
    face = iota((FACES, EL), 0)
    own = (face * EL + iota((FACES, EL), 1) + 2048 * ori_ref[...]).astype(F32)
    slot = iota((REMOTE, EL), 0).astype(F32)
    lists = []
    for k in range(2):
        req = ((face ^ 1) * EL + rel[k]).astype(F32)
        acc_r = jnp.zeros((REMOTE, EL), F32)
        acc_o = jnp.zeros((REMOTE, EL), F32)
        for f in range(FACES):
            hit = place[8 * k + f : 8 * k + f + 1, :] == slot
            acc_r = jnp.where(hit, req[f : f + 1, :], acc_r)
            acc_o = jnp.where(hit, own[f : f + 1, :], acc_o)
        lists.append((jnp.sum(acc_r, 1, keepdims=True), jnp.sum(acc_o, 1, keepdims=True)))
    col = jnp.concatenate([lists[0][0], lists[1][0], lists[0][1], lists[1][1]], 0)
    wide = jnp.broadcast_to(col, (LANES, LANES))
    row = jnp.transpose(wide)[0:8, :]
    turn = jnp.floor(row * (1.0 / 2048.0))
    code = row - 2048.0 * turn
    rows_ref[0:8, :] = code
    rows_ref[8:16, :] = turn
    col_ref[...] = wide[64:128, :]

    o = start[d] - d * EL
    first = EL - o
    q, rot = first >> 7, first & 127
    lane = iota((NODES, LANES), 1)
    keep = lane < LANES - rot
    back = (LANES - rot) & 127
    t0 = pl.ds(pl.multiple_of(q * LANES, LANES), LANES)
    t1 = pl.ds(pl.multiple_of(jnp.minimum(q + 1, 3) * LANES, LANES), LANES)

    def put(to_up, to_down):
        for v in range(VARS):
            rows = slice(v * NODES, v * NODES + NODES)
            to_up[rows, :] = jnp.where(
                keep, pltpu.roll(old[v, :, t0], back, 1), pltpu.roll(old[v, :, t1], back, 1)
            )
            to_down[rows, :] = pltpu.roll(old[v, :, 0:LANES], o & 127, 1)

    @pl.when(even)
    def _():
        put(s_a, s_b)

    @pl.when(jnp.logical_not(even))
    def _():
        put(s_b, s_a)

    s_a[ROWS : ROWS + 8, :] = code
    s_b[ROWS : ROWS + 8, :] = code


def own_kernel(sizes, start, old, col_ref, own, ohs):
    d = rank_of(sizes)
    s = d * EL - start[d]
    q, rot = s >> 7, s & 127
    keep = iota((NODES, LANES), 1) < LANES - rot
    back = (LANES - rot) & 127
    for v in range(VARS):
        rows = slice(v * NODES, v * NODES + NODES)
        t = [
            pltpu.roll(
                old[v, :, pl.ds(pl.multiple_of(jnp.maximum(q + i, 0) * LANES, LANES), LANES)], back, 1
            )
            for i in range(3)
        ]
        own[0, rows, :] = jnp.where(keep, t[0], t[1])
        own[1, rows, :] = jnp.where(keep, t[1], t[2])
    code = col_ref[...].astype(I32)
    lane = iota((64, LANES), 1)
    for h in range(2):
        hit = jnp.where((code & 255) == lane + h * LANES, 1.0, 0.0).astype(BF)
        ohs[0:64, h * LANES : h * LANES + LANES] = hit
        ohs[64:128, h * LANES : h * LANES + LANES] = jnp.zeros((64, LANES), BF)


def requested(fld, one_hot, g):
    acc = None
    for f in range(FACES):
        t = jnp.concatenate(
            [
                jnp.concatenate([face_rows(fld, h, v, f) for v in range(VARS)], 0)
                for h in range(2)
            ],
            1,
        )
        part = mm(jnp.concatenate(split(t), 0), one_hot(f))
        acc = part if acc is None else acc + part
    g[...] = acc[0:80, :] + acc[80:160, :]


def join_kernel(sizes, start, own, r_a, r_b, rows_ref, fld, ohg, g):
    d = rank_of(sizes)
    even = (d & 1) == 0
    o = start[d] - d * EL
    u = start[d + 1] - d * EL
    lane = iota((NODES, LANES), 1)
    for v in range(VARS):
        rows = slice(v * NODES, v * NODES + NODES)
        a, b = r_a[rows, :], r_b[rows, :]
        fld[0, rows, :] = jnp.where(lane < o, jnp.where(even, b, a), own[0, rows, :])
        fld[1, rows, :] = jnp.where(lane + LANES >= u, jnp.where(even, a, b), own[1, rows, :])
    lane8 = iota((8, LANES), 1)
    code = jnp.where(
        lane8 < 32,
        r_a[ROWS : ROWS + 8, :],
        jnp.where(lane8 < 64, r_b[ROWS : ROWS + 8, :], rows_ref[0:8, :]),
    ).astype(I32)
    line = jnp.broadcast_to(code[0:1, :], (EL, LANES)) - iota((EL, LANES), 0)

    def one_hot(f):
        hot = jnp.where(line == f * EL, 1.0, 0.0).astype(BF)
        ohg[f * EL : f * EL + EL, :] = hot
        return hot

    requested(fld, one_hot, g)


def fluxes(u, speeds, p):
    out = []
    for a in range(3):
        s = speeds[a]
        row = [u[0] * s, u[1] * s, u[2] * s, u[3] * s, (u[4] + p) * s]
        row[1 + a] = row[1 + a] + p
        out.append(row)
    return out


def directed(u, axis_is):
    inv = 1.0 / u[0]
    p = 0.4 * (u[4] - 0.5 * ((u[1] * u[1] + u[2] * u[2] + u[3] * u[3]) * inv))
    mom = jnp.where(axis_is[0], u[1], jnp.where(axis_is[1], u[2], u[3]))
    s = mom * inv
    flux = [u[0] * s] + [u[i] * s for i in range(1, 4)] + [(u[4] + p) * s]
    zero = jnp.zeros_like(p)
    flux[1] = flux[1] + jnp.where(axis_is[0], p, zero)
    flux[2] = flux[2] + jnp.where(axis_is[1], p, zero)
    flux[3] = flux[3] + jnp.where(axis_is[0] | axis_is[1], zero, p)
    return flux, jnp.abs(s) + jnp.sqrt(1.4 * p * inv)


def correction(inner, outer, axis_is, half_sign):
    fi, si = directed(inner, axis_is)
    fo, so = directed(outer, axis_is)
    lam = 0.5 * jnp.maximum(si, so)
    return [half_sign * (fo[v] - fi[v]) - lam * (outer[v] - inner[v]) for v in range(VARS)]


def turned(x, b0, b1, b2):
    x = [jnp.where(b1, x[4 * (3 - p) + q], x[4 * p + q]) for p in range(4) for q in range(4)]
    x = [jnp.where(b2, x[4 * p + 3 - q], x[4 * p + q]) for p in range(4) for q in range(4)]
    return [jnp.where(b0, x[4 * t + s], x[4 * s + t]) for s in range(4) for t in range(4)]


def local_kernel(sizes, last, fld, nb_ref, ori_ref, size_ref, d_ref, *rest):
    if last:
        old_fld, part, acc, xs, xg, xq, xo, xc, it = rest
    else:
        part, acc, xs, xg, xq, xo, xc, it = rest
    d = rank_of(sizes)
    dh, dl = split(d_ref[...])
    dd = jnp.concatenate([dh, dl], 0)
    pieces = [[[], []] for _ in range(VARS)]
    for h in range(2):
        u = [fld[h, v * NODES : v * NODES + NODES, :] for v in range(VARS)]
        inv = 1.0 / u[0]
        speeds = [u[i] * inv for i in range(1, 4)]
        p = 0.4 * (u[4] - 0.5 * (u[1] * speeds[0] + u[2] * speeds[1] + u[3] * speeds[2]))
        fl = fluxes(u, speeds, p)
        for v in range(VARS):
            hl = [split(fl[a][v]) for a in range(3)]
            pieces[v][0].append(jnp.concatenate([x[0] for x in hl], 0))
            pieces[v][1].append(jnp.concatenate([x[1] for x in hl], 0))
    for v in range(VARS):
        hi = mm(dd, jnp.concatenate(pieces[v][0], 1))
        lo = mm(dh, jnp.concatenate(pieces[v][1], 1))
        vol = hi[0:NODES, :] + hi[NODES : 2 * NODES, :] + lo
        for h in range(2):
            acc[h, v * NODES : v * NODES + NODES, :] = vol[:, h * LANES : h * LANES + LANES]
    for v in range(VARS):
        for f in range(FACES):
            for h in range(2):
                t = face_rows(fld, h, v, f)
                b = v * 256
                xs[pl.ds(b + 2 * f + h, 16, stride=16), :] = t
                xg[pl.ds(b + 2 * (f ^ 1) + h, 16, stride=16), :] = t
                xq[pl.ds(b + 2 * (f ^ 1) + 1 - h, 16, stride=16), :] = t
    it[...] = jnp.zeros((32, LANES), I32)
    for h in range(2):
        it[pl.ds(h, FACES, stride=2), :] = nb_ref[:, h * LANES : h * LANES + LANES]
        it[pl.ds(16 + h, FACES, stride=2), :] = ori_ref[:, h * LANES : h * LANES + LANES]
    t = it[0:16, :] - d * EL
    turn = it[16:32, :]
    row = iota((16, LANES), 0)
    local = (t >= 0) & (t < EL) & (row < 12)
    same = ((t >> 7) & 1) == (row & 1)
    idx = t & 127
    b0, b1, b2 = (turn & 1) != 0, (turn & 2) != 0, (turn & 4) != 0
    for v in range(VARS):
        got = []
        for m in range(16):
            rows = slice(v * 256 + m * 16, v * 256 + m * 16 + 16)
            ga = jnp.take_along_axis(xg[rows, :], idx, axis=1)
            gb = jnp.take_along_axis(xq[rows, :], idx, axis=1)
            got.append(jnp.where(same, ga, gb))
        for m, x in enumerate(turned(got, b0, b1, b2)):
            xo[v * 256 + m * 16 : v * 256 + m * 16 + 16, :] = x
    axis_is = (row < 4, (row >= 4) & (row < 8))
    half_sign = jnp.where((row & 2) != 0, 0.5, -0.5)
    for m in range(16):
        rows = [slice(v * 256 + m * 16, v * 256 + m * 16 + 16) for v in range(VARS)]
        cor = correction([xs[r, :] for r in rows], [xo[r, :] for r in rows], axis_is, half_sign)
        for v in range(VARS):
            xc[rows[v], :] = jnp.where(local, LIFT * cor[v], 0.0)
    for v in range(VARS):
        for f in range(FACES):
            for h in range(2):
                add_face_rows(
                    acc, h, v * NODES, f, xc[pl.ds(v * 256 + 2 * f + h, 16, stride=16), :]
                )
    for h in range(2):
        size = size_ref[0:1, h * LANES : h * LANES + LANES]
        coef = (TIME_STEP * 2.0) / size
        for v in range(VARS):
            rows = slice(v * NODES, v * NODES + NODES)
            new = fld[h, rows, :] - coef * acc[h, rows, :]
            if last:
                new = 0.5 * old_fld[h, rows, :] + 0.5 * new
            part[h, rows, :] = new


def finish_kernel(last, part, g, r_a, r_b, rows_ref, ohs, size_ref, *rest):
    if last:
        out, ro, y, e = rest
    else:
        ohg, out, g_next, ro, y, e = rest
    lane = iota((80, LANES), 1)
    ro[0:80, :] = jnp.where(lane < 32, r_a[...], r_b[...])
    ro[80:128, :] = jnp.zeros((48, LANES), F32)
    code = pltpu.roll(rows_ref[0:8, :], 64, 1).astype(I32)
    turn = pltpu.roll(rows_ref[8:16, :], 64, 1).astype(I32)
    x = [ro[pl.ds(m, 8, stride=16), :] for m in range(16)]
    for m, val in enumerate(turned(x, (turn & 1) != 0, (turn & 2) != 0, (turn & 4) != 0)):
        y[8 * m : 8 * m + 8, :] = val
    live = iota((16, LANES), 1) < 64
    face = jnp.where(live, jnp.broadcast_to(code[0:1, :], (16, LANES)) >> 8, 0)
    axis_is = (face < 2, (face >= 2) & (face < 4))
    half_sign = jnp.where((face & 1) != 0, 0.5, -0.5)
    inner = [pltpu.roll(g[16 * v : 16 * v + 16, :], 64, 1) for v in range(VARS)]
    outer = [y[pl.ds(v, 16, stride=8), :] for v in range(VARS)]
    cor = correction(inner, outer, axis_is, half_sign)
    e[...] = jnp.zeros((ROWS, LANES), F32)
    for v in range(VARS):
        for f in range(FACES):
            add_face_rows(
                e, None, v * NODES, f, jnp.where(live & (face == f), cor[v], 0.0)
            )
    spread = mm(jnp.concatenate(split(e[...]), 0), ohs[...])
    scale = (TIME_STEP * 2.0 * LIFT) * (0.5 if last else 1.0)
    for h in range(2):
        coef = scale / size_ref[0:1, h * LANES : h * LANES + LANES]
        lanes = slice(h * LANES, h * LANES + LANES)
        for v in range(VARS):
            rows = slice(v * NODES, v * NODES + NODES)
            low = slice(ROWS + v * NODES, ROWS + v * NODES + NODES)
            new = part[h, rows, :] - coef * (spread[rows, lanes] + spread[low, lanes])
            if last:
                out[v, :, lanes] = new
            else:
                out[h, rows, :] = new
    if not last:
        requested(out, lambda f: ohg[f * EL : f * EL + EL, :], g_next)


def call(body, out_shape, scratch, cost, *args):
    spec = pl.BlockSpec(memory_space=pltpu.VMEM)
    specs = [
        pl.BlockSpec(memory_space=pltpu.SMEM) if a.dtype == I32 and a.ndim == 1 else spec
        for a in args
    ]
    return pl.pallas_call(
        body,
        out_shape=out_shape,
        in_specs=specs,
        out_specs=jax.tree.map(lambda _: spec, out_shape),
        scratch_shapes=scratch,
        cost_estimate=pl.CostEstimate(flops=cost, bytes_accessed=cost, transcendentals=0),
        compiler_params=pltpu.CompilerParams(vmem_limit_bytes=32 * 1024 * 1024),
    )(*args)


def shape(*dims, dtype=F32):
    return jax.ShapeDtypeStruct(dims, dtype)


def per_device(sizes, old_state, element_size, old_start, neighbour, orientation):
    n = sizes[0] * sizes[1] * sizes[2]
    pairs_a = [(i, i ^ 1) for i in range(n)]
    pairs_b = [(i, (i + 1) % n if i % 2 else (i - 1) % n) for i in range(n)]

    def exchange(a, b):
        r_b = lax.ppermute(b, AXES, pairs_b)
        r_a = lax.ppermute(a, AXES, pairs_a)
        return r_a, r_b

    size = element_size.reshape(1, EL)
    deriv = jnp.asarray(node_derivatives())
    s_a, s_b, rows, col = call(
        functools.partial(send_kernel, sizes),
        (shape(ROWS + 8, LANES), shape(ROWS + 8, LANES), shape(16, LANES), shape(64, LANES)),
        [pltpu.VMEM((16, EL), F32)],
        10000,
        old_start,
        old_state,
        neighbour,
        orientation,
    )
    r_a, r_b = exchange(s_a, s_b)
    own, ohs = call(
        functools.partial(own_kernel, sizes),
        (shape(2, ROWS, LANES), shape(LANES, EL, dtype=BF)),
        [],
        10000,
        old_start,
        old_state,
        col,
    )
    fld, ohg, g = call(
        functools.partial(join_kernel, sizes),
        (shape(2, ROWS, LANES), shape(FACES * EL, LANES, dtype=BF), shape(80, LANES)),
        [],
        10000,
        old_start,
        own,
        r_a,
        r_b,
        rows,
    )

    def local(last, *args):
        table = pltpu.VMEM((VARS * 256, LANES), F32)
        return call(
            functools.partial(local_kernel, sizes, last),
            shape(2, ROWS, LANES),
            [pltpu.VMEM((2, ROWS, LANES), F32)] + [table] * 5 + [pltpu.VMEM((32, LANES), I32)],
            20000,
            *args,
        )

    scratch = [
        pltpu.VMEM((LANES, LANES), F32),
        pltpu.VMEM((LANES, LANES), F32),
        pltpu.VMEM((ROWS, LANES), F32),
    ]
    r_a, r_b = exchange(g, g)
    part = local(False, fld, neighbour, orientation, size, deriv)
    first, g2 = call(
        functools.partial(finish_kernel, False),
        (shape(2, ROWS, LANES), shape(80, LANES)),
        scratch,
        10000,
        part,
        g,
        r_a,
        r_b,
        rows,
        ohs,
        size,
        ohg,
    )
    r_a, r_b = exchange(g2, g2)
    part = local(True, first, neighbour, orientation, size, deriv, fld)
    return call(
        functools.partial(finish_kernel, True),
        shape(VARS, NODES, EL),
        scratch,
        10000,
        part,
        g2,
        r_a,
        r_b,
        rows,
        ohs,
        size,
    )


def solution(mesh):
    sizes = tuple(mesh.shape[a] for a in AXES)
    in_specs = (P(None, None, AXES), P(AXES), P(), P(None, AXES), P(None, AXES))
    return jax.shard_map(
        functools.partial(per_device, sizes),
        mesh=mesh,
        in_specs=in_specs,
        out_specs=P(None, None, AXES),
        check_vma=False,
    )
```

```python
import functools

import jax
import jax.numpy as jnp
import numpy as np
from jax import lax
from jax.experimental import pallas as pl
from jax.experimental.pallas import tpu as pltpu
from jax.sharding import PartitionSpec as P

AXES = ("gx", "gy", "gz")
TIME_STEP = 0.03
LIFT = 6.0
VARS = 5
NODES = 64
EL = 256
LANES = 128
REMOTE = 32
FACES = 6
ROWS = VARS * NODES
BF = jnp.bfloat16
F32 = jnp.float32
I32 = jnp.int32


def gll_derivative():
    points = np.array([-1.0, -1.0 / np.sqrt(5.0), 1.0 / np.sqrt(5.0), 1.0])
    weights = np.array(
        [1.0 / np.prod([points[c] - points[p] for p in range(4) if p != c]) for c in range(4)]
    )
    matrix = np.zeros((4, 4))
    for row in range(4):
        for col in range(4):
            if row != col:
                matrix[row, col] = weights[col] / weights[row] / (points[row] - points[col])
        matrix[row, row] = -np.sum(matrix[row])
    return matrix


def node_derivatives():
    d, one = gll_derivative(), np.eye(4)
    parts = [
        np.kron(np.kron(d, one), one),
        np.kron(np.kron(one, d), one),
        np.kron(np.kron(one, one), d),
    ]
    return np.concatenate(parts, axis=1).astype(np.float32)


def iota(shape, dim):
    return lax.broadcasted_iota(I32, shape, dim)


def split(x):
    hi = x.astype(BF)
    return hi, (x - hi.astype(F32)).astype(BF)


def mm(a, b):
    return jnp.dot(a, b, preferred_element_type=F32)


def rows_at(lead, base, f, i=None):
    if f < 2:
        rows = pl.ds(base + 48 * f, 16)
    elif f < 4:
        rows = pl.ds(base + 12 * (f - 2) + 16 * i, 4)
    else:
        rows = pl.ds(base + 3 * (f - 4), 16, stride=4)
    return (rows, slice(None)) if lead is None else (lead, rows, slice(None))


def face_rows(ref, lead, v, f):
    if f in (2, 3):
        return jnp.concatenate([ref[rows_at(lead, v * NODES, f, i)] for i in range(4)], 0)
    return ref[rows_at(lead, v * NODES, f)]


def add_face_rows(ref, lead, v, f, val):
    if f in (2, 3):
        for i in range(4):
            r = rows_at(lead, v * NODES, f, i)
            ref[r] = ref[r] + val[4 * i : 4 * i + 4, :]
    else:
        r = rows_at(lead, v * NODES, f)
        ref[r] = ref[r] + val


def rank_of(sizes):
    return (lax.axis_index("gx") * sizes[1] + lax.axis_index("gy")) * sizes[2] + lax.axis_index("gz")


def places(mask):
    count = mask.shape[0]
    upper = jnp.where(iota((EL, EL), 0) <= iota((EL, EL), 1), 1.0, 0.0).astype(BF)
    inclusive = mm(mask.astype(BF), upper)
    total = jnp.broadcast_to(inclusive[:, EL - 1 : EL], (count, LANES)).astype(BF)
    r, c = iota((count, count), 0), iota((count, count), 1)
    lower = jnp.where((c < r) & ((c >> 3) == (r >> 3)), 1.0, 0.0).astype(BF)
    offset = mm(lower, total)[:, 0:1]
    return jnp.where(mask > 0.5, inclusive + offset - 1.0, -1.0)


def listed(place, values):
    slot = iota((REMOTE, EL), 0).astype(F32)
    accs = [jnp.zeros((REMOTE, EL), F32) for _ in values]
    for f in range(FACES):
        hit = place[f : f + 1, :] == slot
        accs = [jnp.where(hit, x[f : f + 1, :], acc) for x, acc in zip(values, accs)]
    return [jnp.sum(acc, 1, keepdims=True) for acc in accs]


def send_kernel(sizes, start_hbm, old, nb, ori, s_a, s_b, rows_ref, col_ref, old_v, nb_v, ori_v, mk, start, sem):
    n = sizes[0] * sizes[1] * sizes[2]
    copies = [
        pltpu.make_async_copy(nb, nb_v, sem.at[0]),
        pltpu.make_async_copy(ori, ori_v, sem.at[1]),
        pltpu.make_async_copy(start_hbm, start, sem.at[2]),
    ] + [pltpu.make_async_copy(old.at[v], old_v.at[v], sem.at[3 + v]) for v in range(VARS)]
    for copy in copies:
        copy.start()
    d = rank_of(sizes)
    even = (d & 1) == 0
    up = jnp.where(d + 1 == n, 0, d + 1) * EL
    down = jnp.where(d == 0, n - 1, d - 1) * EL
    mk[...] = jnp.zeros((16, EL), F32)
    copies[0].wait()
    nb = nb_v[...]
    rel = [nb - jnp.where(even, up, down), nb - jnp.where(even, down, up)]
    for k in range(2):
        mk[8 * k : 8 * k + FACES, :] = jnp.where((rel[k] >= 0) & (rel[k] < EL), 1.0, 0.0)
    place = places(mk[...])
    copies[1].wait()
    face = iota((FACES, EL), 0)
    own = (face * EL + iota((FACES, EL), 1) + 2048 * ori_v[...]).astype(F32)
    lists = []
    for k in range(2):
        lists.append(listed(place[8 * k : 8 * k + 8, :], [((face ^ 1) * EL + rel[k]).astype(F32), own]))
    col = jnp.concatenate([lists[0][0], lists[1][0], lists[0][1], lists[1][1]], 0)
    wide = jnp.broadcast_to(col, (LANES, LANES))
    row = jnp.transpose(wide)[0:8, :]
    turn = jnp.floor(row * (1.0 / 2048.0))
    code = row - 2048.0 * turn
    rows_ref[0:8, :] = code
    rows_ref[8:16, :] = turn
    col_ref[...] = wide[64:128, :]
    s_a[ROWS : ROWS + 8, :] = code
    s_b[ROWS : ROWS + 8, :] = code

    copies[2].wait()
    o = start[d] - d * EL
    first = EL - o
    q, rot = first >> 7, first & 127
    keep = iota((NODES, LANES), 1) < LANES - rot
    back = (LANES - rot) & 127
    t0 = pl.ds(pl.multiple_of(q * LANES, LANES), LANES)
    t1 = pl.ds(pl.multiple_of(jnp.minimum(q + 1, 3) * LANES, LANES), LANES)
    for copy in copies[3:]:
        copy.wait()

    def put(to_up, to_down):
        for v in range(VARS):
            rows = slice(v * NODES, v * NODES + NODES)
            to_up[rows, :] = jnp.where(
                keep, pltpu.roll(old_v[v, :, t0], back, 1), pltpu.roll(old_v[v, :, t1], back, 1)
            )
            to_down[rows, :] = pltpu.roll(old_v[v, :, 0:LANES], o & 127, 1)

    @pl.when(even)
    def _():
        put(s_a, s_b)

    @pl.when(jnp.logical_not(even))
    def _():
        put(s_b, s_a)


def own_kernel(sizes, start, old, col_ref, d_hbm, size_hbm, own, ohs, dd, coef, d_v, size_v, sem):
    copies = [
        pltpu.make_async_copy(d_hbm, d_v, sem.at[0]),
        pltpu.make_async_copy(size_hbm, size_v, sem.at[1]),
    ]
    for copy in copies:
        copy.start()
    d = rank_of(sizes)
    s = d * EL - start[d]
    q, rot = s >> 7, s & 127
    keep = iota((NODES, LANES), 1) < LANES - rot
    back = (LANES - rot) & 127
    for v in range(VARS):
        rows = slice(v * NODES, v * NODES + NODES)
        t = [
            pltpu.roll(
                old[v, :, pl.ds(pl.multiple_of(jnp.maximum(q + i, 0) * LANES, LANES), LANES)], back, 1
            )
            for i in range(3)
        ]
        own[0, rows, :] = jnp.where(keep, t[0], t[1])
        own[1, rows, :] = jnp.where(keep, t[1], t[2])
    code = col_ref[...].astype(I32)
    lane = iota((64, LANES), 1)
    for h in range(2):
        hit = jnp.where((code & 255) == lane + h * LANES, 1.0, 0.0).astype(BF)
        ohs[0:64, h * LANES : h * LANES + LANES] = hit
        ohs[64:128, h * LANES : h * LANES + LANES] = jnp.zeros((64, LANES), BF)
    for copy in copies:
        copy.wait()
    dd[...] = jnp.concatenate(split(d_v[...]), 0)
    coef[...] = (TIME_STEP * 2.0) / size_v[...]


def requested(fld, hot, face, gs, g):
    both = jnp.concatenate([fld[0], fld[1]], 1)
    out = mm(jnp.concatenate(split(both), 0), hot)
    gs[...] = out[0:ROWS, :] + out[ROWS : 2 * ROWS, :]
    for v in range(VARS):
        acc = face_rows(gs, None, v, 0)
        for f in range(1, FACES):
            acc = jnp.where(face == f, face_rows(gs, None, v, f), acc)
        g[16 * v : 16 * v + 16, :] = acc


def join_kernel(sizes, start, own, r_a, r_b, rows_ref, fld, hot_ref, code_ref, g, gs):
    n = sizes[0] * sizes[1] * sizes[2]
    d = rank_of(sizes)
    even = (d & 1) == 0
    o = start[d] - d * EL
    u = start[d + 1] - d * EL
    lane8 = iota((8, LANES), 1)
    code_ref[...] = jnp.where(
        lane8 < 32,
        r_a[ROWS : ROWS + 8, :],
        jnp.where(lane8 < 64, r_b[ROWS : ROWS + 8, :], rows_ref[0:8, :]),
    )

    lane = iota((NODES, LANES), 1)
    for v in range(VARS):
        rows = slice(v * NODES, v * NODES + NODES)
        a, b = r_a[rows, :], r_b[rows, :]
        fld[0, rows, :] = jnp.where(lane < o, jnp.where(even, b, a), own[0, rows, :])
        fld[1, rows, :] = jnp.where(lane + LANES >= u, jnp.where(even, a, b), own[1, rows, :])
    code = code_ref[...].astype(I32)
    spot = jnp.broadcast_to(code[0:1, :] & 255, (EL, LANES))
    hot = jnp.where(spot == iota((EL, LANES), 0), 1.0, 0.0).astype(BF)
    hot_ref[...] = hot
    face = jnp.broadcast_to(code[0:1, :] >> 8, (16, LANES))
    requested(fld, hot, face, gs, g)


def fluxes(u, speeds, p):
    out = []
    for a in range(3):
        s = speeds[a]
        row = [u[0] * s, u[1] * s, u[2] * s, u[3] * s, (u[4] + p) * s]
        row[1 + a] = row[1 + a] + p
        out.append(row)
    return out


def directed(u, axis_is):
    inv = 1.0 / u[0]
    p = 0.4 * (u[4] - 0.5 * ((u[1] * u[1] + u[2] * u[2] + u[3] * u[3]) * inv))
    mom = jnp.where(axis_is[0], u[1], jnp.where(axis_is[1], u[2], u[3]))
    s = mom * inv
    flux = [u[0] * s] + [u[i] * s for i in range(1, 4)] + [(u[4] + p) * s]
    zero = jnp.zeros_like(p)
    flux[1] = flux[1] + jnp.where(axis_is[0], p, zero)
    flux[2] = flux[2] + jnp.where(axis_is[1], p, zero)
    flux[3] = flux[3] + jnp.where(axis_is[0] | axis_is[1], zero, p)
    return flux, jnp.abs(s) + jnp.sqrt(1.4 * p * inv)


def correction(inner, outer, axis_is, half_sign):
    fi, si = directed(inner, axis_is)
    fo, so = directed(outer, axis_is)
    lam = 0.5 * jnp.maximum(si, so)
    return [half_sign * (fo[v] - fi[v]) - lam * (outer[v] - inner[v]) for v in range(VARS)]


def turned(x, b0, b1, b2):
    x = [jnp.where(b1, x[4 * (3 - p) + q], x[4 * p + q]) for p in range(4) for q in range(4)]
    x = [jnp.where(b2, x[4 * p + 3 - q], x[4 * p + q]) for p in range(4) for q in range(4)]
    return [jnp.where(b0, x[4 * t + s], x[4 * s + t]) for s in range(4) for t in range(4)]


def local_kernel(sizes, last, fld, nb_ref, ori_ref, coef_ref, dd_ref, *rest):
    if last:
        old_fld, part, acc, xs, xg, xq, xo, xc, it = rest
    else:
        part, acc, xs, xg, xq, xo, xc, it = rest
    d = rank_of(sizes)
    dd = dd_ref[...]
    dh = dd[0:NODES, :]
    pieces = [[[], []] for _ in range(VARS)]
    for h in range(2):
        u = [fld[h, v * NODES : v * NODES + NODES, :] for v in range(VARS)]
        inv = 1.0 / u[0]
        speeds = [u[i] * inv for i in range(1, 4)]
        p = 0.4 * (u[4] - 0.5 * (u[1] * speeds[0] + u[2] * speeds[1] + u[3] * speeds[2]))
        fl = fluxes(u, speeds, p)
        for v in range(VARS):
            hl = [split(fl[a][v]) for a in range(3)]
            pieces[v][0].append(jnp.concatenate([x[0] for x in hl], 0))
            pieces[v][1].append(jnp.concatenate([x[1] for x in hl], 0))
    for v in range(VARS):
        hi = mm(dd, jnp.concatenate(pieces[v][0], 1))
        lo = mm(dh, jnp.concatenate(pieces[v][1], 1))
        vol = hi[0:NODES, :] + hi[NODES : 2 * NODES, :] + lo
        for h in range(2):
            acc[h, v * NODES : v * NODES + NODES, :] = vol[:, h * LANES : h * LANES + LANES]
    for v in range(VARS):
        for f in range(FACES):
            for h in range(2):
                t = face_rows(fld, h, v, f)
                b = v * 256
                xs[pl.ds(b + 2 * f + h, 16, stride=16), :] = t
                xg[pl.ds(b + 2 * (f ^ 1) + h, 16, stride=16), :] = t
                xq[pl.ds(b + 2 * (f ^ 1) + 1 - h, 16, stride=16), :] = t
    it[...] = jnp.zeros((32, LANES), I32)
    for h in range(2):
        it[pl.ds(h, FACES, stride=2), :] = nb_ref[:, h * LANES : h * LANES + LANES]
        it[pl.ds(16 + h, FACES, stride=2), :] = ori_ref[:, h * LANES : h * LANES + LANES]
    t = it[0:16, :] - d * EL
    turn = it[16:32, :]
    row = iota((16, LANES), 0)
    local = (t >= 0) & (t < EL) & (row < 12)
    same = ((t >> 7) & 1) == (row & 1)
    idx = t & 127
    b0, b1, b2 = (turn & 1) != 0, (turn & 2) != 0, (turn & 4) != 0
    for v in range(VARS):
        got = []
        for m in range(16):
            rows = slice(v * 256 + m * 16, v * 256 + m * 16 + 16)
            ga = jnp.take_along_axis(xg[rows, :], idx, axis=1)
            gb = jnp.take_along_axis(xq[rows, :], idx, axis=1)
            got.append(jnp.where(same, ga, gb))
        for m, x in enumerate(turned(got, b0, b1, b2)):
            xo[v * 256 + m * 16 : v * 256 + m * 16 + 16, :] = x
    axis_is = (row < 4, (row >= 4) & (row < 8))
    half_sign = jnp.where((row & 2) != 0, 0.5, -0.5)
    for m in range(16):
        rows = [slice(v * 256 + m * 16, v * 256 + m * 16 + 16) for v in range(VARS)]
        cor = correction([xs[r, :] for r in rows], [xo[r, :] for r in rows], axis_is, half_sign)
        for v in range(VARS):
            xc[rows[v], :] = jnp.where(local, LIFT * cor[v], 0.0)
    for v in range(VARS):
        for f in range(FACES):
            for h in range(2):
                add_face_rows(
                    acc, h, v, f, xc[pl.ds(v * 256 + 2 * f + h, 16, stride=16), :]
                )
    for h in range(2):
        coef = coef_ref[0:1, h * LANES : h * LANES + LANES]
        for v in range(VARS):
            rows = slice(v * NODES, v * NODES + NODES)
            new = fld[h, rows, :] - coef * acc[h, rows, :]
            if last:
                new = 0.5 * old_fld[h, rows, :] + 0.5 * new
            part[h, rows, :] = new


def finish_kernel(last, part, g, r_a, r_b, rows_ref, ohs, coef_ref, *rest):
    if last:
        out, ro, y, e = rest
    else:
        hot_ref, code_ref, out, g_next, ro, y, e = rest
    lane = iota((80, LANES), 1)
    ro[0:80, :] = jnp.where(lane < 32, r_a[...], r_b[...])
    ro[80:128, :] = jnp.zeros((48, LANES), F32)
    code = pltpu.roll(rows_ref[0:8, :], 64, 1).astype(I32)
    turn = pltpu.roll(rows_ref[8:16, :], 64, 1).astype(I32)
    x = [ro[pl.ds(m, 8, stride=16), :] for m in range(16)]
    for m, val in enumerate(turned(x, (turn & 1) != 0, (turn & 2) != 0, (turn & 4) != 0)):
        y[8 * m : 8 * m + 8, :] = val
    live = iota((16, LANES), 1) < 64
    face = jnp.where(live, jnp.broadcast_to(code[0:1, :], (16, LANES)) >> 8, 0)
    axis_is = (face < 2, (face >= 2) & (face < 4))
    half_sign = jnp.where((face & 1) != 0, 0.5, -0.5)
    inner = [pltpu.roll(g[16 * v : 16 * v + 16, :], 64, 1) for v in range(VARS)]
    outer = [y[pl.ds(v, 16, stride=8), :] for v in range(VARS)]
    cor = correction(inner, outer, axis_is, half_sign)
    e[...] = jnp.zeros((ROWS, LANES), F32)
    for v in range(VARS):
        for f in range(FACES):
            add_face_rows(
                e, None, v, f, jnp.where(live & (face == f), cor[v], 0.0)
            )
    spread = mm(jnp.concatenate(split(e[...]), 0), ohs[...])
    scale = LIFT * (0.5 if last else 1.0)
    for h in range(2):
        coef = scale * coef_ref[0:1, h * LANES : h * LANES + LANES]
        lanes = slice(h * LANES, h * LANES + LANES)
        for v in range(VARS):
            rows = slice(v * NODES, v * NODES + NODES)
            low = slice(ROWS + v * NODES, ROWS + v * NODES + NODES)
            new = part[h, rows, :] - coef * (spread[rows, lanes] + spread[low, lanes])
            if last:
                out[v, :, lanes] = new
            else:
                out[h, rows, :] = new
    if not last:
        asked = jnp.broadcast_to(code_ref[0:1, :].astype(I32) >> 8, (16, LANES))
        requested(out, hot_ref[...], asked, e, g_next)


def call(body, out_shape, scratch, cost, args, hbm=(), spare=None):
    spec = pl.BlockSpec(memory_space=pltpu.VMEM)
    specs = []
    for i, a in enumerate(args):
        if i in hbm:
            specs.append(pl.BlockSpec(memory_space=pltpu.HBM))
        elif a.dtype == I32 and a.ndim == 1:
            specs.append(pl.BlockSpec(memory_space=pltpu.SMEM))
        else:
            specs.append(spec)
    return pl.pallas_call(
        body,
        out_shape=out_shape,
        in_specs=specs,
        out_specs=jax.tree.map(lambda _: spec, out_shape),
        scratch_shapes=scratch,
        cost_estimate=pl.CostEstimate(flops=cost, bytes_accessed=cost, transcendentals=0),
        compiler_params=pltpu.CompilerParams(vmem_limit_bytes=32 * 1024 * 1024),
    )(*[pltpu.with_memory_space_constraint(a, pltpu.HBM) if i in hbm else a for i, a in enumerate(args)])


def shape(*dims, dtype=F32):
    return jax.ShapeDtypeStruct(dims, dtype)


def per_device(sizes, old_state, element_size, old_start, neighbour, orientation):
    n = sizes[0] * sizes[1] * sizes[2]
    pairs_a = [(i, i ^ 1) for i in range(n)]
    pairs_b = [(i, (i + 1) % n if i % 2 else (i - 1) % n) for i in range(n)]

    size = element_size.reshape(1, EL)
    deriv = jnp.asarray(node_derivatives())
    s_a, s_b, rows, col, old_v, nb_v, ori_v = call(
        functools.partial(send_kernel, sizes),
        (
            shape(ROWS + 8, LANES),
            shape(ROWS + 8, LANES),
            shape(16, LANES),
            shape(64, LANES),
            shape(*old_state.shape),
            shape(FACES, EL, dtype=I32),
            shape(FACES, EL, dtype=I32),
        ),
        [
            pltpu.VMEM((16, EL), F32),
            pltpu.SMEM(old_start.shape, I32),
            pltpu.SemaphoreType.DMA((3 + VARS,)),
        ],
        10000,
        (old_start, old_state, neighbour, orientation),
        hbm=(0, 1, 2, 3),
    )
    r_a = lax.ppermute(s_a, AXES, pairs_a)
    r_b = lax.ppermute(s_b, AXES, pairs_b)
    own, ohs, dd, coef = call(
        functools.partial(own_kernel, sizes),
        (
            shape(2, ROWS, LANES),
            shape(LANES, EL, dtype=BF),
            shape(2 * NODES, 3 * NODES, dtype=BF),
            shape(1, EL),
        ),
        [
            pltpu.VMEM((NODES, 3 * NODES), F32),
            pltpu.VMEM((1, EL), F32),
            pltpu.SemaphoreType.DMA((2,)),
        ],
        10000,
        (old_start, old_v, col, deriv, size),
        hbm=(3, 4),
    )
    table = pltpu.VMEM((ROWS, LANES), F32)
    fld, hot, code, g = call(
        functools.partial(join_kernel, sizes),
        (
            shape(2, ROWS, LANES),
            shape(EL, LANES, dtype=BF),
            shape(8, LANES),
            shape(80, LANES),
        ),
        [table],
        10000,
        (old_start, own, r_a, r_b, rows),
    )

    def exchange(x):
        wrap_b = pairs_b
        r_a = lax.ppermute(x, AXES, pairs_a)
        r_b = lax.ppermute(x, AXES, wrap_b)
        return r_a, r_b

    def local(last, *args):
        faces = pltpu.VMEM((VARS * 256, LANES), F32)
        return call(
            functools.partial(local_kernel, sizes, last),
            shape(2, ROWS, LANES),
            [pltpu.VMEM((2, ROWS, LANES), F32)] + [faces] * 5 + [pltpu.VMEM((32, LANES), I32)],
            20000,
            args,
        )

    scratch = [pltpu.VMEM((LANES, LANES), F32), pltpu.VMEM((LANES, LANES), F32), table]
    r_a, r_b = exchange(g)
    part = local(False, fld, nb_v, ori_v, coef, dd)
    first, g2 = call(
        functools.partial(finish_kernel, False),
        (shape(2, ROWS, LANES), shape(80, LANES)),
        scratch,
        10000,
        (part, g, r_a, r_b, rows, ohs, coef, hot, code),
    )
    r_a, r_b = exchange(g2)
    part = local(True, first, nb_v, ori_v, coef, dd, fld)
    return call(
        functools.partial(finish_kernel, True),
        shape(VARS, NODES, EL),
        scratch,
        10000,
        (part, g2, r_a, r_b, rows, ohs, coef),
    )


def solution(mesh):
    sizes = tuple(mesh.shape[a] for a in AXES)
    in_specs = (P(None, None, AXES), P(AXES), P(), P(None, AXES), P(None, AXES))
    return jax.shard_map(
        functools.partial(per_device, sizes),
        mesh=mesh,
        in_specs=in_specs,
        out_specs=P(None, None, AXES),
        check_vma=False,
    )
```

```python
import functools

import jax
import jax.numpy as jnp
import numpy as np
from jax import lax
from jax.experimental import pallas as pl
from jax.experimental.pallas import tpu as pltpu
from jax.sharding import PartitionSpec as P

AXES = ("gx", "gy", "gz")
TIME_STEP = 0.03
LIFT = 6.0
VARS = 5
NODES = 64
EL = 256
LANES = 128
REMOTE = 32
FACES = 6
ROWS = VARS * NODES
BF = jnp.bfloat16
F32 = jnp.float32
I32 = jnp.int32


def gll_derivative():
    points = np.array([-1.0, -1.0 / np.sqrt(5.0), 1.0 / np.sqrt(5.0), 1.0])
    weights = np.array(
        [1.0 / np.prod([points[c] - points[p] for p in range(4) if p != c]) for c in range(4)]
    )
    matrix = np.zeros((4, 4))
    for row in range(4):
        for col in range(4):
            if row != col:
                matrix[row, col] = weights[col] / weights[row] / (points[row] - points[col])
        matrix[row, row] = -np.sum(matrix[row])
    return matrix


def node_derivatives():
    d, one = gll_derivative(), np.eye(4)
    parts = [
        np.kron(np.kron(d, one), one),
        np.kron(np.kron(one, d), one),
        np.kron(np.kron(one, one), d),
    ]
    return np.concatenate(parts, axis=1).astype(np.float32)


def iota(shape, dim):
    return lax.broadcasted_iota(I32, shape, dim)


def split(x):
    hi = x.astype(BF)
    return hi, (x - hi.astype(F32)).astype(BF)


def mm(a, b):
    return jnp.dot(a, b, preferred_element_type=F32)


def rows_at(lead, base, f, i=None):
    if f < 2:
        rows = pl.ds(base + 48 * f, 16)
    elif f < 4:
        rows = pl.ds(base + 12 * (f - 2) + 16 * i, 4)
    else:
        rows = pl.ds(base + 3 * (f - 4), 16, stride=4)
    return (rows, slice(None)) if lead is None else (lead, rows, slice(None))


def face_rows(ref, lead, v, f):
    if f in (2, 3):
        return jnp.concatenate([ref[rows_at(lead, v * NODES, f, i)] for i in range(4)], 0)
    return ref[rows_at(lead, v * NODES, f)]


def add_face_rows(ref, lead, v, f, val):
    if f in (2, 3):
        for i in range(4):
            r = rows_at(lead, v * NODES, f, i)
            ref[r] = ref[r] + val[4 * i : 4 * i + 4, :]
    else:
        r = rows_at(lead, v * NODES, f)
        ref[r] = ref[r] + val


def rank_of(sizes):
    return (lax.axis_index("gx") * sizes[1] + lax.axis_index("gy")) * sizes[2] + lax.axis_index("gz")


def places(mask):
    count = mask.shape[0]
    upper = jnp.where(iota((EL, EL), 0) <= iota((EL, EL), 1), 1.0, 0.0).astype(BF)
    inclusive = mm(mask.astype(BF), upper)
    total = jnp.broadcast_to(inclusive[:, EL - 1 : EL], (count, LANES)).astype(BF)
    r, c = iota((count, count), 0), iota((count, count), 1)
    lower = jnp.where((c < r) & ((c >> 3) == (r >> 3)), 1.0, 0.0).astype(BF)
    offset = mm(lower, total)[:, 0:1]
    return jnp.where(mask > 0.5, inclusive + offset - 1.0, -1.0)


def listed(place, values):
    slot = iota((REMOTE, EL), 0).astype(F32)
    accs = [jnp.zeros((REMOTE, EL), F32) for _ in values]
    for f in range(FACES):
        hit = place[f : f + 1, :] == slot
        accs = [jnp.where(hit, x[f : f + 1, :], acc) for x, acc in zip(values, accs)]
    return [jnp.sum(acc, 1, keepdims=True) for acc in accs]


def send_kernel(sizes, start_hbm, old, nb, ori, s_a, s_b, rows_ref, col_ref, old_v, nb_v, ori_v, edge, mk, start, sem):
    n = sizes[0] * sizes[1] * sizes[2]
    copies = [
        pltpu.make_async_copy(nb, nb_v, sem.at[0]),
        pltpu.make_async_copy(ori, ori_v, sem.at[1]),
        pltpu.make_async_copy(start_hbm, start, sem.at[2]),
    ] + [pltpu.make_async_copy(old.at[v], old_v.at[v], sem.at[3 + v]) for v in range(VARS)]
    for copy in copies:
        copy.start()
    d = rank_of(sizes)
    even = (d & 1) == 0
    up = jnp.where(d + 1 == n, 0, d + 1) * EL
    down = jnp.where(d == 0, n - 1, d - 1) * EL
    mk[...] = jnp.zeros((16, EL), F32)
    copies[0].wait()
    nb = nb_v[...]
    rel = [nb - jnp.where(even, up, down), nb - jnp.where(even, down, up)]
    for k in range(2):
        mk[8 * k : 8 * k + FACES, :] = jnp.where((rel[k] >= 0) & (rel[k] < EL), 1.0, 0.0)
    place = places(mk[...])
    copies[1].wait()
    face = iota((FACES, EL), 0)
    own = (face * EL + iota((FACES, EL), 1) + 2048 * ori_v[...]).astype(F32)
    lists = []
    for k in range(2):
        lists.append(listed(place[8 * k : 8 * k + 8, :], [((face ^ 1) * EL + rel[k]).astype(F32), own]))
    col = jnp.concatenate([lists[0][0], lists[1][0], lists[0][1], lists[1][1]], 0)
    wide = jnp.broadcast_to(col, (LANES, LANES))
    row = jnp.transpose(wide)[0:8, :]
    turn = jnp.floor(row * (1.0 / 2048.0))
    code = row - 2048.0 * turn
    rows_ref[0:8, :] = code
    rows_ref[8:16, :] = turn
    col_ref[...] = wide[64:128, :]
    for out in (s_a, s_b):
        out[ROWS : ROWS + 8, :] = code
        out[ROWS + 8 : ROWS + 16, :] = turn

    copies[2].wait()
    o = start[d] - d * EL
    edge[0:4, :] = jnp.broadcast_to(o, (4, LANES))
    edge[4:8, :] = jnp.broadcast_to(start[d + 1] - d * EL, (4, LANES))
    first = EL - o
    q, rot = first >> 7, first & 127
    keep = iota((NODES, LANES), 1) < LANES - rot
    back = (LANES - rot) & 127
    t0 = pl.ds(pl.multiple_of(q * LANES, LANES), LANES)
    t1 = pl.ds(pl.multiple_of(jnp.minimum(q + 1, 3) * LANES, LANES), LANES)
    for copy in copies[3:]:
        copy.wait()

    def put(to_up, to_down):
        for v in range(VARS):
            rows = slice(v * NODES, v * NODES + NODES)
            to_up[rows, :] = jnp.where(
                keep, pltpu.roll(old_v[v, :, t0], back, 1), pltpu.roll(old_v[v, :, t1], back, 1)
            )
            to_down[rows, :] = pltpu.roll(old_v[v, :, 0:LANES], o & 127, 1)

    @pl.when(even)
    def _():
        put(s_a, s_b)

    @pl.when(jnp.logical_not(even))
    def _():
        put(s_b, s_a)


def own_kernel(
    sizes, start_hbm, old, col_ref, d_hbm, size_hbm, own, ohs, dd, coef, d_v, size_v, start, sem
):
    copies = [
        pltpu.make_async_copy(start_hbm, start, sem.at[2]),
        pltpu.make_async_copy(d_hbm, d_v, sem.at[0]),
        pltpu.make_async_copy(size_hbm, size_v, sem.at[1]),
    ]
    for copy in copies:
        copy.start()
    d = rank_of(sizes)
    copies[0].wait()
    s = d * EL - start[d]
    q, rot = s >> 7, s & 127
    keep = iota((NODES, LANES), 1) < LANES - rot
    back = (LANES - rot) & 127
    for v in range(VARS):
        rows = slice(v * NODES, v * NODES + NODES)
        t = [
            pltpu.roll(
                old[v, :, pl.ds(pl.multiple_of(jnp.maximum(q + i, 0) * LANES, LANES), LANES)], back, 1
            )
            for i in range(3)
        ]
        own[0, rows, :] = jnp.where(keep, t[0], t[1])
        own[1, rows, :] = jnp.where(keep, t[1], t[2])
    code = col_ref[...].astype(I32)
    lane = iota((64, LANES), 1)
    for h in range(2):
        hit = jnp.where((code & 255) == lane + h * LANES, 1.0, 0.0).astype(BF)
        ohs[0:64, h * LANES : h * LANES + LANES] = hit
        ohs[64:128, h * LANES : h * LANES + LANES] = jnp.zeros((64, LANES), BF)
    for copy in copies[1:]:
        copy.wait()
    dd[...] = jnp.concatenate(split(d_v[...]), 0)
    coef[...] = (TIME_STEP * 2.0) / size_v[...]


def chosen(gs, face, v):
    acc = face_rows(gs, None, v, 0)
    for f in range(1, FACES):
        acc = jnp.where(face == f, face_rows(gs, None, v, f), acc)
    return acc


def requested(fld, hot, face, gs, g):
    both = jnp.concatenate([fld[0], fld[1]], 1)
    out = mm(jnp.concatenate(split(both), 0), hot)
    gs[...] = out[0:ROWS, :] + out[ROWS : 2 * ROWS, :]
    for v in range(VARS):
        g[16 * v : 16 * v + 16, :] = chosen(gs, face, v)


def join_kernel(sizes, own, r_a, r_b, rows_ref, edge, fld, hot_ref, code_ref, info, g, gs):
    even = (rank_of(sizes) & 1) == 0
    lane = iota((NODES, LANES), 1)
    below = lane < edge[0:1, :]
    above = lane + LANES >= edge[4:5, :]
    for v in range(VARS):
        rows = slice(v * NODES, v * NODES + NODES)
        a, b = r_a[rows, :], r_b[rows, :]
        fld[0, rows, :] = jnp.where(below, jnp.where(even, b, a), own[0, rows, :])
        fld[1, rows, :] = jnp.where(above, jnp.where(even, a, b), own[1, rows, :])
    lane8 = iota((8, LANES), 1)
    code = jnp.where(
        lane8 < 32,
        r_a[ROWS : ROWS + 8, :],
        jnp.where(lane8 < 64, r_b[ROWS : ROWS + 8, :], rows_ref[0:8, :]),
    ).astype(I32)
    code_ref[...] = code
    lane16 = iota((16, LANES), 1)
    info[...] = jnp.where(
        lane16 < 96, pltpu.roll(rows_ref[...], 64, 1), r_b[ROWS : ROWS + 16, :]
    ).astype(I32)
    spot = jnp.broadcast_to(code[0:1, :] & 255, (EL, LANES))
    hot = jnp.where(spot == iota((EL, LANES), 0), 1.0, 0.0).astype(BF)
    hot_ref[...] = hot
    face = jnp.broadcast_to(code[0:1, :] >> 8, (16, LANES))
    requested(fld, hot, face, gs, g)


def fluxes(u, speeds, p):
    out = []
    for a in range(3):
        s = speeds[a]
        row = [u[0] * s, u[1] * s, u[2] * s, u[3] * s, (u[4] + p) * s]
        row[1 + a] = row[1 + a] + p
        out.append(row)
    return out


def directed(u, axis_is):
    inv = 1.0 / u[0]
    p = 0.4 * (u[4] - 0.5 * ((u[1] * u[1] + u[2] * u[2] + u[3] * u[3]) * inv))
    mom = jnp.where(axis_is[0], u[1], jnp.where(axis_is[1], u[2], u[3]))
    s = mom * inv
    flux = [u[0] * s] + [u[i] * s for i in range(1, 4)] + [(u[4] + p) * s]
    zero = jnp.zeros_like(p)
    flux[1] = flux[1] + jnp.where(axis_is[0], p, zero)
    flux[2] = flux[2] + jnp.where(axis_is[1], p, zero)
    flux[3] = flux[3] + jnp.where(axis_is[0] | axis_is[1], zero, p)
    return flux, jnp.abs(s) + jnp.sqrt(1.4 * p * inv)


def correction(inner, outer, axis_is, half_sign):
    fi, si = directed(inner, axis_is)
    fo, so = directed(outer, axis_is)
    lam = 0.5 * jnp.maximum(si, so)
    return [half_sign * (fo[v] - fi[v]) - lam * (outer[v] - inner[v]) for v in range(VARS)]


def turned(x, b0, b1, b2):
    x = [jnp.where(b1, x[4 * (3 - p) + q], x[4 * p + q]) for p in range(4) for q in range(4)]
    x = [jnp.where(b2, x[4 * p + 3 - q], x[4 * p + q]) for p in range(4) for q in range(4)]
    return [jnp.where(b0, x[4 * t + s], x[4 * s + t]) for s in range(4) for t in range(4)]


def local_kernel(sizes, last, fld, nb_ref, ori_ref, coef_ref, dd_ref, *rest):
    if last:
        old_fld, part, acc, xs, xg, xq, xo, xc, it = rest
    else:
        part, acc, xs, xg, xq, xo, xc, it = rest
    d = rank_of(sizes)
    dd = dd_ref[...]
    dh = dd[0:NODES, :]
    pieces = [[[], []] for _ in range(VARS)]
    for h in range(2):
        u = [fld[h, v * NODES : v * NODES + NODES, :] for v in range(VARS)]
        inv = 1.0 / u[0]
        speeds = [u[i] * inv for i in range(1, 4)]
        p = 0.4 * (u[4] - 0.5 * (u[1] * speeds[0] + u[2] * speeds[1] + u[3] * speeds[2]))
        fl = fluxes(u, speeds, p)
        for v in range(VARS):
            hl = [split(fl[a][v]) for a in range(3)]
            pieces[v][0].append(jnp.concatenate([x[0] for x in hl], 0))
            pieces[v][1].append(jnp.concatenate([x[1] for x in hl], 0))
    for v in range(VARS):
        hi = mm(dd, jnp.concatenate(pieces[v][0], 1))
        lo = mm(dh, jnp.concatenate(pieces[v][1], 1))
        vol = hi[0:NODES, :] + hi[NODES : 2 * NODES, :] + lo
        for h in range(2):
            acc[h, v * NODES : v * NODES + NODES, :] = vol[:, h * LANES : h * LANES + LANES]
    for v in range(VARS):
        for f in range(FACES):
            for h in range(2):
                t = face_rows(fld, h, v, f)
                b = v * 256
                xs[pl.ds(b + 2 * f + h, 16, stride=16), :] = t
                xg[pl.ds(b + 2 * (f ^ 1) + h, 16, stride=16), :] = t
                xq[pl.ds(b + 2 * (f ^ 1) + 1 - h, 16, stride=16), :] = t
    it[...] = jnp.zeros((32, LANES), I32)
    for h in range(2):
        it[pl.ds(h, FACES, stride=2), :] = nb_ref[:, h * LANES : h * LANES + LANES]
        it[pl.ds(16 + h, FACES, stride=2), :] = ori_ref[:, h * LANES : h * LANES + LANES]
    t = it[0:16, :] - d * EL
    turn = it[16:32, :]
    row = iota((16, LANES), 0)
    local = (t >= 0) & (t < EL) & (row < 12)
    same = ((t >> 7) & 1) == (row & 1)
    idx = t & 127
    b0, b1, b2 = (turn & 1) != 0, (turn & 2) != 0, (turn & 4) != 0
    for v in range(VARS):
        got = []
        for m in range(16):
            rows = slice(v * 256 + m * 16, v * 256 + m * 16 + 16)
            ga = jnp.take_along_axis(xg[rows, :], idx, axis=1)
            gb = jnp.take_along_axis(xq[rows, :], idx, axis=1)
            got.append(jnp.where(same, ga, gb))
        for m, x in enumerate(turned(got, b0, b1, b2)):
            xo[v * 256 + m * 16 : v * 256 + m * 16 + 16, :] = x
    axis_is = (row < 4, (row >= 4) & (row < 8))
    half_sign = jnp.where((row & 2) != 0, 0.5, -0.5)
    for m in range(16):
        rows = [slice(v * 256 + m * 16, v * 256 + m * 16 + 16) for v in range(VARS)]
        cor = correction([xs[r, :] for r in rows], [xo[r, :] for r in rows], axis_is, half_sign)
        for v in range(VARS):
            xc[rows[v], :] = jnp.where(local, LIFT * cor[v], 0.0)
    for v in range(VARS):
        for f in range(FACES):
            for h in range(2):
                add_face_rows(
                    acc, h, v, f, xc[pl.ds(v * 256 + 2 * f + h, 16, stride=16), :]
                )
    for h in range(2):
        coef = coef_ref[0:1, h * LANES : h * LANES + LANES]
        for v in range(VARS):
            rows = slice(v * NODES, v * NODES + NODES)
            new = fld[h, rows, :] - coef * acc[h, rows, :]
            if last:
                new = 0.5 * old_fld[h, rows, :] + 0.5 * new
            part[h, rows, :] = new


def face_terms(inner, outer, info, live, ro, y, e):
    ro[0:80, :] = outer
    ro[80:128, :] = jnp.zeros((48, LANES), F32)
    turn = info[8:16, :]
    x = [ro[pl.ds(m, 8, stride=16), :] for m in range(16)]
    for m, val in enumerate(turned(x, (turn & 1) != 0, (turn & 2) != 0, (turn & 4) != 0)):
        y[8 * m : 8 * m + 8, :] = val
    face = jnp.where(live, jnp.broadcast_to(info[0:1, :], (16, LANES)) >> 8, -1)
    axis_is = (face < 2, (face >= 2) & (face < 4))
    half_sign = jnp.where((face & 1) != 0, 0.5, -0.5)
    behind = [y[pl.ds(v, 16, stride=8), :] for v in range(VARS)]
    here = [inner[16 * v : 16 * v + 16, :] for v in range(VARS)]
    cor = correction(here, behind, axis_is, half_sign)
    e[...] = jnp.zeros((ROWS, LANES), F32)
    for v in range(VARS):
        for f in range(FACES):
            add_face_rows(e, None, v, f, jnp.where(face == f, cor[v], 0.0))


def added(part, spread, coef_ref, scale, put):
    for h in range(2):
        lanes = slice(h * LANES, h * LANES + LANES)
        coef = scale * coef_ref[0:1, lanes]
        for v in range(VARS):
            rows = slice(v * NODES, v * NODES + NODES)
            low = slice(ROWS + v * NODES, ROWS + v * NODES + NODES)
            put(h, v, part[h, rows, :] - coef * (spread[rows, lanes] + spread[low, lanes]))


def near_kernel(part, g, r_a, info, ohs, coef_ref, hot_ref, code_ref, fp, pb, ro, y, e, g1):
    lane = iota((16, LANES), 1)
    face_terms(pltpu.roll(g[...], 64, 1), r_a[...], info, lane < 32, ro, y, e)
    spread = mm(jnp.concatenate(split(e[...]), 0), ohs[...])

    def put(h, v, new):
        fp[h, v * NODES : v * NODES + NODES, :] = new

    added(part, spread, coef_ref, LIFT, put)
    hot = hot_ref[...]
    asked = jnp.broadcast_to(code_ref[0:1, :] >> 8, (16, LANES))
    requested(fp, hot, asked, e, g1)
    lane = iota((80, LANES), 1)
    pb[0:80, :] = jnp.where(lane < 32, pltpu.roll(g1[...], 96, 1), g[...])
    ch, cl = split(jnp.broadcast_to(LIFT * coef_ref[0:1, :], (16, EL)))
    pb[80:96, :] = mm(ch, hot) + mm(cl, hot)


def pair_kernel(info, rows_ref, after, pairs):
    theirs = jnp.transpose(jnp.broadcast_to(info[0:1, :].astype(F32), (LANES, LANES))).astype(I32)
    mine = jnp.broadcast_to(rows_ref[0:1, :].astype(I32), (LANES, LANES))
    row, lane = iota((LANES, LANES), 0), iota((LANES, LANES), 1)
    on = ((theirs & 255) == (mine & 255)) & (row >= 96) & (lane >= 32) & (lane < 64)
    pairs[...] = jnp.where(on, 1.0, 0.0).astype(BF)


def far_kernel(
    fp, g, r_b, info, rows_ref, ohs, pairs, coef_ref, hot_ref, code_ref, first, g1, o1, ro, y, e
):
    lane = iota((80, LANES), 1)
    mine = pltpu.roll(g[...], 64, 1)
    got = r_b[0:80, :]
    lane16 = iota((16, LANES), 1)
    live = ((lane16 >= 32) & (lane16 < 64)) | (lane16 >= 96)
    face_terms(
        jnp.where(lane < 64, mine, got), jnp.where(lane < 64, got, mine), info, live, ro, y, e
    )
    parts = jnp.concatenate(split(e[...]), 0)
    spread = mm(parts, ohs[...])

    def put(h, v, new):
        first[h, v * NODES : v * NODES + NODES, :] = new

    added(fp, spread, coef_ref, LIFT, put)
    theirs = mm(parts, pairs[...])
    e[...] = theirs[0:ROWS, :] + theirs[ROWS : 2 * ROWS, :]
    face = jnp.broadcast_to(rows_ref[0:1, :].astype(I32) >> 8, (16, LANES))
    coef = r_b[80:81, :]
    for v in range(VARS):
        rows = slice(16 * v, 16 * v + 16)
        o1[rows, :] = pltpu.roll(r_b[rows, :], 32, 1) - coef * chosen(e, face, v)
    asked = jnp.broadcast_to(code_ref[0:1, :] >> 8, (16, LANES))
    requested(first, hot_ref[...], asked, e, g1)


def last_kernel(part, g1, r_a, o1, info, ohs, coef_ref, out, ro, y, e):
    lane = iota((80, LANES), 1)
    outer = jnp.where(lane < 32, r_a[...], o1[...])
    face_terms(pltpu.roll(g1[...], 64, 1), outer, info, iota((16, LANES), 1) < 64, ro, y, e)
    spread = mm(jnp.concatenate(split(e[...]), 0), ohs[...])

    def put(h, v, new):
        out[v, :, h * LANES : h * LANES + LANES] = new

    added(part, spread, coef_ref, 0.5 * LIFT, put)


def call(body, out_shape, scratch, cost, args, hbm=(), spare=None):
    spec = pl.BlockSpec(memory_space=pltpu.VMEM)
    specs = []
    for i, a in enumerate(args):
        if i in hbm:
            specs.append(pl.BlockSpec(memory_space=pltpu.HBM))
        elif a.dtype == I32 and a.ndim == 1:
            specs.append(pl.BlockSpec(memory_space=pltpu.SMEM))
        else:
            specs.append(spec)
    return pl.pallas_call(
        body,
        out_shape=out_shape,
        in_specs=specs,
        out_specs=jax.tree.map(lambda _: spec, out_shape),
        scratch_shapes=scratch,
        cost_estimate=pl.CostEstimate(flops=cost, bytes_accessed=cost, transcendentals=0),
        compiler_params=pltpu.CompilerParams(vmem_limit_bytes=32 * 1024 * 1024),
    )(*[pltpu.with_memory_space_constraint(a, pltpu.HBM) if i in hbm else a for i, a in enumerate(args)])


def shape(*dims, dtype=F32):
    return jax.ShapeDtypeStruct(dims, dtype)


def per_device(sizes, old_state, element_size, old_start, neighbour, orientation):
    n = sizes[0] * sizes[1] * sizes[2]
    pairs_a = [(i, i ^ 1) for i in range(n)]
    pairs_b = [(i, (i + 1) % n if i % 2 else (i - 1) % n) for i in range(n)]

    size = element_size.reshape(1, EL)
    deriv = jnp.asarray(node_derivatives())
    s_a, s_b, rows, col, old_v, nb_v, ori_v, edge = call(
        functools.partial(send_kernel, sizes),
        (
            shape(ROWS + 16, LANES),
            shape(ROWS + 16, LANES),
            shape(16, LANES),
            shape(64, LANES),
            shape(*old_state.shape),
            shape(FACES, EL, dtype=I32),
            shape(FACES, EL, dtype=I32),
            shape(8, LANES, dtype=I32),
        ),
        [
            pltpu.VMEM((16, EL), F32),
            pltpu.SMEM(old_start.shape, I32),
            pltpu.SemaphoreType.DMA((3 + VARS,)),
        ],
        10000,
        (old_start, old_state, neighbour, orientation),
        hbm=(0, 1, 2, 3),
    )
    r_a = lax.ppermute(s_a, AXES, pairs_a)
    r_b = lax.ppermute(s_b, AXES, pairs_b)
    own, ohs, dd, coef = call(
        functools.partial(own_kernel, sizes),
        (
            shape(2, ROWS, LANES),
            shape(LANES, EL, dtype=BF),
            shape(2 * NODES, 3 * NODES, dtype=BF),
            shape(1, EL),
        ),
        [
            pltpu.VMEM((NODES, 3 * NODES), F32),
            pltpu.VMEM((1, EL), F32),
            pltpu.SMEM(old_start.shape, I32),
            pltpu.SemaphoreType.DMA((3,)),
        ],
        10000,
        (old_start, old_v, col, deriv, size),
        hbm=(0, 3, 4),
    )
    table = pltpu.VMEM((ROWS, LANES), F32)
    square = pltpu.VMEM((LANES, LANES), F32)
    traces = shape(80, LANES)
    state = shape(2, ROWS, LANES)
    fld, hot, code, info, g = call(
        functools.partial(join_kernel, sizes),
        (
            state,
            shape(EL, LANES, dtype=BF),
            shape(8, LANES, dtype=I32),
            shape(16, LANES, dtype=I32),
            traces,
        ),
        [table],
        10000,
        (own, r_a, r_b, rows, edge),
    )

    def local(last, *args):
        faces = pltpu.VMEM((VARS * 256, LANES), F32)
        return call(
            functools.partial(local_kernel, sizes, last),
            state,
            [pltpu.VMEM((2, ROWS, LANES), F32)] + [faces] * 5 + [pltpu.VMEM((32, LANES), I32)],
            20000,
            args,
        )

    r_a = lax.ppermute(g, AXES, pairs_a)
    part = local(False, fld, nb_v, ori_v, coef, dd)
    fp, pb = call(
        near_kernel,
        (state, shape(96, LANES)),
        [square, square, table, pltpu.VMEM((80, LANES), F32)],
        10000,
        (part, g, r_a, info, ohs, coef, hot, code),
    )
    r_b = lax.ppermute(pb, AXES, pairs_b)
    pairs = call(pair_kernel, shape(LANES, LANES, dtype=BF), [], 10000, (info, rows, fp))
    first, g1, o1 = call(
        far_kernel,
        (state, traces, traces),
        [square, square, table],
        10000,
        (fp, g, r_b, info, rows, ohs, pairs, coef, hot, code),
    )
    r_a = lax.ppermute(g1, AXES, pairs_a)
    part = local(True, first, nb_v, ori_v, coef, dd, fld)
    return call(
        last_kernel,
        shape(VARS, NODES, EL),
        [square, square, table],
        10000,
        (part, g1, r_a, o1, info, ohs, coef),
    )


def solution(mesh):
    sizes = tuple(mesh.shape[a] for a in AXES)
    in_specs = (P(None, None, AXES), P(AXES), P(), P(None, AXES), P(None, AXES))
    return jax.shard_map(
        functools.partial(per_device, sizes),
        mesh=mesh,
        in_specs=in_specs,
        out_specs=P(None, None, AXES),
        check_vma=False,
    )
```

```python
import functools

import jax
import jax.numpy as jnp
import numpy as np
from jax import lax
from jax.experimental import pallas as pl
from jax.experimental.pallas import tpu as pltpu
from jax.sharding import PartitionSpec as P

AXES = ("gx", "gy", "gz")
TIME_STEP = 0.03
LIFT = 6.0
VARS = 5
NODES = 64
EL = 256
LANES = 128
REMOTE = 32
FACES = 6
ROWS = VARS * NODES
BF = jnp.bfloat16
F32 = jnp.float32
I32 = jnp.int32


def gll_derivative():
    points = np.array([-1.0, -1.0 / np.sqrt(5.0), 1.0 / np.sqrt(5.0), 1.0])
    weights = np.array(
        [1.0 / np.prod([points[c] - points[p] for p in range(4) if p != c]) for c in range(4)]
    )
    matrix = np.zeros((4, 4))
    for row in range(4):
        for col in range(4):
            if row != col:
                matrix[row, col] = weights[col] / weights[row] / (points[row] - points[col])
        matrix[row, row] = -np.sum(matrix[row])
    return matrix


def node_derivatives():
    d, one = gll_derivative(), np.eye(4)
    parts = [
        np.kron(np.kron(d, one), one),
        np.kron(np.kron(one, d), one),
        np.kron(np.kron(one, one), d),
    ]
    return np.concatenate(parts, axis=1).astype(np.float32)


def iota(shape, dim):
    return lax.broadcasted_iota(I32, shape, dim)


def split(x):
    hi = x.astype(BF)
    return hi, (x - hi.astype(F32)).astype(BF)


def mm(a, b):
    return jnp.dot(a, b, preferred_element_type=F32)


def rows_at(lead, base, f, i=None):
    if f < 2:
        rows = pl.ds(base + 48 * f, 16)
    elif f < 4:
        rows = pl.ds(base + 12 * (f - 2) + 16 * i, 4)
    else:
        rows = pl.ds(base + 3 * (f - 4), 16, stride=4)
    return (rows, slice(None)) if lead is None else (lead, rows, slice(None))


def face_rows(ref, lead, v, f):
    if f in (2, 3):
        return jnp.concatenate([ref[rows_at(lead, v * NODES, f, i)] for i in range(4)], 0)
    return ref[rows_at(lead, v * NODES, f)]


def add_face_rows(ref, lead, v, f, val):
    if f in (2, 3):
        for i in range(4):
            r = rows_at(lead, v * NODES, f, i)
            ref[r] = ref[r] + val[4 * i : 4 * i + 4, :]
    else:
        r = rows_at(lead, v * NODES, f)
        ref[r] = ref[r] + val


def rank_of(sizes):
    return (lax.axis_index("gx") * sizes[1] + lax.axis_index("gy")) * sizes[2] + lax.axis_index("gz")


def places(mask):
    count = mask.shape[0]
    upper = jnp.where(iota((EL, EL), 0) <= iota((EL, EL), 1), 1.0, 0.0).astype(BF)
    inclusive = mm(mask.astype(BF), upper)
    total = jnp.broadcast_to(inclusive[:, EL - 1 : EL], (count, LANES)).astype(BF)
    r, c = iota((count, count), 0), iota((count, count), 1)
    lower = jnp.where((c < r) & ((c >> 3) == (r >> 3)), 1.0, 0.0).astype(BF)
    offset = mm(lower, total)[:, 0:1]
    return jnp.where(mask > 0.5, inclusive + offset - 1.0, -1.0)


def listed(place, values):
    slot = iota((REMOTE, EL), 0).astype(F32)
    accs = [jnp.zeros((REMOTE, EL), F32) for _ in values]
    for f in range(FACES):
        hit = place[f : f + 1, :] == slot
        accs = [jnp.where(hit, x[f : f + 1, :], acc) for x, acc in zip(values, accs)]
    return [jnp.sum(acc, 1, keepdims=True) for acc in accs]


def send_kernel(sizes, start_hbm, old, nb, ori, s_a, s_b, rows_ref, col_ref, old_v, nb_v, ori_v, edge, mk, start, sem):
    n = sizes[0] * sizes[1] * sizes[2]
    copies = [
        pltpu.make_async_copy(nb, nb_v, sem.at[0]),
        pltpu.make_async_copy(ori, ori_v, sem.at[1]),
        pltpu.make_async_copy(start_hbm, start, sem.at[2]),
    ] + [pltpu.make_async_copy(old.at[v], old_v.at[v], sem.at[3 + v]) for v in range(VARS)]
    for copy in copies:
        copy.start()
    d = rank_of(sizes)
    even = (d & 1) == 0
    up = jnp.where(d + 1 == n, 0, d + 1) * EL
    down = jnp.where(d == 0, n - 1, d - 1) * EL
    mk[...] = jnp.zeros((16, EL), F32)
    copies[0].wait()
    nb = nb_v[...]
    rel = [nb - jnp.where(even, up, down), nb - jnp.where(even, down, up)]
    for k in range(2):
        mk[8 * k : 8 * k + FACES, :] = jnp.where((rel[k] >= 0) & (rel[k] < EL), 1.0, 0.0)
    place = places(mk[...])
    copies[1].wait()
    face = iota((FACES, EL), 0)
    own = (face * EL + iota((FACES, EL), 1) + 2048 * ori_v[...]).astype(F32)
    lists = []
    for k in range(2):
        lists.append(listed(place[8 * k : 8 * k + 8, :], [((face ^ 1) * EL + rel[k]).astype(F32), own]))
    col = jnp.concatenate([lists[0][0], lists[1][0], lists[0][1], lists[1][1]], 0)
    wide = jnp.broadcast_to(col, (LANES, LANES))
    row = jnp.transpose(wide)[0:8, :]
    turn = jnp.floor(row * (1.0 / 2048.0))
    code = row - 2048.0 * turn
    rows_ref[0:8, :] = code
    rows_ref[8:16, :] = turn
    col_ref[...] = wide[64:128, :]
    s_a[ROWS : ROWS + 8, :] = code
    s_a[ROWS + 8 : ROWS + 16, :] = turn

    copies[2].wait()
    o = start[d] - d * EL
    edge[0:4, :] = jnp.broadcast_to(o, (4, LANES))
    edge[4:8, :] = jnp.broadcast_to(start[d + 1] - d * EL, (4, LANES))
    first = EL - o
    q, rot = first >> 7, first & 127
    keep = iota((NODES, LANES), 1) < LANES - rot
    back = (LANES - rot) & 127
    t0 = pl.ds(pl.multiple_of(q * LANES, LANES), LANES)
    t1 = pl.ds(pl.multiple_of(jnp.minimum(q + 1, 3) * LANES, LANES), LANES)
    for copy in copies[3:]:
        copy.wait()

    def put(to_up, to_down):
        for v in range(VARS):
            rows = slice(v * NODES, v * NODES + NODES)
            to_up[rows, :] = jnp.where(
                keep, pltpu.roll(old_v[v, :, t0], back, 1), pltpu.roll(old_v[v, :, t1], back, 1)
            )
            to_down[rows, :] = pltpu.roll(old_v[v, :, 0:LANES], o & 127, 1)

    @pl.when(even)
    def _():
        put(s_a, s_b)

    @pl.when(jnp.logical_not(even))
    def _():
        put(s_b, s_a)


def own_kernel(
    sizes, start_hbm, old, col_ref, d_hbm, size_hbm, own, ohs, dd, coef, d_v, size_v, start, sem
):
    copies = [
        pltpu.make_async_copy(start_hbm, start, sem.at[2]),
        pltpu.make_async_copy(d_hbm, d_v, sem.at[0]),
        pltpu.make_async_copy(size_hbm, size_v, sem.at[1]),
    ]
    for copy in copies:
        copy.start()
    d = rank_of(sizes)
    copies[0].wait()
    s = d * EL - start[d]
    q, rot = s >> 7, s & 127
    keep = iota((NODES, LANES), 1) < LANES - rot
    back = (LANES - rot) & 127
    for v in range(VARS):
        rows = slice(v * NODES, v * NODES + NODES)
        t = [
            pltpu.roll(
                old[v, :, pl.ds(pl.multiple_of(jnp.maximum(q + i, 0) * LANES, LANES), LANES)], back, 1
            )
            for i in range(3)
        ]
        own[0, rows, :] = jnp.where(keep, t[0], t[1])
        own[1, rows, :] = jnp.where(keep, t[1], t[2])
    code = col_ref[...].astype(I32)
    lane = iota((64, LANES), 1)
    for h in range(2):
        hit = jnp.where((code & 255) == lane + h * LANES, 1.0, 0.0).astype(BF)
        ohs[0:64, h * LANES : h * LANES + LANES] = hit
        ohs[64:128, h * LANES : h * LANES + LANES] = jnp.zeros((64, LANES), BF)
    for copy in copies[1:]:
        copy.wait()
    dd[...] = jnp.concatenate(split(d_v[...]), 0)
    coef[...] = (TIME_STEP * 2.0) / size_v[...]


def chosen(gs, face, v):
    acc = face_rows(gs, None, v, 0)
    for f in range(1, FACES):
        acc = jnp.where(face == f, face_rows(gs, None, v, f), acc)
    return acc


def requested(fld, hot, face, gs, g):
    both = jnp.concatenate([fld[0], fld[1]], 1)
    out = mm(jnp.concatenate(split(both), 0), hot)
    gs[...] = out[0:ROWS, :] + out[ROWS : 2 * ROWS, :]
    for v in range(VARS):
        g[16 * v : 16 * v + 16, :] = chosen(gs, face, v)


def join_kernel(sizes, own, r_a, r_b, c_b, rows_ref, edge, fld, hot_ref, code_ref, info, g, gs):
    even = (rank_of(sizes) & 1) == 0
    lane = iota((NODES, LANES), 1)
    below = lane < edge[0:1, :]
    above = lane + LANES >= edge[4:5, :]
    for v in range(VARS):
        rows = slice(v * NODES, v * NODES + NODES)
        a, b = r_a[rows, :], r_b[rows, :]
        fld[0, rows, :] = jnp.where(below, jnp.where(even, b, a), own[0, rows, :])
        fld[1, rows, :] = jnp.where(above, jnp.where(even, a, b), own[1, rows, :])
    lane8 = iota((8, LANES), 1)
    code = jnp.where(
        lane8 < 32,
        r_a[ROWS : ROWS + 8, :],
        jnp.where(lane8 < 64, c_b[0:8, :], rows_ref[0:8, :]),
    ).astype(I32)
    code_ref[...] = code
    lane16 = iota((16, LANES), 1)
    info[...] = jnp.where(
        lane16 < 96, pltpu.roll(rows_ref[...], 64, 1), c_b[...]
    ).astype(I32)
    spot = jnp.broadcast_to(code[0:1, :] & 255, (EL, LANES))
    hot = jnp.where(spot == iota((EL, LANES), 0), 1.0, 0.0).astype(BF)
    hot_ref[...] = hot
    face = jnp.broadcast_to(code[0:1, :] >> 8, (16, LANES))
    requested(fld, hot, face, gs, g)


def fluxes(u, speeds, p):
    out = []
    for a in range(3):
        s = speeds[a]
        row = [u[0] * s, u[1] * s, u[2] * s, u[3] * s, (u[4] + p) * s]
        row[1 + a] = row[1 + a] + p
        out.append(row)
    return out


def directed(u, axis_is):
    inv = 1.0 / u[0]
    p = 0.4 * (u[4] - 0.5 * ((u[1] * u[1] + u[2] * u[2] + u[3] * u[3]) * inv))
    mom = jnp.where(axis_is[0], u[1], jnp.where(axis_is[1], u[2], u[3]))
    s = mom * inv
    flux = [u[0] * s] + [u[i] * s for i in range(1, 4)] + [(u[4] + p) * s]
    zero = jnp.zeros_like(p)
    flux[1] = flux[1] + jnp.where(axis_is[0], p, zero)
    flux[2] = flux[2] + jnp.where(axis_is[1], p, zero)
    flux[3] = flux[3] + jnp.where(axis_is[0] | axis_is[1], zero, p)
    return flux, jnp.abs(s) + jnp.sqrt(1.4 * p * inv)


def correction(inner, outer, axis_is, half_sign):
    fi, si = directed(inner, axis_is)
    fo, so = directed(outer, axis_is)
    lam = 0.5 * jnp.maximum(si, so)
    return [half_sign * (fo[v] - fi[v]) - lam * (outer[v] - inner[v]) for v in range(VARS)]


def turned(x, b0, b1, b2):
    x = [jnp.where(b1, x[4 * (3 - p) + q], x[4 * p + q]) for p in range(4) for q in range(4)]
    x = [jnp.where(b2, x[4 * p + 3 - q], x[4 * p + q]) for p in range(4) for q in range(4)]
    return [jnp.where(b0, x[4 * t + s], x[4 * s + t]) for s in range(4) for t in range(4)]


def local_kernel(sizes, last, fld, nb_ref, ori_ref, coef_ref, dd_ref, *rest):
    if last:
        old_fld, part, acc, xs, xg, xq, xo, xc, it = rest
    else:
        part, acc, xs, xg, xq, xo, xc, it = rest
    d = rank_of(sizes)
    dd = dd_ref[...]
    dh = dd[0:NODES, :]
    pieces = [[[], []] for _ in range(VARS)]
    for h in range(2):
        u = [fld[h, v * NODES : v * NODES + NODES, :] for v in range(VARS)]
        inv = 1.0 / u[0]
        speeds = [u[i] * inv for i in range(1, 4)]
        p = 0.4 * (u[4] - 0.5 * (u[1] * speeds[0] + u[2] * speeds[1] + u[3] * speeds[2]))
        fl = fluxes(u, speeds, p)
        for v in range(VARS):
            hl = [split(fl[a][v]) for a in range(3)]
            pieces[v][0].append(jnp.concatenate([x[0] for x in hl], 0))
            pieces[v][1].append(jnp.concatenate([x[1] for x in hl], 0))
    for v in range(VARS):
        hi = mm(dd, jnp.concatenate(pieces[v][0], 1))
        lo = mm(dh, jnp.concatenate(pieces[v][1], 1))
        vol = hi[0:NODES, :] + hi[NODES : 2 * NODES, :] + lo
        for h in range(2):
            acc[h, v * NODES : v * NODES + NODES, :] = vol[:, h * LANES : h * LANES + LANES]
    for v in range(VARS):
        for f in range(FACES):
            for h in range(2):
                t = face_rows(fld, h, v, f)
                b = v * 256
                xs[pl.ds(b + 2 * f + h, 16, stride=16), :] = t
                xg[pl.ds(b + 2 * (f ^ 1) + h, 16, stride=16), :] = t
                xq[pl.ds(b + 2 * (f ^ 1) + 1 - h, 16, stride=16), :] = t
    it[...] = jnp.zeros((32, LANES), I32)
    for h in range(2):
        it[pl.ds(h, FACES, stride=2), :] = nb_ref[:, h * LANES : h * LANES + LANES]
        it[pl.ds(16 + h, FACES, stride=2), :] = ori_ref[:, h * LANES : h * LANES + LANES]
    t = it[0:16, :] - d * EL
    turn = it[16:32, :]
    row = iota((16, LANES), 0)
    local = (t >= 0) & (t < EL) & (row < 12)
    same = ((t >> 7) & 1) == (row & 1)
    idx = t & 127
    b0, b1, b2 = (turn & 1) != 0, (turn & 2) != 0, (turn & 4) != 0
    for v in range(VARS):
        got = []
        for m in range(16):
            rows = slice(v * 256 + m * 16, v * 256 + m * 16 + 16)
            ga = jnp.take_along_axis(xg[rows, :], idx, axis=1)
            gb = jnp.take_along_axis(xq[rows, :], idx, axis=1)
            got.append(jnp.where(same, ga, gb))
        for m, x in enumerate(turned(got, b0, b1, b2)):
            xo[v * 256 + m * 16 : v * 256 + m * 16 + 16, :] = x
    axis_is = (row < 4, (row >= 4) & (row < 8))
    half_sign = jnp.where((row & 2) != 0, 0.5, -0.5)
    for m in range(16):
        rows = [slice(v * 256 + m * 16, v * 256 + m * 16 + 16) for v in range(VARS)]
        cor = correction([xs[r, :] for r in rows], [xo[r, :] for r in rows], axis_is, half_sign)
        for v in range(VARS):
            xc[rows[v], :] = jnp.where(local, LIFT * cor[v], 0.0)
    for v in range(VARS):
        for f in range(FACES):
            for h in range(2):
                add_face_rows(
                    acc, h, v, f, xc[pl.ds(v * 256 + 2 * f + h, 16, stride=16), :]
                )
    for h in range(2):
        coef = coef_ref[0:1, h * LANES : h * LANES + LANES]
        for v in range(VARS):
            rows = slice(v * NODES, v * NODES + NODES)
            new = fld[h, rows, :] - coef * acc[h, rows, :]
            if last:
                new = 0.5 * old_fld[h, rows, :] + 0.5 * new
            part[h, rows, :] = new


def face_terms(inner, outer, info, live, ro, y, e):
    ro[0:80, :] = outer
    ro[80:128, :] = jnp.zeros((48, LANES), F32)
    turn = info[8:16, :]
    x = [ro[pl.ds(m, 8, stride=16), :] for m in range(16)]
    for m, val in enumerate(turned(x, (turn & 1) != 0, (turn & 2) != 0, (turn & 4) != 0)):
        y[8 * m : 8 * m + 8, :] = val
    face = jnp.where(live, jnp.broadcast_to(info[0:1, :], (16, LANES)) >> 8, -1)
    axis_is = (face < 2, (face >= 2) & (face < 4))
    half_sign = jnp.where((face & 1) != 0, 0.5, -0.5)
    behind = [y[pl.ds(v, 16, stride=8), :] for v in range(VARS)]
    here = [inner[16 * v : 16 * v + 16, :] for v in range(VARS)]
    cor = correction(here, behind, axis_is, half_sign)
    e[...] = jnp.zeros((ROWS, LANES), F32)
    for v in range(VARS):
        for f in range(FACES):
            add_face_rows(e, None, v, f, jnp.where(face == f, cor[v], 0.0))


def added(part, spread, coef_ref, scale, put):
    for h in range(2):
        lanes = slice(h * LANES, h * LANES + LANES)
        coef = scale * coef_ref[0:1, lanes]
        for v in range(VARS):
            rows = slice(v * NODES, v * NODES + NODES)
            low = slice(ROWS + v * NODES, ROWS + v * NODES + NODES)
            put(h, v, part[h, rows, :] - coef * (spread[rows, lanes] + spread[low, lanes]))


def near_kernel(part, g, r_a, info, ohs, coef_ref, hot_ref, code_ref, fp, pb, ro, y, e, g1):
    lane = iota((16, LANES), 1)
    face_terms(pltpu.roll(g[...], 64, 1), r_a[...], info, lane < 32, ro, y, e)
    spread = mm(jnp.concatenate(split(e[...]), 0), ohs[...])

    def put(h, v, new):
        fp[h, v * NODES : v * NODES + NODES, :] = new

    added(part, spread, coef_ref, LIFT, put)
    hot = hot_ref[...]
    asked = jnp.broadcast_to(code_ref[0:1, :] >> 8, (16, LANES))
    requested(fp, hot, asked, e, g1)
    lane = iota((80, LANES), 1)
    pb[0:80, :] = jnp.where(lane < 32, pltpu.roll(g1[...], 96, 1), g[...])
    ch, cl = split(jnp.broadcast_to(LIFT * coef_ref[0:1, :], (16, EL)))
    pb[80:96, :] = mm(ch, hot) + mm(cl, hot)


def pair_kernel(info, rows_ref, after, pairs):
    theirs = jnp.transpose(jnp.broadcast_to(info[0:1, :].astype(F32), (LANES, LANES))).astype(I32)
    mine = jnp.broadcast_to(rows_ref[0:1, :].astype(I32), (LANES, LANES))
    row, lane = iota((LANES, LANES), 0), iota((LANES, LANES), 1)
    on = ((theirs & 255) == (mine & 255)) & (row >= 96) & (lane >= 32) & (lane < 64)
    pairs[...] = jnp.where(on, 1.0, 0.0).astype(BF)


def far_kernel(
    fp, g, r_b, info, rows_ref, ohs, pairs, coef_ref, hot_ref, code_ref, first, g1, o1, ro, y, e
):
    lane = iota((80, LANES), 1)
    mine = pltpu.roll(g[...], 64, 1)
    got = r_b[0:80, :]
    lane16 = iota((16, LANES), 1)
    live = ((lane16 >= 32) & (lane16 < 64)) | (lane16 >= 96)
    face_terms(
        jnp.where(lane < 64, mine, got), jnp.where(lane < 64, got, mine), info, live, ro, y, e
    )
    parts = jnp.concatenate(split(e[...]), 0)
    spread = mm(parts, ohs[...])

    def put(h, v, new):
        first[h, v * NODES : v * NODES + NODES, :] = new

    added(fp, spread, coef_ref, LIFT, put)
    theirs = mm(parts, pairs[...])
    e[...] = theirs[0:ROWS, :] + theirs[ROWS : 2 * ROWS, :]
    face = jnp.broadcast_to(rows_ref[0:1, :].astype(I32) >> 8, (16, LANES))
    coef = r_b[80:81, :]
    for v in range(VARS):
        rows = slice(16 * v, 16 * v + 16)
        o1[rows, :] = pltpu.roll(r_b[rows, :], 32, 1) - coef * chosen(e, face, v)
    asked = jnp.broadcast_to(code_ref[0:1, :] >> 8, (16, LANES))
    requested(first, hot_ref[...], asked, e, g1)


def last_kernel(part, g1, r_a, o1, info, ohs, coef_ref, out, ro, y, e):
    lane = iota((80, LANES), 1)
    outer = jnp.where(lane < 32, r_a[...], o1[...])
    face_terms(pltpu.roll(g1[...], 64, 1), outer, info, iota((16, LANES), 1) < 64, ro, y, e)
    spread = mm(jnp.concatenate(split(e[...]), 0), ohs[...])

    def put(h, v, new):
        out[v, :, h * LANES : h * LANES + LANES] = new

    added(part, spread, coef_ref, 0.5 * LIFT, put)


def call(body, out_shape, scratch, cost, args, hbm=(), spare=None):
    spec = pl.BlockSpec(memory_space=pltpu.VMEM)
    specs = []
    for i, a in enumerate(args):
        if i in hbm:
            specs.append(pl.BlockSpec(memory_space=pltpu.HBM))
        elif a.dtype == I32 and a.ndim == 1:
            specs.append(pl.BlockSpec(memory_space=pltpu.SMEM))
        else:
            specs.append(spec)
    return pl.pallas_call(
        body,
        out_shape=out_shape,
        in_specs=specs,
        out_specs=jax.tree.map(lambda _: spec, out_shape),
        scratch_shapes=scratch,
        cost_estimate=pl.CostEstimate(flops=cost, bytes_accessed=cost, transcendentals=0),
        compiler_params=pltpu.CompilerParams(vmem_limit_bytes=32 * 1024 * 1024),
    )(*[pltpu.with_memory_space_constraint(a, pltpu.HBM) if i in hbm else a for i, a in enumerate(args)])


def shape(*dims, dtype=F32):
    return jax.ShapeDtypeStruct(dims, dtype)


def per_device(sizes, old_state, element_size, old_start, neighbour, orientation):
    n = sizes[0] * sizes[1] * sizes[2]
    pairs_a = [(i, i ^ 1) for i in range(n)]
    pairs_b = [(i, (i + 1) % n if i % 2 else (i - 1) % n) for i in range(n)]

    size = element_size.reshape(1, EL)
    deriv = jnp.asarray(node_derivatives())
    s_a, s_b, rows, col, old_v, nb_v, ori_v, edge = call(
        functools.partial(send_kernel, sizes),
        (
            shape(ROWS + 16, LANES),
            shape(ROWS, LANES),
            shape(16, LANES),
            shape(64, LANES),
            shape(*old_state.shape),
            shape(FACES, EL, dtype=I32),
            shape(FACES, EL, dtype=I32),
            shape(8, LANES, dtype=I32),
        ),
        [
            pltpu.VMEM((16, EL), F32),
            pltpu.SMEM(old_start.shape, I32),
            pltpu.SemaphoreType.DMA((3 + VARS,)),
        ],
        10000,
        (old_start, old_state, neighbour, orientation),
        hbm=(0, 1, 2, 3),
    )
    r_a = lax.ppermute(s_a, AXES, pairs_a)
    c_b = lax.ppermute(rows, AXES, pairs_b)
    r_b = lax.ppermute(s_b, AXES, pairs_b[1:-1])
    own, ohs, dd, coef = call(
        functools.partial(own_kernel, sizes),
        (
            shape(2, ROWS, LANES),
            shape(LANES, EL, dtype=BF),
            shape(2 * NODES, 3 * NODES, dtype=BF),
            shape(1, EL),
        ),
        [
            pltpu.VMEM((NODES, 3 * NODES), F32),
            pltpu.VMEM((1, EL), F32),
            pltpu.SMEM(old_start.shape, I32),
            pltpu.SemaphoreType.DMA((3,)),
        ],
        10000,
        (old_start, old_v, col, deriv, size),
        hbm=(0, 3, 4),
    )
    table = pltpu.VMEM((ROWS, LANES), F32)
    square = pltpu.VMEM((LANES, LANES), F32)
    traces = shape(80, LANES)
    state = shape(2, ROWS, LANES)
    fld, hot, code, info, g = call(
        functools.partial(join_kernel, sizes),
        (
            state,
            shape(EL, LANES, dtype=BF),
            shape(8, LANES, dtype=I32),
            shape(16, LANES, dtype=I32),
            traces,
        ),
        [table],
        10000,
        (own, r_a, r_b, c_b, rows, edge),
    )

    def local(last, *args):
        faces = pltpu.VMEM((VARS * 256, LANES), F32)
        return call(
            functools.partial(local_kernel, sizes, last),
            state,
            [pltpu.VMEM((2, ROWS, LANES), F32)] + [faces] * 5 + [pltpu.VMEM((32, LANES), I32)],
            20000,
            args,
        )

    r_a = lax.ppermute(g, AXES, pairs_a)
    part = local(False, fld, nb_v, ori_v, coef, dd)
    fp, pb = call(
        near_kernel,
        (state, shape(96, LANES)),
        [square, square, table, pltpu.VMEM((80, LANES), F32)],
        10000,
        (part, g, r_a, info, ohs, coef, hot, code),
    )
    r_b = lax.ppermute(pb, AXES, pairs_b)
    pairs = call(pair_kernel, shape(LANES, LANES, dtype=BF), [], 10000, (info, rows, fp))
    first, g1, o1 = call(
        far_kernel,
        (state, traces, traces),
        [square, square, table],
        10000,
        (fp, g, r_b, info, rows, ohs, pairs, coef, hot, code),
    )
    r_a = lax.ppermute(g1, AXES, pairs_a)
    part = local(True, first, nb_v, ori_v, coef, dd, fld)
    return call(
        last_kernel,
        shape(VARS, NODES, EL),
        [square, square, table],
        10000,
        (part, g1, r_a, o1, info, ohs, coef),
    )


def solution(mesh):
    sizes = tuple(mesh.shape[a] for a in AXES)
    in_specs = (P(None, None, AXES), P(AXES), P(), P(None, AXES), P(None, AXES))
    return jax.shard_map(
        functools.partial(per_device, sizes),
        mesh=mesh,
        in_specs=in_specs,
        out_specs=P(None, None, AXES),
        check_vma=False,
    )
```

```python
import functools

import jax
import jax.numpy as jnp
import numpy as np
from jax import lax
from jax.experimental import pallas as pl
from jax.experimental.pallas import tpu as pltpu
from jax.sharding import PartitionSpec as P

AXES = ("gx", "gy", "gz")
TIME_STEP = 0.03
LIFT = 6.0
VARS = 5
NODES = 64
EL = 256
LANES = 128
PITCH = 12
TABLE = 16 * PITCH
REMOTE = 32
FACES = 6
ROWS = VARS * NODES
BF = jnp.bfloat16
F32 = jnp.float32
I32 = jnp.int32


def gll_derivative():
    points = np.array([-1.0, -1.0 / np.sqrt(5.0), 1.0 / np.sqrt(5.0), 1.0])
    weights = np.array(
        [1.0 / np.prod([points[c] - points[p] for p in range(4) if p != c]) for c in range(4)]
    )
    matrix = np.zeros((4, 4))
    for row in range(4):
        for col in range(4):
            if row != col:
                matrix[row, col] = weights[col] / weights[row] / (points[row] - points[col])
        matrix[row, row] = -np.sum(matrix[row])
    return matrix


def node_derivatives():
    d, one = gll_derivative(), np.eye(4)
    parts = [
        np.kron(np.kron(d, one), one),
        np.kron(np.kron(one, d), one),
        np.kron(np.kron(one, one), d),
    ]
    return np.concatenate(parts, axis=1).astype(np.float32)


def iota(shape, dim):
    return lax.broadcasted_iota(I32, shape, dim)


def split(x):
    hi = x.astype(BF)
    return hi, (x - hi.astype(F32)).astype(BF)


def mm(a, b):
    return jnp.dot(a, b, preferred_element_type=F32)


def rows_at(lead, base, f, i=None):
    if f < 2:
        rows = pl.ds(base + 48 * f, 16)
    elif f < 4:
        rows = pl.ds(base + 12 * (f - 2) + 16 * i, 4)
    else:
        rows = pl.ds(base + 3 * (f - 4), 16, stride=4)
    return (rows, slice(None)) if lead is None else (lead, rows, slice(None))


def face_rows(ref, lead, v, f):
    if f in (2, 3):
        return jnp.concatenate([ref[rows_at(lead, v * NODES, f, i)] for i in range(4)], 0)
    return ref[rows_at(lead, v * NODES, f)]


def put_face_rows(across, lead, v, f, val):
    ref = across[f // 2]
    if f in (2, 3):
        for i in range(4):
            ref[rows_at(lead, v * NODES, f, i)] = val[4 * i : 4 * i + 4, :]
    else:
        ref[rows_at(lead, v * NODES, f)] = val


def rank_of(sizes):
    return (lax.axis_index("gx") * sizes[1] + lax.axis_index("gy")) * sizes[2] + lax.axis_index("gz")


def places(mask):
    count = mask.shape[0]
    upper = jnp.where(iota((EL, EL), 0) <= iota((EL, EL), 1), 1.0, 0.0).astype(BF)
    inclusive = mm(mask.astype(BF), upper)
    total = jnp.broadcast_to(inclusive[:, EL - 1 : EL], (count, LANES)).astype(BF)
    r, c = iota((count, count), 0), iota((count, count), 1)
    lower = jnp.where((c < r) & ((c >> 3) == (r >> 3)), 1.0, 0.0).astype(BF)
    offset = mm(lower, total)[:, 0:1]
    return jnp.where(mask > 0.5, inclusive + offset - 1.0, -1.0)


def listed(place, values):
    slot = iota((REMOTE, EL), 0).astype(F32)
    accs = [jnp.zeros((REMOTE, EL), F32) for _ in values]
    for f in range(FACES):
        hit = place[f : f + 1, :] == slot
        accs = [jnp.where(hit, x[f : f + 1, :], acc) for x, acc in zip(values, accs)]
    return [jnp.sum(acc, 1, keepdims=True) for acc in accs]


def send_kernel(sizes, start_hbm, old, nb, ori, s_a, s_b, rows_ref, col_ref, old_v, nb_v, ori_v, edge, mk, start, sem):
    n = sizes[0] * sizes[1] * sizes[2]
    copies = [
        pltpu.make_async_copy(nb, nb_v, sem.at[0]),
        pltpu.make_async_copy(ori, ori_v, sem.at[1]),
        pltpu.make_async_copy(start_hbm, start, sem.at[2]),
    ] + [pltpu.make_async_copy(old.at[v], old_v.at[v], sem.at[3 + v]) for v in range(VARS)]
    for copy in copies:
        copy.start()
    d = rank_of(sizes)
    even = (d & 1) == 0
    up = jnp.where(d + 1 == n, 0, d + 1) * EL
    down = jnp.where(d == 0, n - 1, d - 1) * EL
    mk[...] = jnp.zeros((16, EL), F32)
    copies[0].wait()
    nb = nb_v[...]
    rel = [nb - jnp.where(even, up, down), nb - jnp.where(even, down, up)]
    for k in range(2):
        mk[8 * k : 8 * k + FACES, :] = jnp.where((rel[k] >= 0) & (rel[k] < EL), 1.0, 0.0)
    place = places(mk[...])
    copies[1].wait()
    face = iota((FACES, EL), 0)
    own = (face * EL + iota((FACES, EL), 1) + 2048 * ori_v[...]).astype(F32)
    lists = []
    for k in range(2):
        lists.append(listed(place[8 * k : 8 * k + 8, :], [((face ^ 1) * EL + rel[k]).astype(F32), own]))
    col = jnp.concatenate([lists[0][0], lists[1][0], lists[0][1], lists[1][1]], 0)
    wide = jnp.broadcast_to(col, (LANES, LANES))
    row = jnp.transpose(wide)[0:8, :]
    turn = jnp.floor(row * (1.0 / 2048.0))
    code = row - 2048.0 * turn
    rows_ref[0:8, :] = code
    rows_ref[8:16, :] = turn
    col_ref[...] = wide[64:128, :]
    s_a[ROWS : ROWS + 8, :] = code
    s_a[ROWS + 8 : ROWS + 16, :] = turn

    copies[2].wait()
    o = start[d] - d * EL
    edge[0:4, :] = jnp.broadcast_to(o, (4, LANES))
    edge[4:8, :] = jnp.broadcast_to(start[d + 1] - d * EL, (4, LANES))
    first = EL - o
    q, rot = first >> 7, first & 127
    keep = iota((NODES, LANES), 1) < LANES - rot
    back = (LANES - rot) & 127
    t0 = pl.ds(pl.multiple_of(q * LANES, LANES), LANES)
    t1 = pl.ds(pl.multiple_of(jnp.minimum(q + 1, 3) * LANES, LANES), LANES)
    for copy in copies[3:]:
        copy.wait()

    def put(to_up, to_down):
        for v in range(VARS):
            rows = slice(v * NODES, v * NODES + NODES)
            to_up[rows, :] = jnp.where(
                keep, pltpu.roll(old_v[v, :, t0], back, 1), pltpu.roll(old_v[v, :, t1], back, 1)
            )
            to_down[rows, :] = pltpu.roll(old_v[v, :, 0:LANES], o & 127, 1)

    @pl.when(even)
    def _():
        put(s_a, s_b)

    @pl.when(jnp.logical_not(even))
    def _():
        put(s_b, s_a)


def own_kernel(
    sizes, start_hbm, old, col_ref, d_hbm, size_hbm, own, ohs, dd, coef, d_v, size_v, start, sem
):
    copies = [
        pltpu.make_async_copy(start_hbm, start, sem.at[2]),
        pltpu.make_async_copy(d_hbm, d_v, sem.at[0]),
        pltpu.make_async_copy(size_hbm, size_v, sem.at[1]),
    ]
    for copy in copies:
        copy.start()
    d = rank_of(sizes)
    copies[0].wait()
    s = d * EL - start[d]
    q, rot = s >> 7, s & 127
    keep = iota((NODES, LANES), 1) < LANES - rot
    back = (LANES - rot) & 127
    for v in range(VARS):
        rows = slice(v * NODES, v * NODES + NODES)
        t = [
            pltpu.roll(
                old[v, :, pl.ds(pl.multiple_of(jnp.maximum(q + i, 0) * LANES, LANES), LANES)], back, 1
            )
            for i in range(3)
        ]
        own[0, rows, :] = jnp.where(keep, t[0], t[1])
        own[1, rows, :] = jnp.where(keep, t[1], t[2])
    code = col_ref[...].astype(I32)
    lane = iota((64, LANES), 1)
    for h in range(2):
        hit = jnp.where((code & 255) == lane + h * LANES, 1.0, 0.0).astype(BF)
        ohs[0:64, h * LANES : h * LANES + LANES] = hit
        ohs[64:128, h * LANES : h * LANES + LANES] = jnp.zeros((64, LANES), BF)
    for copy in copies[1:]:
        copy.wait()
    dd[...] = jnp.concatenate(split(d_v[...]), 0)
    coef[...] = (TIME_STEP * 2.0) / size_v[...]


def chosen(gs, face, v):
    acc = face_rows(gs, None, v, 0)
    for f in range(1, FACES):
        acc = jnp.where(face == f, face_rows(gs, None, v, f), acc)
    return acc


def requested(fld, hot, face, gs, g):
    both = jnp.concatenate([fld[0], fld[1]], 1)
    out = mm(jnp.concatenate(split(both), 0), hot)
    gs[...] = out[0:ROWS, :] + out[ROWS : 2 * ROWS, :]
    for v in range(VARS):
        g[16 * v : 16 * v + 16, :] = chosen(gs, face, v)


def join_kernel(sizes, own, r_a, r_b, c_b, rows_ref, edge, fld, hot_ref, code_ref, info, g, gs):
    even = (rank_of(sizes) & 1) == 0
    lane = iota((NODES, LANES), 1)
    below = lane < edge[0:1, :]
    above = lane + LANES >= edge[4:5, :]
    for v in range(VARS):
        rows = slice(v * NODES, v * NODES + NODES)
        a, b = r_a[rows, :], r_b[rows, :]
        fld[0, rows, :] = jnp.where(below, jnp.where(even, b, a), own[0, rows, :])
        fld[1, rows, :] = jnp.where(above, jnp.where(even, a, b), own[1, rows, :])
    lane8 = iota((8, LANES), 1)
    code = jnp.where(
        lane8 < 32,
        r_a[ROWS : ROWS + 8, :],
        jnp.where(lane8 < 64, c_b[0:8, :], rows_ref[0:8, :]),
    ).astype(I32)
    code_ref[...] = code
    lane16 = iota((16, LANES), 1)
    info[...] = jnp.where(
        lane16 < 96, pltpu.roll(rows_ref[...], 64, 1), c_b[...]
    ).astype(I32)
    spot = jnp.broadcast_to(code[0:1, :] & 255, (EL, LANES))
    hot = jnp.where(spot == iota((EL, LANES), 0), 1.0, 0.0).astype(BF)
    hot_ref[...] = hot
    face = jnp.broadcast_to(code[0:1, :] >> 8, (16, LANES))
    requested(fld, hot, face, gs, g)


def fluxes(u, speeds, p):
    out = []
    for a in range(3):
        s = speeds[a]
        row = [u[0] * s, u[1] * s, u[2] * s, u[3] * s, (u[4] + p) * s]
        row[1 + a] = row[1 + a] + p
        out.append(row)
    return out


def directed(u, axis_is):
    inv = 1.0 / u[0]
    p = 0.4 * (u[4] - 0.5 * ((u[1] * u[1] + u[2] * u[2] + u[3] * u[3]) * inv))
    mom = jnp.where(axis_is[0], u[1], jnp.where(axis_is[1], u[2], u[3]))
    s = mom * inv
    flux = [u[0] * s] + [u[i] * s for i in range(1, 4)] + [(u[4] + p) * s]
    zero = jnp.zeros_like(p)
    flux[1] = flux[1] + jnp.where(axis_is[0], p, zero)
    flux[2] = flux[2] + jnp.where(axis_is[1], p, zero)
    flux[3] = flux[3] + jnp.where(axis_is[0] | axis_is[1], zero, p)
    return flux, jnp.abs(s) + jnp.sqrt(1.4 * p * inv)


def correction(inner, outer, axis_is, half_sign):
    fi, si = directed(inner, axis_is)
    fo, so = directed(outer, axis_is)
    lam = 0.5 * jnp.maximum(si, so)
    return [half_sign * (fo[v] - fi[v]) - lam * (outer[v] - inner[v]) for v in range(VARS)]


def turned(x, b0, b1, b2):
    x = [jnp.where(b1, x[4 * (3 - p) + q], x[4 * p + q]) for p in range(4) for q in range(4)]
    x = [jnp.where(b2, x[4 * p + 3 - q], x[4 * p + q]) for p in range(4) for q in range(4)]
    return [jnp.where(b0, x[4 * t + s], x[4 * s + t]) for s in range(4) for t in range(4)]


def local_kernel(sizes, last, fld, nb_ref, ori_ref, coef_ref, dd_ref, *rest):
    if last:
        old_fld, part, acc, ax, ay, az, xs, xg, xq, xo, xc, it = rest
    else:
        part, acc, ax, ay, az, xs, xg, xq, xo, xc, it = rest
    for ref in (ax, ay, az):
        ref[...] = jnp.zeros((2, ROWS, LANES), F32)
    d = rank_of(sizes)
    dd = dd_ref[...]
    dh = dd[0:NODES, :]
    pieces = [[[], []] for _ in range(VARS)]
    for h in range(2):
        u = [fld[h, v * NODES : v * NODES + NODES, :] for v in range(VARS)]
        inv = 1.0 / u[0]
        speeds = [u[i] * inv for i in range(1, 4)]
        p = 0.4 * (u[4] - 0.5 * (u[1] * speeds[0] + u[2] * speeds[1] + u[3] * speeds[2]))
        fl = fluxes(u, speeds, p)
        for v in range(VARS):
            hl = [split(fl[a][v]) for a in range(3)]
            pieces[v][0].append(jnp.concatenate([x[0] for x in hl], 0))
            pieces[v][1].append(jnp.concatenate([x[1] for x in hl], 0))
    for v in range(VARS):
        hi = mm(dd, jnp.concatenate(pieces[v][0], 1))
        lo = mm(dh, jnp.concatenate(pieces[v][1], 1))
        vol = hi[0:NODES, :] + hi[NODES : 2 * NODES, :] + lo
        for h in range(2):
            acc[h, v * NODES : v * NODES + NODES, :] = vol[:, h * LANES : h * LANES + LANES]
    for v in range(VARS):
        for f in range(FACES):
            for h in range(2):
                t = face_rows(fld, h, v, f)
                b = v * TABLE
                xs[pl.ds(b + 2 * f + h, 16, stride=PITCH), :] = t
                xg[pl.ds(b + 2 * (f ^ 1) + h, 16, stride=PITCH), :] = t
                xq[pl.ds(b + 2 * (f ^ 1) + 1 - h, 16, stride=PITCH), :] = t
    it[...] = jnp.zeros((32, LANES), I32)
    for h in range(2):
        it[pl.ds(h, FACES, stride=2), :] = nb_ref[:, h * LANES : h * LANES + LANES]
        it[pl.ds(16 + h, FACES, stride=2), :] = ori_ref[:, h * LANES : h * LANES + LANES]
    t = it[0:16, :] - d * EL
    turn = it[16:32, :]
    row = iota((16, LANES), 0)
    local = (t >= 0) & (t < EL) & (row < 12)
    same = ((t >> 7) & 1) == (row & 1)
    idx = t & 127
    b0, b1, b2 = (turn & 1) != 0, (turn & 2) != 0, (turn & 4) != 0
    for v in range(VARS):
        got = []
        for m in range(16):
            rows = pl.ds(v * TABLE + m * PITCH, 16)
            ga = jnp.take_along_axis(xg[rows, :], idx, axis=1)
            gb = jnp.take_along_axis(xq[rows, :], idx, axis=1)
            got.append(jnp.where(same, ga, gb))
        for m, x in enumerate(turned(got, b0, b1, b2)):
            xo[pl.ds(v * TABLE + m * PITCH, 12), :] = x[0:12, :]
    axis_is = (row < 4, (row >= 4) & (row < 8))
    half_sign = jnp.where((row & 2) != 0, 0.5, -0.5)
    for m in range(16):
        rows = [pl.ds(v * TABLE + m * PITCH, 16) for v in range(VARS)]
        cor = correction([xs[r, :] for r in rows], [xo[r, :] for r in rows], axis_is, half_sign)
        for v in range(VARS):
            val = jnp.where(local, LIFT * cor[v], 0.0)
            xc[pl.ds(v * TABLE + m * PITCH, 12), :] = val[0:12, :]
    for v in range(VARS):
        for f in range(FACES):
            for h in range(2):
                put_face_rows(
                    (ax, ay, az), h, v, f, xc[pl.ds(v * TABLE + 2 * f + h, 16, stride=PITCH), :]
                )
    for h in range(2):
        coef = coef_ref[0:1, h * LANES : h * LANES + LANES]
        for v in range(VARS):
            rows = slice(v * NODES, v * NODES + NODES)
            rate = acc[h, rows, :] + ax[h, rows, :] + ay[h, rows, :] + az[h, rows, :]
            new = fld[h, rows, :] - coef * rate
            if last:
                new = 0.5 * old_fld[h, rows, :] + 0.5 * new
            part[h, rows, :] = new


def face_terms(inner, outer, info, live, ro, y, ex, ey, ez):
    for v in range(VARS):
        ro[17 * v : 17 * v + 16, :] = outer[16 * v : 16 * v + 16, :]
    turn = info[8:16, :]
    x = [ro[pl.ds(m, 8, stride=17), :] for m in range(16)]
    for m, val in enumerate(turned(x, (turn & 1) != 0, (turn & 2) != 0, (turn & 4) != 0)):
        y[9 * m : 9 * m + 8, :] = val
    face = jnp.where(live, jnp.broadcast_to(info[0:1, :], (16, LANES)) >> 8, -1)
    axis_is = (face < 2, (face >= 2) & (face < 4))
    half_sign = jnp.where((face & 1) != 0, 0.5, -0.5)
    behind = [y[pl.ds(v, 16, stride=9), :] for v in range(VARS)]
    here = [inner[16 * v : 16 * v + 16, :] for v in range(VARS)]
    cor = correction(here, behind, axis_is, half_sign)
    for ref in (ex, ey, ez):
        ref[...] = jnp.zeros((ROWS, LANES), F32)
    for v in range(VARS):
        for f in range(FACES):
            put_face_rows((ex, ey, ez), None, v, f, jnp.where(face == f, cor[v], 0.0))
    return jnp.concatenate(split(ex[...] + ey[...] + ez[...]), 0)


def added(part, spread, coef_ref, scale, put):
    for h in range(2):
        lanes = slice(h * LANES, h * LANES + LANES)
        coef = scale * coef_ref[0:1, lanes]
        for v in range(VARS):
            rows = slice(v * NODES, v * NODES + NODES)
            low = slice(ROWS + v * NODES, ROWS + v * NODES + NODES)
            put(h, v, part[h, rows, :] - coef * (spread[rows, lanes] + spread[low, lanes]))


def near_kernel(part, g, r_a, info, ohs, coef_ref, hot_ref, code_ref, fp, pb, ro, y, ex, ey, ez, g1):
    lane = iota((16, LANES), 1)
    parts = face_terms(pltpu.roll(g[...], 64, 1), r_a[...], info, lane < 32, ro, y, ex, ey, ez)
    spread = mm(parts, ohs[...])

    def put(h, v, new):
        fp[h, v * NODES : v * NODES + NODES, :] = new

    added(part, spread, coef_ref, LIFT, put)
    hot = hot_ref[...]
    asked = jnp.broadcast_to(code_ref[0:1, :] >> 8, (16, LANES))
    requested(fp, hot, asked, ex, g1)
    lane = iota((80, LANES), 1)
    pb[0:80, :] = jnp.where(lane < 32, pltpu.roll(g1[...], 96, 1), g[...])
    ch, cl = split(jnp.broadcast_to(LIFT * coef_ref[0:1, :], (16, EL)))
    pb[80:96, :] = mm(ch, hot) + mm(cl, hot)


def pair_kernel(info, rows_ref, after, pairs):
    theirs = jnp.transpose(jnp.broadcast_to(info[0:1, :].astype(F32), (LANES, LANES))).astype(I32)
    mine = jnp.broadcast_to(rows_ref[0:1, :].astype(I32), (LANES, LANES))
    row, lane = iota((LANES, LANES), 0), iota((LANES, LANES), 1)
    on = ((theirs & 255) == (mine & 255)) & (row >= 96) & (lane >= 32) & (lane < 64)
    pairs[...] = jnp.where(on, 1.0, 0.0).astype(BF)


def far_kernel(
    fp, g, r_b, info, rows_ref, ohs, pairs, coef_ref, hot_ref, code_ref, first, g1, o1, ro, y, ex, ey, ez
):
    lane = iota((80, LANES), 1)
    mine = pltpu.roll(g[...], 64, 1)
    got = r_b[0:80, :]
    lane16 = iota((16, LANES), 1)
    live = ((lane16 >= 32) & (lane16 < 64)) | (lane16 >= 96)
    inner, outer = jnp.where(lane < 64, mine, got), jnp.where(lane < 64, got, mine)
    parts = face_terms(inner, outer, info, live, ro, y, ex, ey, ez)
    spread = mm(parts, ohs[...])

    def put(h, v, new):
        first[h, v * NODES : v * NODES + NODES, :] = new

    added(fp, spread, coef_ref, LIFT, put)
    theirs = mm(parts, pairs[...])
    ey[...] = theirs[0:ROWS, :] + theirs[ROWS : 2 * ROWS, :]
    face = jnp.broadcast_to(rows_ref[0:1, :].astype(I32) >> 8, (16, LANES))
    coef = r_b[80:81, :]
    for v in range(VARS):
        rows = slice(16 * v, 16 * v + 16)
        o1[rows, :] = pltpu.roll(r_b[rows, :], 32, 1) - coef * chosen(ey, face, v)
    asked = jnp.broadcast_to(code_ref[0:1, :] >> 8, (16, LANES))
    requested(first, hot_ref[...], asked, ex, g1)


def last_kernel(part, g1, r_a, o1, info, ohs, coef_ref, out, ro, y, ex, ey, ez):
    lane = iota((80, LANES), 1)
    outer = jnp.where(lane < 32, r_a[...], o1[...])
    live = iota((16, LANES), 1) < 64
    parts = face_terms(pltpu.roll(g1[...], 64, 1), outer, info, live, ro, y, ex, ey, ez)
    spread = mm(parts, ohs[...])

    def put(h, v, new):
        out[v, :, h * LANES : h * LANES + LANES] = new

    added(part, spread, coef_ref, 0.5 * LIFT, put)


def call(body, out_shape, scratch, cost, args, hbm=(), spare=None):
    spec = pl.BlockSpec(memory_space=pltpu.VMEM)
    specs = []
    for i, a in enumerate(args):
        if i in hbm:
            specs.append(pl.BlockSpec(memory_space=pltpu.HBM))
        elif a.dtype == I32 and a.ndim == 1:
            specs.append(pl.BlockSpec(memory_space=pltpu.SMEM))
        else:
            specs.append(spec)
    return pl.pallas_call(
        body,
        out_shape=out_shape,
        in_specs=specs,
        out_specs=jax.tree.map(lambda _: spec, out_shape),
        scratch_shapes=scratch,
        cost_estimate=pl.CostEstimate(flops=cost, bytes_accessed=cost, transcendentals=0),
        compiler_params=pltpu.CompilerParams(vmem_limit_bytes=32 * 1024 * 1024),
    )(*[pltpu.with_memory_space_constraint(a, pltpu.HBM) if i in hbm else a for i, a in enumerate(args)])


def shape(*dims, dtype=F32):
    return jax.ShapeDtypeStruct(dims, dtype)


def per_device(sizes, old_state, element_size, old_start, neighbour, orientation):
    n = sizes[0] * sizes[1] * sizes[2]
    pairs_a = [(i, i ^ 1) for i in range(n)]
    pairs_b = [(i, (i + 1) % n if i % 2 else (i - 1) % n) for i in range(n)]

    size = element_size.reshape(1, EL)
    deriv = jnp.asarray(node_derivatives())
    s_a, s_b, rows, col, old_v, nb_v, ori_v, edge = call(
        functools.partial(send_kernel, sizes),
        (
            shape(ROWS + 16, LANES),
            shape(ROWS, LANES),
            shape(16, LANES),
            shape(64, LANES),
            shape(*old_state.shape),
            shape(FACES, EL, dtype=I32),
            shape(FACES, EL, dtype=I32),
            shape(8, LANES, dtype=I32),
        ),
        [
            pltpu.VMEM((16, EL), F32),
            pltpu.SMEM(old_start.shape, I32),
            pltpu.SemaphoreType.DMA((3 + VARS,)),
        ],
        10000,
        (old_start, old_state, neighbour, orientation),
        hbm=(0, 1, 2, 3),
    )
    r_a = lax.ppermute(s_a, AXES, pairs_a)
    c_b = lax.ppermute(rows, AXES, pairs_b)
    r_b = lax.ppermute(s_b, AXES, pairs_b[1:-1])
    own, ohs, dd, coef = call(
        functools.partial(own_kernel, sizes),
        (
            shape(2, ROWS, LANES),
            shape(LANES, EL, dtype=BF),
            shape(2 * NODES, 3 * NODES, dtype=BF),
            shape(1, EL),
        ),
        [
            pltpu.VMEM((NODES, 3 * NODES), F32),
            pltpu.VMEM((1, EL), F32),
            pltpu.SMEM(old_start.shape, I32),
            pltpu.SemaphoreType.DMA((3,)),
        ],
        10000,
        (old_start, old_v, col, deriv, size),
        hbm=(0, 3, 4),
    )
    table = pltpu.VMEM((ROWS, LANES), F32)
    square = pltpu.VMEM((LANES + 24, LANES), F32)
    traces = shape(80, LANES)
    state = shape(2, ROWS, LANES)
    fld, hot, code, info, g = call(
        functools.partial(join_kernel, sizes),
        (
            state,
            shape(EL, LANES, dtype=BF),
            shape(8, LANES, dtype=I32),
            shape(16, LANES, dtype=I32),
            traces,
        ),
        [table],
        10000,
        (own, r_a, r_b, c_b, rows, edge),
    )

    def local(last, *args):
        faces = pltpu.VMEM((VARS * TABLE + 8, LANES), F32)
        return call(
            functools.partial(local_kernel, sizes, last),
            state,
            [pltpu.VMEM((2, ROWS, LANES), F32)] * 4 + [faces] * 5 + [pltpu.VMEM((32, LANES), I32)],
            20000,
            args,
        )

    r_a = lax.ppermute(g, AXES, pairs_a)
    part = local(False, fld, nb_v, ori_v, coef, dd)
    fp, pb = call(
        near_kernel,
        (state, shape(96, LANES)),
        [square, square, table, table, table, pltpu.VMEM((80, LANES), F32)],
        10000,
        (part, g, r_a, info, ohs, coef, hot, code),
    )
    r_b = lax.ppermute(pb, AXES, pairs_b)
    pairs = call(pair_kernel, shape(LANES, LANES, dtype=BF), [], 10000, (info, rows, fp))
    first, g1, o1 = call(
        far_kernel,
        (state, traces, traces),
        [square, square, table, table, table],
        10000,
        (fp, g, r_b, info, rows, ohs, pairs, coef, hot, code),
    )
    r_a = lax.ppermute(g1, AXES, pairs_a)
    part = local(True, first, nb_v, ori_v, coef, dd, fld)
    return call(
        last_kernel,
        shape(VARS, NODES, EL),
        [square, square, table, table, table],
        10000,
        (part, g1, r_a, o1, info, ohs, coef),
    )


def solution(mesh):
    sizes = tuple(mesh.shape[a] for a in AXES)
    in_specs = (P(None, None, AXES), P(AXES), P(), P(None, AXES), P(None, AXES))
    return jax.shard_map(
        functools.partial(per_device, sizes),
        mesh=mesh,
        in_specs=in_specs,
        out_specs=P(None, None, AXES),
        check_vma=False,
    )
```

```python
import functools

import jax
import jax.numpy as jnp
import numpy as np
from jax import lax
from jax.experimental import pallas as pl
from jax.experimental.pallas import tpu as pltpu
from jax.sharding import PartitionSpec as P

AXES = ("gx", "gy", "gz")
TIME_STEP = 0.03
LIFT = 6.0
VARS = 5
NODES = 64
EL = 256
LANES = 128
PITCH = 12
TABLE = 16 * PITCH
REMOTE = 32
FACES = 6
ROWS = VARS * NODES
BF = jnp.bfloat16
F32 = jnp.float32
I32 = jnp.int32


def gll_derivative():
    points = np.array([-1.0, -1.0 / np.sqrt(5.0), 1.0 / np.sqrt(5.0), 1.0])
    weights = np.array(
        [1.0 / np.prod([points[c] - points[p] for p in range(4) if p != c]) for c in range(4)]
    )
    matrix = np.zeros((4, 4))
    for row in range(4):
        for col in range(4):
            if row != col:
                matrix[row, col] = weights[col] / weights[row] / (points[row] - points[col])
        matrix[row, row] = -np.sum(matrix[row])
    return matrix


def node_derivatives():
    d, one = gll_derivative(), np.eye(4)
    parts = [
        np.kron(np.kron(d, one), one),
        np.kron(np.kron(one, d), one),
        np.kron(np.kron(one, one), d),
    ]
    return np.concatenate(parts, axis=1).astype(np.float32)


def iota(shape, dim):
    return lax.broadcasted_iota(I32, shape, dim)


def split(x):
    hi = x.astype(BF)
    return hi, (x - hi.astype(F32)).astype(BF)


def mm(a, b):
    return jnp.dot(a, b, preferred_element_type=F32)


def rows_at(lead, base, f, i=None):
    if f < 2:
        rows = pl.ds(base + 48 * f, 16)
    elif f < 4:
        rows = pl.ds(base + 12 * (f - 2) + 16 * i, 4)
    else:
        rows = pl.ds(base + 3 * (f - 4), 16, stride=4)
    return (rows, slice(None)) if lead is None else (lead, rows, slice(None))


def face_rows(ref, lead, v, f):
    if f in (2, 3):
        return jnp.concatenate([ref[rows_at(lead, v * NODES, f, i)] for i in range(4)], 0)
    return ref[rows_at(lead, v * NODES, f)]


def put_face_rows(across, lead, v, f, val):
    ref = across[f // 2]
    if f in (2, 3):
        for i in range(4):
            ref[rows_at(lead, v * NODES, f, i)] = val[4 * i : 4 * i + 4, :]
    else:
        ref[rows_at(lead, v * NODES, f)] = val


def rank_of(sizes):
    return (lax.axis_index("gx") * sizes[1] + lax.axis_index("gy")) * sizes[2] + lax.axis_index("gz")


def places(mask):
    count = mask.shape[0]
    upper = jnp.where(iota((EL, EL), 0) <= iota((EL, EL), 1), 1.0, 0.0).astype(BF)
    inclusive = mm(mask.astype(BF), upper)
    total = jnp.broadcast_to(inclusive[:, EL - 1 : EL], (count, LANES)).astype(BF)
    r, c = iota((count, count), 0), iota((count, count), 1)
    lower = jnp.where((c < r) & ((c >> 3) == (r >> 3)), 1.0, 0.0).astype(BF)
    offset = mm(lower, total)[:, 0:1]
    return jnp.where(mask > 0.5, inclusive + offset - 1.0, -1.0)


def listed(place, values):
    slot = iota((REMOTE, EL), 0).astype(F32)
    accs = [jnp.zeros((REMOTE, EL), F32) for _ in values]
    for f in range(FACES):
        hit = place[f : f + 1, :] == slot
        accs = [jnp.where(hit, x[f : f + 1, :], acc) for x, acc in zip(values, accs)]
    return [jnp.sum(acc, 1, keepdims=True) for acc in accs]


def send_kernel(sizes, start_hbm, old, nb, ori, s_a, s_b, rows_ref, col_ref, old_v, nb_v, ori_v, edge, mk, start, sem):
    n = sizes[0] * sizes[1] * sizes[2]
    copies = [
        pltpu.make_async_copy(nb, nb_v, sem.at[0]),
        pltpu.make_async_copy(ori, ori_v, sem.at[1]),
        pltpu.make_async_copy(start_hbm, start, sem.at[2]),
    ] + [pltpu.make_async_copy(old.at[v], old_v.at[v], sem.at[3 + v]) for v in range(VARS)]
    for copy in copies:
        copy.start()
    d = rank_of(sizes)
    even = (d & 1) == 0
    up = jnp.where(d + 1 == n, 0, d + 1) * EL
    down = jnp.where(d == 0, n - 1, d - 1) * EL
    mk[...] = jnp.zeros((16, EL), F32)
    copies[0].wait()
    nb = nb_v[...]
    rel = [nb - jnp.where(even, up, down), nb - jnp.where(even, down, up)]
    for k in range(2):
        mk[8 * k : 8 * k + FACES, :] = jnp.where((rel[k] >= 0) & (rel[k] < EL), 1.0, 0.0)
    place = places(mk[...])
    copies[1].wait()
    face = iota((FACES, EL), 0)
    own = (face * EL + iota((FACES, EL), 1) + 2048 * ori_v[...]).astype(F32)
    lists = []
    for k in range(2):
        lists.append(listed(place[8 * k : 8 * k + 8, :], [((face ^ 1) * EL + rel[k]).astype(F32), own]))
    col = jnp.concatenate([lists[0][0], lists[1][0], lists[0][1], lists[1][1]], 0)
    wide = jnp.broadcast_to(col, (LANES, LANES))
    row = jnp.transpose(wide)[0:8, :]
    turn = jnp.floor(row * (1.0 / 2048.0))
    code = row - 2048.0 * turn
    rows_ref[0:8, :] = code
    rows_ref[8:16, :] = turn
    col_ref[...] = wide[64:128, :]
    s_a[ROWS : ROWS + 8, :] = code
    s_a[ROWS + 8 : ROWS + 16, :] = turn

    copies[2].wait()
    o = start[d] - d * EL
    edge[0:4, :] = jnp.broadcast_to(o, (4, LANES))
    edge[4:8, :] = jnp.broadcast_to(start[d + 1] - d * EL, (4, LANES))
    first = EL - o
    q, rot = first >> 7, first & 127
    keep = iota((NODES, LANES), 1) < LANES - rot
    back = (LANES - rot) & 127
    t0 = pl.ds(pl.multiple_of(q * LANES, LANES), LANES)
    t1 = pl.ds(pl.multiple_of(jnp.minimum(q + 1, 3) * LANES, LANES), LANES)
    for copy in copies[3:]:
        copy.wait()

    def put(to_up, to_down):
        for v in range(VARS):
            rows = slice(v * NODES, v * NODES + NODES)
            to_up[rows, :] = jnp.where(
                keep, pltpu.roll(old_v[v, :, t0], back, 1), pltpu.roll(old_v[v, :, t1], back, 1)
            )
            to_down[rows, :] = pltpu.roll(old_v[v, :, 0:LANES], o & 127, 1)

    @pl.when(even)
    def _():
        put(s_a, s_b)

    @pl.when(jnp.logical_not(even))
    def _():
        put(s_b, s_a)


def own_kernel(
    sizes, start_hbm, old, col_ref, d_hbm, size_hbm, own, ohs, dd, coef, d_v, size_v, start, sem
):
    copies = [
        pltpu.make_async_copy(start_hbm, start, sem.at[2]),
        pltpu.make_async_copy(d_hbm, d_v, sem.at[0]),
        pltpu.make_async_copy(size_hbm, size_v, sem.at[1]),
    ]
    for copy in copies:
        copy.start()
    d = rank_of(sizes)
    copies[0].wait()
    s = d * EL - start[d]
    q, rot = s >> 7, s & 127
    keep = iota((NODES, LANES), 1) < LANES - rot
    back = (LANES - rot) & 127
    for v in range(VARS):
        rows = slice(v * NODES, v * NODES + NODES)
        t = [
            pltpu.roll(
                old[v, :, pl.ds(pl.multiple_of(jnp.maximum(q + i, 0) * LANES, LANES), LANES)], back, 1
            )
            for i in range(3)
        ]
        own[0, rows, :] = jnp.where(keep, t[0], t[1])
        own[1, rows, :] = jnp.where(keep, t[1], t[2])
    code = col_ref[...].astype(I32)
    lane = iota((64, LANES), 1)
    for h in range(2):
        hit = jnp.where((code & 255) == lane + h * LANES, 1.0, 0.0).astype(BF)
        ohs[0:64, h * LANES : h * LANES + LANES] = hit
        ohs[64:128, h * LANES : h * LANES + LANES] = jnp.zeros((64, LANES), BF)
    for copy in copies[1:]:
        copy.wait()
    dd[...] = jnp.concatenate(split(d_v[...]), 0)
    coef[...] = (TIME_STEP * 2.0) / size_v[...]


def chosen(gs, face, v):
    acc = face_rows(gs, None, v, 0)
    for f in range(1, FACES):
        acc = jnp.where(face == f, face_rows(gs, None, v, f), acc)
    return acc


def requested(fld, hot, face, gs, g):
    both = jnp.concatenate([fld[0], fld[1]], 1)
    out = mm(jnp.concatenate(split(both), 0), hot)
    gs[...] = out[0:ROWS, :] + out[ROWS : 2 * ROWS, :]
    for v in range(VARS):
        g[16 * v : 16 * v + 16, :] = chosen(gs, face, v)


def join_kernel(
    sizes, own, r_a, r_b, c_b, rows_ref, edge, col_ref, fld, hot_ref, code_ref, info, meet, g, gs
):
    even = (rank_of(sizes) & 1) == 0
    lane = iota((NODES, LANES), 1)
    below = lane < edge[0:1, :]
    above = lane + LANES >= edge[4:5, :]
    for v in range(VARS):
        rows = slice(v * NODES, v * NODES + NODES)
        a, b = r_a[rows, :], r_b[rows, :]
        fld[0, rows, :] = jnp.where(below, jnp.where(even, b, a), own[0, rows, :])
        fld[1, rows, :] = jnp.where(above, jnp.where(even, a, b), own[1, rows, :])
    lane8 = iota((8, LANES), 1)
    code = jnp.where(
        lane8 < 32,
        r_a[ROWS : ROWS + 8, :],
        jnp.where(lane8 < 64, c_b[0:8, :], rows_ref[0:8, :]),
    ).astype(I32)
    code_ref[...] = code
    lane16 = iota((16, LANES), 1)
    info[...] = jnp.where(
        lane16 < 96, pltpu.roll(rows_ref[...], 64, 1), c_b[...]
    ).astype(I32)
    spot = jnp.broadcast_to(code[0:1, :] & 255, (EL, LANES))
    hot = jnp.where(spot == iota((EL, LANES), 0), 1.0, 0.0).astype(BF)
    hot_ref[...] = hot
    face = jnp.broadcast_to(code[0:1, :] >> 8, (16, LANES))
    requested(fld, hot, face, gs, g)
    same = (col_ref[...].astype(I32) & 255) == jnp.broadcast_to(code[0:1, :] & 255, (64, LANES))
    meet[0:64, :] = jnp.where(same, 1.0, 0.0).astype(BF)
    meet[64:128, :] = jnp.zeros((64, LANES), BF)


def fluxes(u, speeds, p):
    out = []
    for a in range(3):
        s = speeds[a]
        row = [u[0] * s, u[1] * s, u[2] * s, u[3] * s, (u[4] + p) * s]
        row[1 + a] = row[1 + a] + p
        out.append(row)
    return out


def directed(u, axis_is):
    inv = 1.0 / u[0]
    p = 0.4 * (u[4] - 0.5 * ((u[1] * u[1] + u[2] * u[2] + u[3] * u[3]) * inv))
    mom = jnp.where(axis_is[0], u[1], jnp.where(axis_is[1], u[2], u[3]))
    s = mom * inv
    flux = [u[0] * s] + [u[i] * s for i in range(1, 4)] + [(u[4] + p) * s]
    zero = jnp.zeros_like(p)
    flux[1] = flux[1] + jnp.where(axis_is[0], p, zero)
    flux[2] = flux[2] + jnp.where(axis_is[1], p, zero)
    flux[3] = flux[3] + jnp.where(axis_is[0] | axis_is[1], zero, p)
    return flux, jnp.abs(s) + jnp.sqrt(1.4 * p * inv)


def correction(inner, outer, axis_is, half_sign):
    fi, si = directed(inner, axis_is)
    fo, so = directed(outer, axis_is)
    lam = 0.5 * jnp.maximum(si, so)
    return [half_sign * (fo[v] - fi[v]) - lam * (outer[v] - inner[v]) for v in range(VARS)]


def turned(x, b0, b1, b2):
    x = [jnp.where(b1, x[4 * (3 - p) + q], x[4 * p + q]) for p in range(4) for q in range(4)]
    x = [jnp.where(b2, x[4 * p + 3 - q], x[4 * p + q]) for p in range(4) for q in range(4)]
    return [jnp.where(b0, x[4 * t + s], x[4 * s + t]) for s in range(4) for t in range(4)]


def local_kernel(sizes, last, fld, nb_ref, ori_ref, coef_ref, dd_ref, *rest):
    if last:
        old_fld, e, ohs, part, acc, ax, ay, az, xs, xg, xq, xo, xc, it, first = rest

        def put(h, v, new):
            first[h, v * NODES : v * NODES + NODES, :] = new

        added(fld, mm(e[...], ohs[...]), coef_ref, LIFT, put)
        fld = first
    else:
        part, acc, ax, ay, az, xs, xg, xq, xo, xc, it = rest
    for ref in (ax, ay, az):
        ref[...] = jnp.zeros((2, ROWS, LANES), F32)
    d = rank_of(sizes)
    dd = dd_ref[...]
    dh = dd[0:NODES, :]
    pieces = [[[], []] for _ in range(VARS)]
    for h in range(2):
        u = [fld[h, v * NODES : v * NODES + NODES, :] for v in range(VARS)]
        inv = 1.0 / u[0]
        speeds = [u[i] * inv for i in range(1, 4)]
        p = 0.4 * (u[4] - 0.5 * (u[1] * speeds[0] + u[2] * speeds[1] + u[3] * speeds[2]))
        fl = fluxes(u, speeds, p)
        for v in range(VARS):
            hl = [split(fl[a][v]) for a in range(3)]
            pieces[v][0].append(jnp.concatenate([x[0] for x in hl], 0))
            pieces[v][1].append(jnp.concatenate([x[1] for x in hl], 0))
    for v in range(VARS):
        hi = mm(dd, jnp.concatenate(pieces[v][0], 1))
        lo = mm(dh, jnp.concatenate(pieces[v][1], 1))
        vol = hi[0:NODES, :] + hi[NODES : 2 * NODES, :] + lo
        for h in range(2):
            acc[h, v * NODES : v * NODES + NODES, :] = vol[:, h * LANES : h * LANES + LANES]
    for v in range(VARS):
        for f in range(FACES):
            for h in range(2):
                t = face_rows(fld, h, v, f)
                b = v * TABLE
                xs[pl.ds(b + 2 * f + h, 16, stride=PITCH), :] = t
                xg[pl.ds(b + 2 * (f ^ 1) + h, 16, stride=PITCH), :] = t
                xq[pl.ds(b + 2 * (f ^ 1) + 1 - h, 16, stride=PITCH), :] = t
    it[...] = jnp.zeros((32, LANES), I32)
    for h in range(2):
        it[pl.ds(h, FACES, stride=2), :] = nb_ref[:, h * LANES : h * LANES + LANES]
        it[pl.ds(16 + h, FACES, stride=2), :] = ori_ref[:, h * LANES : h * LANES + LANES]
    t = it[0:16, :] - d * EL
    turn = it[16:32, :]
    row = iota((16, LANES), 0)
    local = (t >= 0) & (t < EL) & (row < 12)
    same = ((t >> 7) & 1) == (row & 1)
    idx = t & 127
    b0, b1, b2 = (turn & 1) != 0, (turn & 2) != 0, (turn & 4) != 0
    for v in range(VARS):
        got = []
        for m in range(16):
            rows = pl.ds(v * TABLE + m * PITCH, 16)
            ga = jnp.take_along_axis(xg[rows, :], idx, axis=1)
            gb = jnp.take_along_axis(xq[rows, :], idx, axis=1)
            got.append(jnp.where(same, ga, gb))
        for m, x in enumerate(turned(got, b0, b1, b2)):
            xo[pl.ds(v * TABLE + m * PITCH, 12), :] = x[0:12, :]
    axis_is = (row < 4, (row >= 4) & (row < 8))
    half_sign = jnp.where((row & 2) != 0, 0.5, -0.5)
    for m in range(16):
        rows = [pl.ds(v * TABLE + m * PITCH, 16) for v in range(VARS)]
        cor = correction([xs[r, :] for r in rows], [xo[r, :] for r in rows], axis_is, half_sign)
        for v in range(VARS):
            val = jnp.where(local, LIFT * cor[v], 0.0)
            xc[pl.ds(v * TABLE + m * PITCH, 12), :] = val[0:12, :]
    for v in range(VARS):
        for f in range(FACES):
            for h in range(2):
                put_face_rows(
                    (ax, ay, az), h, v, f, xc[pl.ds(v * TABLE + 2 * f + h, 16, stride=PITCH), :]
                )
    for h in range(2):
        coef = coef_ref[0:1, h * LANES : h * LANES + LANES]
        for v in range(VARS):
            rows = slice(v * NODES, v * NODES + NODES)
            rate = acc[h, rows, :] + ax[h, rows, :] + ay[h, rows, :] + az[h, rows, :]
            new = fld[h, rows, :] - coef * rate
            if last:
                new = 0.5 * old_fld[h, rows, :] + 0.5 * new
            part[h, rows, :] = new


def face_terms(inner, outer, info, live, ro, y, ex, ey, ez):
    for v in range(VARS):
        ro[17 * v : 17 * v + 16, :] = outer[16 * v : 16 * v + 16, :]
    turn = info[8:16, :]
    x = [ro[pl.ds(m, 8, stride=17), :] for m in range(16)]
    for m, val in enumerate(turned(x, (turn & 1) != 0, (turn & 2) != 0, (turn & 4) != 0)):
        y[9 * m : 9 * m + 8, :] = val
    face = jnp.where(live, jnp.broadcast_to(info[0:1, :], (16, LANES)) >> 8, -1)
    axis_is = (face < 2, (face >= 2) & (face < 4))
    half_sign = jnp.where((face & 1) != 0, 0.5, -0.5)
    behind = [y[pl.ds(v, 16, stride=9), :] for v in range(VARS)]
    here = [inner[16 * v : 16 * v + 16, :] for v in range(VARS)]
    cor = correction(here, behind, axis_is, half_sign)
    for ref in (ex, ey, ez):
        ref[...] = jnp.zeros((ROWS, LANES), F32)
    for v in range(VARS):
        for f in range(FACES):
            put_face_rows((ex, ey, ez), None, v, f, jnp.where(face == f, cor[v], 0.0))
    return jnp.concatenate(split(ex[...] + ey[...] + ez[...]), 0)


def added(part, spread, coef_ref, scale, put):
    for h in range(2):
        lanes = slice(h * LANES, h * LANES + LANES)
        coef = scale * coef_ref[0:1, lanes]
        for v in range(VARS):
            rows = slice(v * NODES, v * NODES + NODES)
            low = slice(ROWS + v * NODES, ROWS + v * NODES + NODES)
            put(h, v, part[h, rows, :] - coef * (spread[rows, lanes] + spread[low, lanes]))


def near_kernel(
    part, g, r_a, info, meet, coef_ref, hot_ref, code_ref, parts, q, pb, ro, y, ex, ey, ez, gs, g1
):
    hot = hot_ref[...]
    asked = jnp.broadcast_to(code_ref[0:1, :] >> 8, (16, LANES))
    requested(part, hot, asked, gs, g1)
    ch, cl = split(jnp.broadcast_to(LIFT * coef_ref[0:1, :], (16, EL)))
    coef = mm(ch, hot) + mm(cl, hot)
    lane = iota((16, LANES), 1)
    terms = face_terms(pltpu.roll(g[...], 64, 1), r_a[...], info, lane < 32, ro, y, ex, ey, ez)
    parts[...] = terms
    change = mm(terms, meet[...])
    ex[...] = change[0:ROWS, :] + change[ROWS : 2 * ROWS, :]
    for v in range(VARS):
        rows = slice(16 * v, 16 * v + 16)
        new = g1[rows, :] - coef * chosen(ex, asked, v)
        q[rows, :] = new
        pb[rows, :] = jnp.where(lane < 32, pltpu.roll(new, 96, 1), g[rows, :])
    pb[80:96, :] = coef


def pair_kernel(info, rows_ref, meet, after, pairs):
    theirs = jnp.transpose(jnp.broadcast_to(info[0:1, :].astype(F32), (LANES, LANES))).astype(I32)
    mine = jnp.broadcast_to(rows_ref[0:1, :].astype(I32), (LANES, LANES))
    row, lane = iota((LANES, LANES), 0), iota((LANES, LANES), 1)
    to_b = (lane >= 32) & (lane < 64)
    on = ((theirs & 255) == (mine & 255)) & (row >= 96) & to_b
    kept = jnp.where(to_b, 0.0, meet[...].astype(F32))
    pairs[...] = jnp.where(on, 1.0, kept).astype(BF)


def far_kernel(g, q1, pb, r_b, info, rows_ref, code_ref, pairs, e1, q, e, ro, y, ex, ey, ez):
    lane = iota((80, LANES), 1)
    mine = pltpu.roll(g[...], 64, 1)
    got = r_b[0:80, :]
    lane16 = iota((16, LANES), 1)
    to_b = (lane16 >= 32) & (lane16 < 64)
    inner, outer = jnp.where(lane < 64, mine, got), jnp.where(lane < 64, got, mine)
    terms = face_terms(inner, outer, info, to_b | (lane16 >= 96), ro, y, ex, ey, ez)
    e[...] = e1[...] + terms
    change = mm(terms, pairs[...])
    ex[...] = change[0:ROWS, :] + change[ROWS : 2 * ROWS, :]
    code = jnp.where(to_b[0:1, :], rows_ref[0:1, :].astype(I32), code_ref[0:1, :])
    face = jnp.broadcast_to(code >> 8, (16, LANES))
    coef = jnp.where(to_b, r_b[80:96, :], pb[80:96, :])
    for v in range(VARS):
        rows = slice(16 * v, 16 * v + 16)
        base = jnp.where(to_b, pltpu.roll(r_b[rows, :], 32, 1), q1[rows, :])
        q[rows, :] = base - coef * chosen(ex, face, v)


def last_kernel(part, q, r_a, info, ohs, coef_ref, out, ro, y, ex, ey, ez):
    lane = iota((80, LANES), 1)
    outer = jnp.where(lane < 32, r_a[...], q[...])
    live = iota((16, LANES), 1) < 64
    parts = face_terms(pltpu.roll(q[...], 64, 1), outer, info, live, ro, y, ex, ey, ez)
    spread = mm(parts, ohs[...])

    def put(h, v, new):
        out[v, :, h * LANES : h * LANES + LANES] = new

    added(part, spread, coef_ref, 0.5 * LIFT, put)


def call(body, out_shape, scratch, cost, args, hbm=(), spare=None):
    spec = pl.BlockSpec(memory_space=pltpu.VMEM)
    specs = []
    for i, a in enumerate(args):
        if i in hbm:
            specs.append(pl.BlockSpec(memory_space=pltpu.HBM))
        elif a.dtype == I32 and a.ndim == 1:
            specs.append(pl.BlockSpec(memory_space=pltpu.SMEM))
        else:
            specs.append(spec)
    return pl.pallas_call(
        body,
        out_shape=out_shape,
        in_specs=specs,
        out_specs=jax.tree.map(lambda _: spec, out_shape),
        scratch_shapes=scratch,
        cost_estimate=pl.CostEstimate(flops=cost, bytes_accessed=cost, transcendentals=0),
        compiler_params=pltpu.CompilerParams(vmem_limit_bytes=32 * 1024 * 1024),
    )(*[pltpu.with_memory_space_constraint(a, pltpu.HBM) if i in hbm else a for i, a in enumerate(args)])


def shape(*dims, dtype=F32):
    return jax.ShapeDtypeStruct(dims, dtype)


def per_device(sizes, old_state, element_size, old_start, neighbour, orientation):
    n = sizes[0] * sizes[1] * sizes[2]
    pairs_a = [(i, i ^ 1) for i in range(n)]
    pairs_b = [(i, (i + 1) % n if i % 2 else (i - 1) % n) for i in range(n)]

    size = element_size.reshape(1, EL)
    deriv = jnp.asarray(node_derivatives())
    s_a, s_b, rows, col, old_v, nb_v, ori_v, edge = call(
        functools.partial(send_kernel, sizes),
        (
            shape(ROWS + 16, LANES),
            shape(ROWS, LANES),
            shape(16, LANES),
            shape(64, LANES),
            shape(*old_state.shape),
            shape(FACES, EL, dtype=I32),
            shape(FACES, EL, dtype=I32),
            shape(8, LANES, dtype=I32),
        ),
        [
            pltpu.VMEM((16, EL), F32),
            pltpu.SMEM(old_start.shape, I32),
            pltpu.SemaphoreType.DMA((3 + VARS,)),
        ],
        10000,
        (old_start, old_state, neighbour, orientation),
        hbm=(0, 1, 2, 3),
    )
    r_a = lax.ppermute(s_a, AXES, pairs_a)
    c_b = lax.ppermute(rows, AXES, pairs_b)
    r_b = lax.ppermute(s_b, AXES, pairs_b[1:-1])
    own, ohs, dd, coef = call(
        functools.partial(own_kernel, sizes),
        (
            shape(2, ROWS, LANES),
            shape(LANES, EL, dtype=BF),
            shape(2 * NODES, 3 * NODES, dtype=BF),
            shape(1, EL),
        ),
        [
            pltpu.VMEM((NODES, 3 * NODES), F32),
            pltpu.VMEM((1, EL), F32),
            pltpu.SMEM(old_start.shape, I32),
            pltpu.SemaphoreType.DMA((3,)),
        ],
        10000,
        (old_start, old_v, col, deriv, size),
        hbm=(0, 3, 4),
    )
    table = pltpu.VMEM((ROWS, LANES), F32)
    square = pltpu.VMEM((LANES + 24, LANES), F32)
    traces = shape(80, LANES)
    state = shape(2, ROWS, LANES)
    fld, hot, code, info, meet, g = call(
        functools.partial(join_kernel, sizes),
        (
            state,
            shape(EL, LANES, dtype=BF),
            shape(8, LANES, dtype=I32),
            shape(16, LANES, dtype=I32),
            shape(LANES, LANES, dtype=BF),
            traces,
        ),
        [table],
        10000,
        (own, r_a, r_b, c_b, rows, edge, col),
    )

    def local(last, *args):
        faces = pltpu.VMEM((VARS * TABLE + 8, LANES), F32)
        both = pltpu.VMEM((2, ROWS, LANES), F32)
        return call(
            functools.partial(local_kernel, sizes, last),
            state,
            [both] * 4 + [faces] * 5 + [pltpu.VMEM((32, LANES), I32)] + ([both] if last else []),
            20000,
            args,
        )

    r_a = lax.ppermute(g, AXES, pairs_a)
    part = local(False, fld, nb_v, ori_v, coef, dd)
    terms = shape(2 * ROWS, LANES, dtype=BF)
    scratch = [square, square, table, table, table]
    e1, q1, pb = call(
        near_kernel,
        (terms, traces, shape(96, LANES)),
        scratch + [table, pltpu.VMEM((80, LANES), F32)],
        10000,
        (part, g, r_a, info, meet, coef, hot, code),
    )
    r_b = lax.ppermute(pb, AXES, pairs_b)
    pairs = call(
        pair_kernel, shape(LANES, LANES, dtype=BF), [], 10000, (info, rows, meet, q1)
    )
    q, e = call(
        far_kernel,
        (traces, terms),
        scratch,
        10000,
        (g, q1, pb, r_b, info, rows, code, pairs, e1),
    )
    r_a = lax.ppermute(q, AXES, pairs_a)
    part = local(True, part, nb_v, ori_v, coef, dd, fld, e, ohs)
    return call(
        last_kernel,
        shape(VARS, NODES, EL),
        scratch,
        10000,
        (part, q, r_a, info, ohs, coef),
    )


def solution(mesh):
    sizes = tuple(mesh.shape[a] for a in AXES)
    in_specs = (P(None, None, AXES), P(AXES), P(), P(None, AXES), P(None, AXES))
    return jax.shard_map(
        functools.partial(per_device, sizes),
        mesh=mesh,
        in_specs=in_specs,
        out_specs=P(None, None, AXES),
        check_vma=False,
    )
```

```python
import functools

import jax
import jax.numpy as jnp
import numpy as np
from jax import lax
from jax.experimental import pallas as pl
from jax.experimental.pallas import tpu as pltpu
from jax.sharding import PartitionSpec as P

AXES = ("gx", "gy", "gz")
TIME_STEP = 0.03
LIFT = 6.0
VARS = 5
NODES = 64
EL = 256
LANES = 128
PITCH = 12
TABLE = 16 * PITCH
REMOTE = 32
FACES = 6
ROWS = VARS * NODES
BF = jnp.bfloat16
F32 = jnp.float32
I32 = jnp.int32


def gll_derivative():
    points = np.array([-1.0, -1.0 / np.sqrt(5.0), 1.0 / np.sqrt(5.0), 1.0])
    weights = np.array(
        [1.0 / np.prod([points[c] - points[p] for p in range(4) if p != c]) for c in range(4)]
    )
    matrix = np.zeros((4, 4))
    for row in range(4):
        for col in range(4):
            if row != col:
                matrix[row, col] = weights[col] / weights[row] / (points[row] - points[col])
        matrix[row, row] = -np.sum(matrix[row])
    return matrix


def node_derivatives():
    d, one = gll_derivative(), np.eye(4)
    parts = [
        np.kron(np.kron(d, one), one),
        np.kron(np.kron(one, d), one),
        np.kron(np.kron(one, one), d),
    ]
    return np.concatenate(parts, axis=1).astype(np.float32)


def iota(shape, dim):
    return lax.broadcasted_iota(I32, shape, dim)


def split(x):
    hi = x.astype(BF)
    return hi, (x - hi.astype(F32)).astype(BF)


def mm(a, b):
    return jnp.dot(a, b, preferred_element_type=F32)


def rows_at(lead, base, f, i=None):
    if f < 2:
        rows = pl.ds(base + 48 * f, 16)
    elif f < 4:
        rows = pl.ds(base + 12 * (f - 2) + 16 * i, 4)
    else:
        rows = pl.ds(base + 3 * (f - 4), 16, stride=4)
    return (rows, slice(None)) if lead is None else (lead, rows, slice(None))


def face_rows(ref, lead, v, f):
    if f in (2, 3):
        return jnp.concatenate([ref[rows_at(lead, v * NODES, f, i)] for i in range(4)], 0)
    return ref[rows_at(lead, v * NODES, f)]


def put_face_rows(across, lead, v, f, val):
    ref = across[f // 2]
    if f in (2, 3):
        for i in range(4):
            ref[rows_at(lead, v * NODES, f, i)] = val[4 * i : 4 * i + 4, :]
    else:
        ref[rows_at(lead, v * NODES, f)] = val


def rank_of(sizes):
    return (lax.axis_index("gx") * sizes[1] + lax.axis_index("gy")) * sizes[2] + lax.axis_index("gz")


def places(mask):
    count = mask.shape[0]
    upper = jnp.where(iota((EL, EL), 0) <= iota((EL, EL), 1), 1.0, 0.0).astype(BF)
    inclusive = mm(mask.astype(BF), upper)
    total = jnp.broadcast_to(inclusive[:, EL - 1 : EL], (count, LANES)).astype(BF)
    r, c = iota((count, count), 0), iota((count, count), 1)
    lower = jnp.where((c < r) & ((c >> 3) == (r >> 3)), 1.0, 0.0).astype(BF)
    offset = mm(lower, total)[:, 0:1]
    return jnp.where(mask > 0.5, inclusive + offset - 1.0, -1.0)


def listed(place, values):
    slot = iota((REMOTE, EL), 0).astype(F32)
    accs = [jnp.zeros((REMOTE, EL), F32) for _ in values]
    for f in range(FACES):
        hit = place[f : f + 1, :] == slot
        accs = [jnp.where(hit, x[f : f + 1, :], acc) for x, acc in zip(values, accs)]
    return [jnp.sum(acc, 1, keepdims=True) for acc in accs]


def send_kernel(sizes, start_hbm, old, nb, ori, s_a, s_b, rows_ref, col_ref, old_v, nb_v, ori_v, edge, mk, start, sem):
    n = sizes[0] * sizes[1] * sizes[2]
    copies = [
        pltpu.make_async_copy(nb, nb_v, sem.at[0]),
        pltpu.make_async_copy(ori, ori_v, sem.at[1]),
        pltpu.make_async_copy(start_hbm, start, sem.at[2]),
        pltpu.make_async_copy(old, old_v, sem.at[3]),
    ]
    for copy in copies:
        copy.start()
    d = rank_of(sizes)
    even = (d & 1) == 0
    up = jnp.where(d + 1 == n, 0, d + 1) * EL
    down = jnp.where(d == 0, n - 1, d - 1) * EL
    mk[...] = jnp.zeros((16, EL), F32)
    copies[0].wait()
    nb = nb_v[...]
    rel = [nb - jnp.where(even, up, down), nb - jnp.where(even, down, up)]
    for k in range(2):
        mk[8 * k : 8 * k + FACES, :] = jnp.where((rel[k] >= 0) & (rel[k] < EL), 1.0, 0.0)
    place = places(mk[...])
    copies[1].wait()
    face = iota((FACES, EL), 0)
    own = (face * EL + iota((FACES, EL), 1) + 2048 * ori_v[...]).astype(F32)
    lists = []
    for k in range(2):
        lists.append(listed(place[8 * k : 8 * k + 8, :], [((face ^ 1) * EL + rel[k]).astype(F32), own]))
    col = jnp.concatenate([lists[0][0], lists[1][0], lists[0][1], lists[1][1]], 0)
    wide = jnp.broadcast_to(col, (LANES, LANES))
    row = jnp.transpose(wide)[0:8, :]
    turn = jnp.floor(row * (1.0 / 2048.0))
    code = row - 2048.0 * turn
    rows_ref[0:8, :] = code
    rows_ref[8:16, :] = turn
    col_ref[...] = wide[64:128, :]
    s_a[ROWS : ROWS + 8, :] = code
    s_a[ROWS + 8 : ROWS + 16, :] = turn

    copies[2].wait()
    o = start[d] - d * EL
    edge[0:4, :] = jnp.broadcast_to(o, (4, LANES))
    edge[4:8, :] = jnp.broadcast_to(start[d + 1] - d * EL, (4, LANES))
    first = EL - o
    q, rot = first >> 7, first & 127
    keep = iota((NODES, LANES), 1) < LANES - rot
    back = (LANES - rot) & 127
    t0 = pl.ds(pl.multiple_of(q * LANES, LANES), LANES)
    t1 = pl.ds(pl.multiple_of(jnp.minimum(q + 1, 3) * LANES, LANES), LANES)
    for copy in copies[3:]:
        copy.wait()

    def put(to_up, to_down):
        for v in range(VARS):
            rows = slice(v * NODES, v * NODES + NODES)
            to_up[rows, :] = jnp.where(
                keep, pltpu.roll(old_v[v, :, t0], back, 1), pltpu.roll(old_v[v, :, t1], back, 1)
            )
            to_down[rows, :] = pltpu.roll(old_v[v, :, 0:LANES], o & 127, 1)

    @pl.when(even)
    def _():
        put(s_a, s_b)

    @pl.when(jnp.logical_not(even))
    def _():
        put(s_b, s_a)


def own_kernel(
    sizes, start_hbm, old, col_ref, d_hbm, size_hbm, own, ohs, dd, coef, d_v, size_v, start, sem
):
    copies = [
        pltpu.make_async_copy(start_hbm, start, sem.at[2]),
        pltpu.make_async_copy(d_hbm, d_v, sem.at[0]),
        pltpu.make_async_copy(size_hbm, size_v, sem.at[1]),
    ]
    for copy in copies:
        copy.start()
    d = rank_of(sizes)
    copies[0].wait()
    s = d * EL - start[d]
    q, rot = s >> 7, s & 127
    keep = iota((NODES, LANES), 1) < LANES - rot
    back = (LANES - rot) & 127
    for v in range(VARS):
        rows = slice(v * NODES, v * NODES + NODES)
        t = [
            pltpu.roll(
                old[v, :, pl.ds(pl.multiple_of(jnp.maximum(q + i, 0) * LANES, LANES), LANES)], back, 1
            )
            for i in range(3)
        ]
        own[0, rows, :] = jnp.where(keep, t[0], t[1])
        own[1, rows, :] = jnp.where(keep, t[1], t[2])
    code = col_ref[...].astype(I32)
    lane = iota((64, LANES), 1)
    for h in range(2):
        hit = jnp.where((code & 255) == lane + h * LANES, 1.0, 0.0).astype(BF)
        ohs[0:64, h * LANES : h * LANES + LANES] = hit
        ohs[64:128, h * LANES : h * LANES + LANES] = jnp.zeros((64, LANES), BF)
    for copy in copies[1:]:
        copy.wait()
    dd[...] = jnp.concatenate(split(d_v[...]), 0)
    coef[...] = (TIME_STEP * 2.0) / size_v[...]


def chosen(gs, face, v):
    acc = face_rows(gs, None, v, 0)
    for f in range(1, FACES):
        acc = jnp.where(face == f, face_rows(gs, None, v, f), acc)
    return acc


def requested(fld, hot, face, gs, g):
    both = jnp.concatenate([fld[0], fld[1]], 1)
    out = mm(jnp.concatenate(split(both), 0), hot)
    gs[...] = out[0:ROWS, :] + out[ROWS : 2 * ROWS, :]
    for v in range(VARS):
        g[16 * v : 16 * v + 16, :] = chosen(gs, face, v)


def join_kernel(
    sizes, own, r_a, r_b, c_b, rows_ref, edge, col_ref, fld, hot_ref, code_ref, info, meet, g, gs
):
    even = (rank_of(sizes) & 1) == 0
    lane = iota((NODES, LANES), 1)
    below = lane < edge[0:1, :]
    above = lane + LANES >= edge[4:5, :]
    for v in range(VARS):
        rows = slice(v * NODES, v * NODES + NODES)
        a, b = r_a[rows, :], r_b[rows, :]
        fld[0, rows, :] = jnp.where(below, jnp.where(even, b, a), own[0, rows, :])
        fld[1, rows, :] = jnp.where(above, jnp.where(even, a, b), own[1, rows, :])
    lane8 = iota((8, LANES), 1)
    code = jnp.where(
        lane8 < 32,
        r_a[ROWS : ROWS + 8, :],
        jnp.where(lane8 < 64, c_b[0:8, :], rows_ref[0:8, :]),
    ).astype(I32)
    code_ref[...] = code
    lane16 = iota((16, LANES), 1)
    info[...] = jnp.where(
        lane16 < 96, pltpu.roll(rows_ref[...], 64, 1), c_b[...]
    ).astype(I32)
    spot = jnp.broadcast_to(code[0:1, :] & 255, (EL, LANES))
    hot = jnp.where(spot == iota((EL, LANES), 0), 1.0, 0.0).astype(BF)
    hot_ref[...] = hot
    face = jnp.broadcast_to(code[0:1, :] >> 8, (16, LANES))
    requested(fld, hot, face, gs, g)
    same = (col_ref[...].astype(I32) & 255) == jnp.broadcast_to(code[0:1, :] & 255, (64, LANES))
    meet[0:64, :] = jnp.where(same, 1.0, 0.0).astype(BF)
    meet[64:128, :] = jnp.zeros((64, LANES), BF)


def fluxes(u, speeds, p):
    out = []
    for a in range(3):
        s = speeds[a]
        row = [u[0] * s, u[1] * s, u[2] * s, u[3] * s, (u[4] + p) * s]
        row[1 + a] = row[1 + a] + p
        out.append(row)
    return out


def directed(u, axis_is):
    inv = pl.reciprocal(u[0])
    p = 0.4 * u[4] - 0.2 * ((u[1] * u[1] + u[2] * u[2] + u[3] * u[3]) * inv)
    mom = jnp.where(axis_is[0], u[1], jnp.where(axis_is[1], u[2], u[3]))
    s = mom * inv
    return p, mom, s, jnp.abs(s) + jnp.sqrt(1.4 * (p * inv))


def correction(inner, outer, axis_is, sign_scale, scale):
    pi, mi, si, ci = directed(inner, axis_is)
    po, mo, so, co = directed(outer, axis_is)
    lam = scale * jnp.maximum(ci, co)
    dp = po - pi
    along = (axis_is[0], axis_is[1], jnp.logical_not(axis_is[0] | axis_is[1]))
    flux = [mo - mi]
    flux += [
        (outer[i] * so - inner[i] * si) + jnp.where(along[i - 1], dp, 0.0) for i in range(1, 4)
    ]
    flux += [(outer[4] + po) * so - (inner[4] + pi) * si]
    return [sign_scale * flux[v] - lam * (outer[v] - inner[v]) for v in range(VARS)]


def turned(x, b0, b1, b2):
    x = [jnp.where(b1, x[4 * (3 - p) + q], x[4 * p + q]) for p in range(4) for q in range(4)]
    x = [jnp.where(b2, x[4 * p + 3 - q], x[4 * p + q]) for p in range(4) for q in range(4)]
    return [jnp.where(b0, x[4 * t + s], x[4 * s + t]) for s in range(4) for t in range(4)]


def local_kernel(sizes, last, fld, nb_ref, ori_ref, coef_ref, dd_ref, *rest):
    if last:
        old_fld, e, ohs, part, acc, ax, ay, az, xs, xg, xq, xo, xc, it, first = rest

        def put(h, v, new):
            first[h, v * NODES : v * NODES + NODES, :] = new

        added(fld, mm(e[...], ohs[...]), coef_ref, LIFT, put)
        fld = first
    else:
        part, acc, ax, ay, az, xs, xg, xq, xo, xc, it = rest
    for ref in (ax, ay, az):
        ref[...] = jnp.zeros((2, ROWS, LANES), F32)
    d = rank_of(sizes)
    dd = dd_ref[...]
    dh = dd[0:NODES, :]
    pieces = [[[], []] for _ in range(VARS)]
    for h in range(2):
        u = [fld[h, v * NODES : v * NODES + NODES, :] for v in range(VARS)]
        inv = 1.0 / u[0]
        speeds = [u[i] * inv for i in range(1, 4)]
        p = 0.4 * (u[4] - 0.5 * (u[1] * speeds[0] + u[2] * speeds[1] + u[3] * speeds[2]))
        fl = fluxes(u, speeds, p)
        for v in range(VARS):
            hl = [split(fl[a][v]) for a in range(3)]
            pieces[v][0].append(jnp.concatenate([x[0] for x in hl], 0))
            pieces[v][1].append(jnp.concatenate([x[1] for x in hl], 0))
    for v in range(VARS):
        hi = mm(dd, jnp.concatenate(pieces[v][0], 1))
        lo = mm(dh, jnp.concatenate(pieces[v][1], 1))
        vol = hi[0:NODES, :] + hi[NODES : 2 * NODES, :] + lo
        for h in range(2):
            acc[h, v * NODES : v * NODES + NODES, :] = vol[:, h * LANES : h * LANES + LANES]
    for v in range(VARS):
        for f in range(FACES):
            for h in range(2):
                t = face_rows(fld, h, v, f)
                b = v * TABLE
                xs[pl.ds(b + 2 * f + h, 16, stride=PITCH), :] = t
                xg[pl.ds(b + 2 * (f ^ 1) + h, 16, stride=PITCH), :] = t
                xq[pl.ds(b + 2 * (f ^ 1) + 1 - h, 16, stride=PITCH), :] = t
    it[...] = jnp.zeros((32, LANES), I32)
    for h in range(2):
        it[pl.ds(h, FACES, stride=2), :] = nb_ref[:, h * LANES : h * LANES + LANES]
        it[pl.ds(16 + h, FACES, stride=2), :] = ori_ref[:, h * LANES : h * LANES + LANES]
    t = it[0:16, :] - d * EL
    turn = it[16:32, :]
    row = iota((16, LANES), 0)
    local = (t >= 0) & (t < EL) & (row < 12)
    same = ((t >> 7) & 1) == (row & 1)
    idx = t & 127
    b0, b1, b2 = (turn & 1) != 0, (turn & 2) != 0, (turn & 4) != 0
    for v in range(VARS):
        got = []
        for m in range(16):
            rows = pl.ds(v * TABLE + m * PITCH, 16)
            ga = jnp.take_along_axis(xg[rows, :], idx, axis=1)
            gb = jnp.take_along_axis(xq[rows, :], idx, axis=1)
            got.append(jnp.where(same, ga, gb))
        for m, x in enumerate(turned(got, b0, b1, b2)):
            xo[pl.ds(v * TABLE + m * PITCH, 12), :] = x[0:12, :]
    axis_is = (row < 4, (row >= 4) & (row < 8))
    sign_scale = jnp.where((row & 2) != 0, 0.5 * LIFT, -0.5 * LIFT)
    for m in range(16):
        rows = [pl.ds(v * TABLE + m * PITCH, 16) for v in range(VARS)]
        inner, outer = [xs[r, :] for r in rows], [xo[r, :] for r in rows]
        cor = correction(inner, outer, axis_is, sign_scale, 0.5 * LIFT)
        for v in range(VARS):
            val = jnp.where(local, cor[v], 0.0)
            xc[pl.ds(v * TABLE + m * PITCH, 12), :] = val[0:12, :]
    for v in range(VARS):
        for f in range(FACES):
            for h in range(2):
                put_face_rows(
                    (ax, ay, az), h, v, f, xc[pl.ds(v * TABLE + 2 * f + h, 16, stride=PITCH), :]
                )
    for h in range(2):
        coef = coef_ref[0:1, h * LANES : h * LANES + LANES]
        for v in range(VARS):
            rows = slice(v * NODES, v * NODES + NODES)
            rate = acc[h, rows, :] + ax[h, rows, :] + ay[h, rows, :] + az[h, rows, :]
            new = fld[h, rows, :] - coef * rate
            if last:
                new = 0.5 * old_fld[h, rows, :] + 0.5 * new
            part[h, rows, :] = new


def face_terms(inner, outer, info, live, ro, y, ex, ey, ez):
    for v in range(VARS):
        ro[17 * v : 17 * v + 16, :] = outer[16 * v : 16 * v + 16, :]
    turn = info[8:16, :]
    x = [ro[pl.ds(m, 8, stride=17), :] for m in range(16)]
    for m, val in enumerate(turned(x, (turn & 1) != 0, (turn & 2) != 0, (turn & 4) != 0)):
        y[9 * m : 9 * m + 8, :] = val
    face = jnp.where(live, jnp.broadcast_to(info[0:1, :], (16, LANES)) >> 8, -1)
    axis_is = (face < 2, (face >= 2) & (face < 4))
    half_sign = jnp.where((face & 1) != 0, 0.5, -0.5)
    behind = [y[pl.ds(v, 16, stride=9), :] for v in range(VARS)]
    here = [inner[16 * v : 16 * v + 16, :] for v in range(VARS)]
    cor = correction(here, behind, axis_is, half_sign, 0.5)
    for ref in (ex, ey, ez):
        ref[...] = jnp.zeros((ROWS, LANES), F32)
    for v in range(VARS):
        for f in range(FACES):
            put_face_rows((ex, ey, ez), None, v, f, jnp.where(face == f, cor[v], 0.0))
    return jnp.concatenate(split(ex[...] + ey[...] + ez[...]), 0)


def added(part, spread, coef_ref, scale, put):
    for h in range(2):
        lanes = slice(h * LANES, h * LANES + LANES)
        coef = scale * coef_ref[0:1, lanes]
        for v in range(VARS):
            rows = slice(v * NODES, v * NODES + NODES)
            low = slice(ROWS + v * NODES, ROWS + v * NODES + NODES)
            put(h, v, part[h, rows, :] - coef * (spread[rows, lanes] + spread[low, lanes]))


def near_kernel(
    part, g, r_a, info, meet, coef_ref, hot_ref, code_ref, parts, q, pb, unit, ro, y, ex, ey, ez, gs, g1
):
    hot = hot_ref[...]
    asked = jnp.broadcast_to(code_ref[0:1, :] >> 8, (16, LANES))
    requested(part, hot, asked, gs, g1)
    ch, cl = split(jnp.broadcast_to(LIFT * coef_ref[0:1, :], (16, EL)))
    coef = mm(ch, hot) + mm(cl, hot)
    lane = iota((16, LANES), 1)
    terms = face_terms(pltpu.roll(g[...], 64, 1), r_a[...], info, lane < 32, ro, y, ex, ey, ez)
    parts[...] = terms
    change = mm(terms, meet[...])
    ex[...] = change[0:ROWS, :] + change[ROWS : 2 * ROWS, :]
    for v in range(VARS):
        rows = slice(16 * v, 16 * v + 16)
        new = g1[rows, :] - coef * chosen(ex, asked, v)
        q[rows, :] = new
        sent = jnp.where((lane >= 64) & (lane < 96), pltpu.roll(coef, 32, 1), g[rows, :])
        pb[rows, :] = jnp.where(lane < 32, pltpu.roll(new, 96, 1), sent)
    unit[...] = coef


def pair_kernel(info, rows_ref, meet, after, pairs):
    theirs = jnp.transpose(jnp.broadcast_to(info[0:1, :].astype(F32), (LANES, LANES))).astype(I32)
    mine = jnp.broadcast_to(rows_ref[0:1, :].astype(I32), (LANES, LANES))
    row, lane = iota((LANES, LANES), 0), iota((LANES, LANES), 1)
    to_b = (lane >= 32) & (lane < 64)
    on = ((theirs & 255) == (mine & 255)) & (row >= 96) & to_b
    kept = jnp.where(to_b, 0.0, meet[...].astype(F32))
    pairs[...] = jnp.where(on, 1.0, kept).astype(BF)


def far_kernel(g, q1, unit, r_b, info, rows_ref, code_ref, pairs, e1, q, e, ro, y, ex, ey, ez):
    lane = iota((80, LANES), 1)
    mine = pltpu.roll(g[...], 64, 1)
    got = r_b[...]
    lane16 = iota((16, LANES), 1)
    to_b = (lane16 >= 32) & (lane16 < 64)
    inner, outer = jnp.where(lane < 64, mine, got), jnp.where(lane < 64, got, mine)
    terms = face_terms(inner, outer, info, to_b | (lane16 >= 96), ro, y, ex, ey, ez)
    e[...] = e1[...] + terms
    change = mm(terms, pairs[...])
    ex[...] = change[0:ROWS, :] + change[ROWS : 2 * ROWS, :]
    code = jnp.where(to_b[0:1, :], rows_ref[0:1, :].astype(I32), code_ref[0:1, :])
    face = jnp.broadcast_to(code >> 8, (16, LANES))
    coef = jnp.where(to_b, pltpu.roll(r_b[0:16, :], 96, 1), unit[...])
    for v in range(VARS):
        rows = slice(16 * v, 16 * v + 16)
        base = jnp.where(to_b, pltpu.roll(r_b[rows, :], 32, 1), q1[rows, :])
        q[rows, :] = base - coef * chosen(ex, face, v)


def last_kernel(part, q, r_a, info, ohs, coef_ref, out_hbm, ro, y, ex, ey, ez, out, sem):
    lane = iota((80, LANES), 1)
    outer = jnp.where(lane < 32, r_a[...], q[...])
    live = iota((16, LANES), 1) < 64
    parts = face_terms(pltpu.roll(q[...], 64, 1), outer, info, live, ro, y, ex, ey, ez)
    spread = mm(parts, ohs[...])
    copies = []
    for v in range(VARS):
        for h in range(2):
            lanes = slice(h * LANES, h * LANES + LANES)
            rows = slice(v * NODES, v * NODES + NODES)
            low = slice(ROWS + v * NODES, ROWS + v * NODES + NODES)
            coef = (0.5 * LIFT) * coef_ref[0:1, lanes]
            out[v, :, lanes] = part[h, rows, :] - coef * (spread[rows, lanes] + spread[low, lanes])
        copies.append(pltpu.make_async_copy(out.at[v], out_hbm.at[v], sem.at[v]))
        copies[v].start()
    for copy in copies:
        copy.wait()


def call(body, out_shape, scratch, cost, args, hbm=(), out_hbm=False):
    spec = pl.BlockSpec(memory_space=pltpu.VMEM)
    specs = []
    for i, a in enumerate(args):
        if i in hbm:
            specs.append(pl.BlockSpec(memory_space=pltpu.HBM))
        elif a.dtype == I32 and a.ndim == 1:
            specs.append(pl.BlockSpec(memory_space=pltpu.SMEM))
        else:
            specs.append(spec)
    return pl.pallas_call(
        body,
        out_shape=out_shape,
        in_specs=specs,
        out_specs=pl.BlockSpec(memory_space=pltpu.HBM)
        if out_hbm
        else jax.tree.map(lambda _: spec, out_shape),
        scratch_shapes=scratch,
        cost_estimate=pl.CostEstimate(flops=cost, bytes_accessed=cost, transcendentals=0),
        compiler_params=pltpu.CompilerParams(vmem_limit_bytes=32 * 1024 * 1024),
    )(*[pltpu.with_memory_space_constraint(a, pltpu.HBM) if i in hbm else a for i, a in enumerate(args)])


def shape(*dims, dtype=F32):
    return jax.ShapeDtypeStruct(dims, dtype)


def per_device(sizes, old_state, element_size, old_start, neighbour, orientation):
    n = sizes[0] * sizes[1] * sizes[2]
    pairs_a = [(i, i ^ 1) for i in range(n)]
    pairs_b = [(i, (i + 1) % n if i % 2 else (i - 1) % n) for i in range(n)]

    size = element_size.reshape(1, EL)
    deriv = jnp.asarray(node_derivatives())
    s_a, s_b, rows, col, old_v, nb_v, ori_v, edge = call(
        functools.partial(send_kernel, sizes),
        (
            shape(ROWS + 16, LANES),
            shape(ROWS, LANES),
            shape(16, LANES),
            shape(64, LANES),
            shape(*old_state.shape),
            shape(FACES, EL, dtype=I32),
            shape(FACES, EL, dtype=I32),
            shape(8, LANES, dtype=I32),
        ),
        [
            pltpu.VMEM((16, EL), F32),
            pltpu.SMEM(old_start.shape, I32),
            pltpu.SemaphoreType.DMA((4,)),
        ],
        10000,
        (old_start, old_state, neighbour, orientation),
        hbm=(0, 1, 2, 3),
    )
    r_a = lax.ppermute(s_a, AXES, pairs_a)
    c_b = lax.ppermute(rows, AXES, pairs_b)
    r_b = lax.ppermute(s_b, AXES, pairs_b[1:-1])
    own, ohs, dd, coef = call(
        functools.partial(own_kernel, sizes),
        (
            shape(2, ROWS, LANES),
            shape(LANES, EL, dtype=BF),
            shape(2 * NODES, 3 * NODES, dtype=BF),
            shape(1, EL),
        ),
        [
            pltpu.VMEM((NODES, 3 * NODES), F32),
            pltpu.VMEM((1, EL), F32),
            pltpu.SMEM(old_start.shape, I32),
            pltpu.SemaphoreType.DMA((3,)),
        ],
        10000,
        (old_start, old_v, col, deriv, size),
        hbm=(0, 3, 4),
    )
    table = pltpu.VMEM((ROWS, LANES), F32)
    square = pltpu.VMEM((LANES + 24, LANES), F32)
    traces = shape(80, LANES)
    state = shape(2, ROWS, LANES)
    fld, hot, code, info, meet, g = call(
        functools.partial(join_kernel, sizes),
        (
            state,
            shape(EL, LANES, dtype=BF),
            shape(8, LANES, dtype=I32),
            shape(16, LANES, dtype=I32),
            shape(LANES, LANES, dtype=BF),
            traces,
        ),
        [table],
        10000,
        (own, r_a, r_b, c_b, rows, edge, col),
    )

    def local(last, *args):
        faces = pltpu.VMEM((VARS * TABLE + 8, LANES), F32)
        both = pltpu.VMEM((2, ROWS, LANES), F32)
        return call(
            functools.partial(local_kernel, sizes, last),
            state,
            [both] * 4 + [faces] * 5 + [pltpu.VMEM((32, LANES), I32)] + ([both] if last else []),
            20000,
            args,
        )

    r_a = lax.ppermute(g, AXES, pairs_a)
    part = local(False, fld, nb_v, ori_v, coef, dd)
    terms = shape(2 * ROWS, LANES, dtype=BF)
    scratch = [square, square, table, table, table]
    e1, q1, pb, unit = call(
        near_kernel,
        (terms, traces, traces, shape(16, LANES)),
        scratch + [table, pltpu.VMEM((80, LANES), F32)],
        10000,
        (part, g, r_a, info, meet, coef, hot, code),
    )
    r_b = lax.ppermute(pb, AXES, pairs_b)
    pairs = call(
        pair_kernel, shape(LANES, LANES, dtype=BF), [], 10000, (info, rows, meet, q1)
    )
    q, e = call(
        far_kernel,
        (traces, terms),
        scratch,
        10000,
        (g, q1, unit, r_b, info, rows, code, pairs, e1),
    )
    r_a = lax.ppermute(q, AXES, pairs_a)
    part = local(True, part, nb_v, ori_v, coef, dd, fld, e, ohs)
    return call(
        last_kernel,
        shape(VARS, NODES, EL),
        scratch + [pltpu.VMEM((VARS, NODES, EL), F32), pltpu.SemaphoreType.DMA((VARS,))],
        10000,
        (part, q, r_a, info, ohs, coef),
        out_hbm=True,
    )


def solution(mesh):
    sizes = tuple(mesh.shape[a] for a in AXES)
    in_specs = (P(None, None, AXES), P(AXES), P(), P(None, AXES), P(None, AXES))
    return jax.shard_map(
        functools.partial(per_device, sizes),
        mesh=mesh,
        in_specs=in_specs,
        out_specs=P(None, None, AXES),
        check_vma=False,
    )
```

```python
import functools

import jax
import jax.numpy as jnp
import numpy as np
from jax import lax
from jax.experimental import pallas as pl
from jax.experimental.pallas import tpu as pltpu
from jax.sharding import PartitionSpec as P

AXES = ("gx", "gy", "gz")
TIME_STEP = 0.03
LIFT = 6.0
VARS = 5
NODES = 64
EL = 256
LANES = 128
PITCH = 12
TABLE = 16 * PITCH
REMOTE = 32
FACES = 6
ROWS = VARS * NODES
BF = jnp.bfloat16
F32 = jnp.float32
I32 = jnp.int32


def gll_derivative():
    points = np.array([-1.0, -1.0 / np.sqrt(5.0), 1.0 / np.sqrt(5.0), 1.0])
    weights = np.array(
        [1.0 / np.prod([points[c] - points[p] for p in range(4) if p != c]) for c in range(4)]
    )
    matrix = np.zeros((4, 4))
    for row in range(4):
        for col in range(4):
            if row != col:
                matrix[row, col] = weights[col] / weights[row] / (points[row] - points[col])
        matrix[row, row] = -np.sum(matrix[row])
    return matrix


def node_derivatives():
    d, one = gll_derivative(), np.eye(4)
    parts = [
        np.kron(np.kron(d, one), one),
        np.kron(np.kron(one, d), one),
        np.kron(np.kron(one, one), d),
    ]
    return np.concatenate(parts, axis=1).astype(np.float32)


def iota(shape, dim):
    return lax.broadcasted_iota(I32, shape, dim)


def split(x):
    hi = x.astype(BF)
    return hi, (x - hi.astype(F32)).astype(BF)


def mm(a, b):
    return jnp.dot(a, b, preferred_element_type=F32)


def rows_at(lead, base, f, i=None):
    if f < 2:
        rows = pl.ds(base + 48 * f, 16)
    elif f < 4:
        rows = pl.ds(base + 12 * (f - 2) + 16 * i, 4)
    else:
        rows = pl.ds(base + 3 * (f - 4), 16, stride=4)
    return (rows, slice(None)) if lead is None else (lead, rows, slice(None))


def face_rows(ref, lead, v, f):
    if f in (2, 3):
        return jnp.concatenate([ref[rows_at(lead, v * NODES, f, i)] for i in range(4)], 0)
    return ref[rows_at(lead, v * NODES, f)]


def put_face_rows(across, lead, v, f, val):
    ref = across[f // 2]
    if f in (2, 3):
        for i in range(4):
            ref[rows_at(lead, v * NODES, f, i)] = val[4 * i : 4 * i + 4, :]
    else:
        ref[rows_at(lead, v * NODES, f)] = val


def rank_of(sizes):
    return (lax.axis_index("gx") * sizes[1] + lax.axis_index("gy")) * sizes[2] + lax.axis_index("gz")


def places(mask):
    count = mask.shape[0]
    upper = jnp.where(iota((EL, EL), 0) <= iota((EL, EL), 1), 1.0, 0.0).astype(BF)
    inclusive = mm(mask.astype(BF), upper)
    total = jnp.broadcast_to(inclusive[:, EL - 1 : EL], (count, LANES)).astype(BF)
    r, c = iota((count, count), 0), iota((count, count), 1)
    lower = jnp.where((c < r) & ((c >> 3) == (r >> 3)), 1.0, 0.0).astype(BF)
    offset = mm(lower, total)[:, 0:1]
    return jnp.where(mask > 0.5, inclusive + offset - 1.0, -1.0)


def listed(place, values):
    slot = iota((REMOTE, EL), 0).astype(F32)
    accs = [jnp.zeros((REMOTE, EL), F32) for _ in values]
    for f in range(FACES):
        hit = place[f : f + 1, :] == slot
        accs = [jnp.where(hit, x[f : f + 1, :], acc) for x, acc in zip(values, accs)]
    return [jnp.sum(acc, 1, keepdims=True) for acc in accs]


def send_kernel(sizes, start_hbm, old, nb, ori, s_a, s_b, rows_ref, col_ref, old_v, nb_v, ori_v, edge, mk, start, sem):
    n = sizes[0] * sizes[1] * sizes[2]
    copies = [
        pltpu.make_async_copy(nb, nb_v, sem.at[0]),
        pltpu.make_async_copy(ori, ori_v, sem.at[1]),
        pltpu.make_async_copy(start_hbm, start, sem.at[2]),
        pltpu.make_async_copy(old, old_v, sem.at[3]),
    ]
    for copy in copies:
        copy.start()
    d = rank_of(sizes)
    even = (d & 1) == 0
    up = jnp.where(d + 1 == n, 0, d + 1) * EL
    down = jnp.where(d == 0, n - 1, d - 1) * EL
    mk[...] = jnp.zeros((16, EL), F32)
    copies[0].wait()
    nb = nb_v[...]
    rel = [nb - jnp.where(even, up, down), nb - jnp.where(even, down, up)]
    for k in range(2):
        mk[8 * k : 8 * k + FACES, :] = jnp.where((rel[k] >= 0) & (rel[k] < EL), 1.0, 0.0)
    place = places(mk[...])
    copies[1].wait()
    face = iota((FACES, EL), 0)
    own = (face * EL + iota((FACES, EL), 1) + 2048 * ori_v[...]).astype(F32)
    lists = []
    for k in range(2):
        lists.append(listed(place[8 * k : 8 * k + 8, :], [((face ^ 1) * EL + rel[k]).astype(F32), own]))
    col = jnp.concatenate([lists[0][0], lists[1][0], lists[0][1], lists[1][1]], 0)
    wide = jnp.broadcast_to(col, (LANES, LANES))
    row = jnp.transpose(wide)[0:8, :]
    turn = jnp.floor(row * (1.0 / 2048.0))
    code = row - 2048.0 * turn
    rows_ref[0:8, :] = code
    rows_ref[8:16, :] = turn
    col_ref[...] = wide[64:128, :]
    s_a[ROWS : ROWS + 8, :] = code
    s_a[ROWS + 8 : ROWS + 16, :] = turn

    copies[2].wait()
    o = start[d] - d * EL
    edge[0:4, :] = jnp.broadcast_to(o, (4, LANES))
    edge[4:8, :] = jnp.broadcast_to(start[d + 1] - d * EL, (4, LANES))
    first = EL - o
    q, rot = first >> 7, first & 127
    keep = iota((NODES, LANES), 1) < LANES - rot
    back = (LANES - rot) & 127
    t0 = pl.ds(pl.multiple_of(q * LANES, LANES), LANES)
    t1 = pl.ds(pl.multiple_of(jnp.minimum(q + 1, 3) * LANES, LANES), LANES)
    for copy in copies[3:]:
        copy.wait()

    def put(to_up, to_down):
        for v in range(VARS):
            rows = slice(v * NODES, v * NODES + NODES)
            to_up[rows, :] = jnp.where(
                keep, pltpu.roll(old_v[v, :, t0], back, 1), pltpu.roll(old_v[v, :, t1], back, 1)
            )
            to_down[rows, :] = pltpu.roll(old_v[v, :, 0:LANES], o & 127, 1)

    @pl.when(even)
    def _():
        put(s_a, s_b)

    @pl.when(jnp.logical_not(even))
    def _():
        put(s_b, s_a)


def own_kernel(
    sizes, start_hbm, old, col_ref, d_hbm, size_hbm, own, ohs, dd, coef, d_v, size_v, start, sem
):
    copies = [
        pltpu.make_async_copy(start_hbm, start, sem.at[2]),
        pltpu.make_async_copy(d_hbm, d_v, sem.at[0]),
        pltpu.make_async_copy(size_hbm, size_v, sem.at[1]),
    ]
    for copy in copies:
        copy.start()
    d = rank_of(sizes)
    copies[0].wait()
    s = d * EL - start[d]
    q, rot = s >> 7, s & 127
    keep = iota((NODES, LANES), 1) < LANES - rot
    back = (LANES - rot) & 127
    for v in range(VARS):
        rows = slice(v * NODES, v * NODES + NODES)
        t = [
            pltpu.roll(
                old[v, :, pl.ds(pl.multiple_of(jnp.maximum(q + i, 0) * LANES, LANES), LANES)], back, 1
            )
            for i in range(3)
        ]
        own[0, rows, :] = jnp.where(keep, t[0], t[1])
        own[1, rows, :] = jnp.where(keep, t[1], t[2])
    code = col_ref[...].astype(I32)
    lane = iota((64, LANES), 1)
    for h in range(2):
        hit = jnp.where((code & 255) == lane + h * LANES, 1.0, 0.0).astype(BF)
        ohs[0:64, h * LANES : h * LANES + LANES] = hit
        ohs[64:128, h * LANES : h * LANES + LANES] = jnp.zeros((64, LANES), BF)
    for copy in copies[1:]:
        copy.wait()
    dd[...] = jnp.concatenate(split(d_v[...]), 0)
    coef[...] = (TIME_STEP * 2.0) / size_v[...]


def chosen(gs, face, v):
    acc = face_rows(gs, None, v, 0)
    for f in range(1, FACES):
        acc = jnp.where(face == f, face_rows(gs, None, v, f), acc)
    return acc


def requested(fld, hot, face, gs, g):
    both = jnp.concatenate([fld[0], fld[1]], 1)
    out = mm(jnp.concatenate(split(both), 0), hot)
    gs[...] = out[0:ROWS, :] + out[ROWS : 2 * ROWS, :]
    for v in range(VARS):
        g[16 * v : 16 * v + 16, :] = chosen(gs, face, v)


def join_kernel(
    sizes, own, r_a, r_b, c_b, rows_ref, edge, col_ref, fld, hot_ref, code_ref, info, meet, g, gs
):
    even = (rank_of(sizes) & 1) == 0
    lane = iota((NODES, LANES), 1)
    below = lane < edge[0:1, :]
    above = lane + LANES >= edge[4:5, :]
    for v in range(VARS):
        rows = slice(v * NODES, v * NODES + NODES)
        a, b = r_a[rows, :], r_b[rows, :]
        fld[0, rows, :] = jnp.where(below, jnp.where(even, b, a), own[0, rows, :])
        fld[1, rows, :] = jnp.where(above, jnp.where(even, a, b), own[1, rows, :])
    lane8 = iota((8, LANES), 1)
    code = jnp.where(
        lane8 < 32,
        r_a[ROWS : ROWS + 8, :],
        jnp.where(lane8 < 64, c_b[0:8, :], rows_ref[0:8, :]),
    ).astype(I32)
    code_ref[...] = code
    lane16 = iota((16, LANES), 1)
    info[...] = jnp.where(
        lane16 < 96, pltpu.roll(rows_ref[...], 64, 1), c_b[...]
    ).astype(I32)
    spot = jnp.broadcast_to(code[0:1, :] & 255, (EL, LANES))
    hot = jnp.where(spot == iota((EL, LANES), 0), 1.0, 0.0).astype(BF)
    hot_ref[...] = hot
    face = jnp.broadcast_to(code[0:1, :] >> 8, (16, LANES))
    requested(fld, hot, face, gs, g)
    same = (col_ref[...].astype(I32) & 255) == jnp.broadcast_to(code[0:1, :] & 255, (64, LANES))
    meet[0:64, :] = jnp.where(same, 1.0, 0.0).astype(BF)
    meet[64:128, :] = jnp.zeros((64, LANES), BF)


def flux_parts(u):
    inv = pl.reciprocal(u[0])
    speeds = [u[i] * inv for i in range(1, 4)]
    p = 0.4 * (u[4] - 0.5 * (u[1] * speeds[0] + u[2] * speeds[1] + u[3] * speeds[2]))
    enthalpy = u[4] + p
    stress = {}
    for a in range(3):
        for b in range(a, 3):
            t = u[1 + a] * speeds[b]
            stress[a, b] = stress[b, a] = split(t + p if a == b else t)
    out = [[split(u[1 + a]) for a in range(3)]]
    out += [[stress[a, b] for a in range(3)] for b in range(3)]
    out.append([split(enthalpy * speeds[a]) for a in range(3)])
    return out


def directed(u, axis_is):
    inv = pl.reciprocal(u[0])
    p = 0.4 * u[4] - 0.2 * ((u[1] * u[1] + u[2] * u[2] + u[3] * u[3]) * inv)
    mom = jnp.where(axis_is[0], u[1], jnp.where(axis_is[1], u[2], u[3]))
    s = mom * inv
    t = 1.4 * (p * inv)
    return p, mom, s, jnp.abs(s) + t * lax.rsqrt(jnp.maximum(t, 1.2e-38))


def correction(inner, outer, axis_is, sign_scale, scale):
    pi, mi, si, ci = directed(inner, axis_is)
    po, mo, so, co = directed(outer, axis_is)
    lam = scale * jnp.maximum(ci, co)
    dp = po - pi
    along = (axis_is[0], axis_is[1], jnp.logical_not(axis_is[0] | axis_is[1]))
    flux = [mo - mi]
    flux += [
        (outer[i] * so - inner[i] * si) + jnp.where(along[i - 1], dp, 0.0) for i in range(1, 4)
    ]
    flux += [(outer[4] + po) * so - (inner[4] + pi) * si]
    return [sign_scale * flux[v] - lam * (outer[v] - inner[v]) for v in range(VARS)]


def turned(x, b0, b1, b2):
    x = [jnp.where(b1, x[4 * (3 - p) + q], x[4 * p + q]) for p in range(4) for q in range(4)]
    x = [jnp.where(b2, x[4 * p + 3 - q], x[4 * p + q]) for p in range(4) for q in range(4)]
    return [jnp.where(b0, x[4 * t + s], x[4 * s + t]) for s in range(4) for t in range(4)]


def local_kernel(sizes, last, fld, nb_ref, ori_ref, coef_ref, dd_ref, *rest):
    if last:
        old_fld, e, ohs, part, acc, ax, ay, az, xs, xg, xq, xo, xc, it, first = rest

        def put(h, v, new):
            first[h, v * NODES : v * NODES + NODES, :] = new

        added(fld, mm(e[...], ohs[...]), coef_ref, LIFT, put)
        fld = first
    else:
        part, acc, ax, ay, az, xs, xg, xq, xo, xc, it = rest
    for ref in (ax, ay, az):
        ref[...] = jnp.zeros((2, ROWS, LANES), F32)
    d = rank_of(sizes)
    dd = dd_ref[...]
    dh = dd[0:NODES, :]
    pieces = [[[], []] for _ in range(VARS)]
    for h in range(2):
        u = [fld[h, v * NODES : v * NODES + NODES, :] for v in range(VARS)]
        fl = flux_parts(u)
        for v in range(VARS):
            hl = fl[v]
            pieces[v][0].append(jnp.concatenate([x[0] for x in hl], 0))
            pieces[v][1].append(jnp.concatenate([x[1] for x in hl], 0))
    for v in range(VARS):
        hi = mm(dd, jnp.concatenate(pieces[v][0], 1))
        lo = mm(dh, jnp.concatenate(pieces[v][1], 1))
        vol = hi[0:NODES, :] + hi[NODES : 2 * NODES, :] + lo
        for h in range(2):
            acc[h, v * NODES : v * NODES + NODES, :] = vol[:, h * LANES : h * LANES + LANES]
    for v in range(VARS):
        for f in range(FACES):
            for h in range(2):
                t = face_rows(fld, h, v, f)
                b = v * TABLE
                xs[pl.ds(b + 2 * f + h, 16, stride=PITCH), :] = t
                xg[pl.ds(b + 2 * (f ^ 1) + h, 16, stride=PITCH), :] = t
                xq[pl.ds(b + 2 * (f ^ 1) + 1 - h, 16, stride=PITCH), :] = t
    it[...] = jnp.zeros((32, LANES), I32)
    for h in range(2):
        it[pl.ds(h, FACES, stride=2), :] = nb_ref[:, h * LANES : h * LANES + LANES]
        it[pl.ds(16 + h, FACES, stride=2), :] = ori_ref[:, h * LANES : h * LANES + LANES]
    t = it[0:16, :] - d * EL
    turn = it[16:32, :]
    row = iota((16, LANES), 0)
    local = (t >= 0) & (t < EL) & (row < 12)
    same = ((t >> 7) & 1) == (row & 1)
    idx = t & 127
    b0, b1, b2 = (turn & 1) != 0, (turn & 2) != 0, (turn & 4) != 0
    for v in range(VARS):
        got = []
        for m in range(16):
            rows = pl.ds(v * TABLE + m * PITCH, 16)
            ga = jnp.take_along_axis(xg[rows, :], idx, axis=1)
            gb = jnp.take_along_axis(xq[rows, :], idx, axis=1)
            got.append(jnp.where(same, ga, gb))
        for m, x in enumerate(turned(got, b0, b1, b2)):
            xo[pl.ds(v * TABLE + m * PITCH, 12), :] = x[0:12, :]
    axis_is = (row < 4, (row >= 4) & (row < 8))
    sign_scale = jnp.where((row & 2) != 0, 0.5 * LIFT, -0.5 * LIFT)
    for m in range(16):
        rows = [pl.ds(v * TABLE + m * PITCH, 16) for v in range(VARS)]
        inner, outer = [xs[r, :] for r in rows], [xo[r, :] for r in rows]
        cor = correction(inner, outer, axis_is, sign_scale, 0.5 * LIFT)
        for v in range(VARS):
            val = jnp.where(local, cor[v], 0.0)
            xc[pl.ds(v * TABLE + m * PITCH, 12), :] = val[0:12, :]
    for v in range(VARS):
        for f in range(FACES):
            for h in range(2):
                put_face_rows(
                    (ax, ay, az), h, v, f, xc[pl.ds(v * TABLE + 2 * f + h, 16, stride=PITCH), :]
                )
    for h in range(2):
        coef = coef_ref[0:1, h * LANES : h * LANES + LANES]
        for v in range(VARS):
            rows = slice(v * NODES, v * NODES + NODES)
            rate = acc[h, rows, :] + ax[h, rows, :] + ay[h, rows, :] + az[h, rows, :]
            new = fld[h, rows, :] - coef * rate
            if last:
                new = 0.5 * old_fld[h, rows, :] + 0.5 * new
            part[h, rows, :] = new


def face_terms(inner, outer, info, live, ro, y, ex, ey, ez):
    for v in range(VARS):
        ro[17 * v : 17 * v + 16, :] = outer[16 * v : 16 * v + 16, :]
    turn = info[8:16, :]
    x = [ro[pl.ds(m, 8, stride=17), :] for m in range(16)]
    for m, val in enumerate(turned(x, (turn & 1) != 0, (turn & 2) != 0, (turn & 4) != 0)):
        y[9 * m : 9 * m + 8, :] = val
    face = jnp.where(live, jnp.broadcast_to(info[0:1, :], (16, LANES)) >> 8, -1)
    axis_is = (face < 2, (face >= 2) & (face < 4))
    half_sign = jnp.where((face & 1) != 0, 0.5, -0.5)
    behind = [y[pl.ds(v, 16, stride=9), :] for v in range(VARS)]
    here = [inner[16 * v : 16 * v + 16, :] for v in range(VARS)]
    cor = correction(here, behind, axis_is, half_sign, 0.5)
    for ref in (ex, ey, ez):
        ref[...] = jnp.zeros((ROWS, LANES), F32)
    for v in range(VARS):
        for f in range(FACES):
            put_face_rows((ex, ey, ez), None, v, f, jnp.where(face == f, cor[v], 0.0))
    return jnp.concatenate(split(ex[...] + ey[...] + ez[...]), 0)


def added(part, spread, coef_ref, scale, put):
    for h in range(2):
        lanes = slice(h * LANES, h * LANES + LANES)
        coef = scale * coef_ref[0:1, lanes]
        for v in range(VARS):
            rows = slice(v * NODES, v * NODES + NODES)
            low = slice(ROWS + v * NODES, ROWS + v * NODES + NODES)
            put(h, v, part[h, rows, :] - coef * (spread[rows, lanes] + spread[low, lanes]))


def near_kernel(
    part, g, r_a, info, meet, coef_ref, hot_ref, code_ref, parts, q, pb, unit, ro, y, ex, ey, ez, gs, g1
):
    hot = hot_ref[...]
    asked = jnp.broadcast_to(code_ref[0:1, :] >> 8, (16, LANES))
    requested(part, hot, asked, gs, g1)
    ch, cl = split(jnp.broadcast_to(LIFT * coef_ref[0:1, :], (16, EL)))
    coef = mm(ch, hot) + mm(cl, hot)
    lane = iota((16, LANES), 1)
    terms = face_terms(pltpu.roll(g[...], 64, 1), r_a[...], info, lane < 32, ro, y, ex, ey, ez)
    parts[...] = terms
    change = mm(terms, meet[...])
    ex[...] = change[0:ROWS, :] + change[ROWS : 2 * ROWS, :]
    for v in range(VARS):
        rows = slice(16 * v, 16 * v + 16)
        new = g1[rows, :] - coef * chosen(ex, asked, v)
        q[rows, :] = new
        sent = jnp.where((lane >= 64) & (lane < 96), pltpu.roll(coef, 32, 1), g[rows, :])
        pb[rows, :] = jnp.where(lane < 32, pltpu.roll(new, 96, 1), sent)
    unit[...] = coef


def pair_kernel(info, rows_ref, meet, after, pairs):
    theirs = jnp.transpose(jnp.broadcast_to(info[0:1, :].astype(F32), (LANES, LANES))).astype(I32)
    mine = jnp.broadcast_to(rows_ref[0:1, :].astype(I32), (LANES, LANES))
    row, lane = iota((LANES, LANES), 0), iota((LANES, LANES), 1)
    to_b = (lane >= 32) & (lane < 64)
    on = ((theirs & 255) == (mine & 255)) & (row >= 96) & to_b
    kept = jnp.where(to_b, 0.0, meet[...].astype(F32))
    pairs[...] = jnp.where(on, 1.0, kept).astype(BF)


def far_kernel(g, q1, unit, r_b, info, rows_ref, code_ref, pairs, e1, q, e, ro, y, ex, ey, ez):
    lane = iota((80, LANES), 1)
    mine = pltpu.roll(g[...], 64, 1)
    got = r_b[...]
    lane16 = iota((16, LANES), 1)
    to_b = (lane16 >= 32) & (lane16 < 64)
    inner, outer = jnp.where(lane < 64, mine, got), jnp.where(lane < 64, got, mine)
    terms = face_terms(inner, outer, info, to_b | (lane16 >= 96), ro, y, ex, ey, ez)
    e[...] = e1[...] + terms
    change = mm(terms, pairs[...])
    ex[...] = change[0:ROWS, :] + change[ROWS : 2 * ROWS, :]
    code = jnp.where(to_b[0:1, :], rows_ref[0:1, :].astype(I32), code_ref[0:1, :])
    face = jnp.broadcast_to(code >> 8, (16, LANES))
    coef = jnp.where(to_b, pltpu.roll(r_b[0:16, :], 96, 1), unit[...])
    for v in range(VARS):
        rows = slice(16 * v, 16 * v + 16)
        base = jnp.where(to_b, pltpu.roll(r_b[rows, :], 32, 1), q1[rows, :])
        q[rows, :] = base - coef * chosen(ex, face, v)


def last_kernel(part, q, r_a, info, ohs, coef_ref, out_hbm, ro, y, ex, ey, ez, out, sem):
    lane = iota((80, LANES), 1)
    outer = jnp.where(lane < 32, r_a[...], q[...])
    live = iota((16, LANES), 1) < 64
    parts = face_terms(pltpu.roll(q[...], 64, 1), outer, info, live, ro, y, ex, ey, ez)
    spread = mm(parts, ohs[...])
    copies = []
    for v in range(VARS):
        for h in range(2):
            lanes = slice(h * LANES, h * LANES + LANES)
            rows = slice(v * NODES, v * NODES + NODES)
            low = slice(ROWS + v * NODES, ROWS + v * NODES + NODES)
            coef = (0.5 * LIFT) * coef_ref[0:1, lanes]
            out[v, :, lanes] = part[h, rows, :] - coef * (spread[rows, lanes] + spread[low, lanes])
        copies.append(pltpu.make_async_copy(out.at[v], out_hbm.at[v], sem.at[v]))
        copies[v].start()
    for copy in copies:
        copy.wait()


def call(body, out_shape, scratch, cost, args, hbm=(), out_hbm=False):
    spec = pl.BlockSpec(memory_space=pltpu.VMEM)
    specs = []
    for i, a in enumerate(args):
        if i in hbm:
            specs.append(pl.BlockSpec(memory_space=pltpu.HBM))
        elif a.dtype == I32 and a.ndim == 1:
            specs.append(pl.BlockSpec(memory_space=pltpu.SMEM))
        else:
            specs.append(spec)
    return pl.pallas_call(
        body,
        out_shape=out_shape,
        in_specs=specs,
        out_specs=pl.BlockSpec(memory_space=pltpu.HBM)
        if out_hbm
        else jax.tree.map(lambda _: spec, out_shape),
        scratch_shapes=scratch,
        cost_estimate=pl.CostEstimate(flops=cost, bytes_accessed=cost, transcendentals=0),
        compiler_params=pltpu.CompilerParams(vmem_limit_bytes=32 * 1024 * 1024),
    )(*[pltpu.with_memory_space_constraint(a, pltpu.HBM) if i in hbm else a for i, a in enumerate(args)])


def shape(*dims, dtype=F32):
    return jax.ShapeDtypeStruct(dims, dtype)


def per_device(sizes, old_state, element_size, old_start, neighbour, orientation):
    n = sizes[0] * sizes[1] * sizes[2]
    pairs_a = [(i, i ^ 1) for i in range(n)]
    pairs_b = [(i, (i + 1) % n if i % 2 else (i - 1) % n) for i in range(n)]

    size = element_size.reshape(1, EL)
    deriv = jnp.asarray(node_derivatives())
    s_a, s_b, rows, col, old_v, nb_v, ori_v, edge = call(
        functools.partial(send_kernel, sizes),
        (
            shape(ROWS + 16, LANES),
            shape(ROWS, LANES),
            shape(16, LANES),
            shape(64, LANES),
            shape(*old_state.shape),
            shape(FACES, EL, dtype=I32),
            shape(FACES, EL, dtype=I32),
            shape(8, LANES, dtype=I32),
        ),
        [
            pltpu.VMEM((16, EL), F32),
            pltpu.SMEM(old_start.shape, I32),
            pltpu.SemaphoreType.DMA((4,)),
        ],
        10000,
        (old_start, old_state, neighbour, orientation),
        hbm=(0, 1, 2, 3),
    )
    r_a = lax.ppermute(s_a, AXES, pairs_a)
    c_b = lax.ppermute(rows, AXES, pairs_b)
    r_b = lax.ppermute(s_b, AXES, pairs_b[1:-1])
    own, ohs, dd, coef = call(
        functools.partial(own_kernel, sizes),
        (
            shape(2, ROWS, LANES),
            shape(LANES, EL, dtype=BF),
            shape(2 * NODES, 3 * NODES, dtype=BF),
            shape(1, EL),
        ),
        [
            pltpu.VMEM((NODES, 3 * NODES), F32),
            pltpu.VMEM((1, EL), F32),
            pltpu.SMEM(old_start.shape, I32),
            pltpu.SemaphoreType.DMA((3,)),
        ],
        10000,
        (old_start, old_v, col, deriv, size),
        hbm=(0, 3, 4),
    )
    table = pltpu.VMEM((ROWS, LANES), F32)
    square = pltpu.VMEM((LANES + 24, LANES), F32)
    traces = shape(80, LANES)
    state = shape(2, ROWS, LANES)
    fld, hot, code, info, meet, g = call(
        functools.partial(join_kernel, sizes),
        (
            state,
            shape(EL, LANES, dtype=BF),
            shape(8, LANES, dtype=I32),
            shape(16, LANES, dtype=I32),
            shape(LANES, LANES, dtype=BF),
            traces,
        ),
        [table],
        10000,
        (own, r_a, r_b, c_b, rows, edge, col),
    )

    def local(last, *args):
        faces = pltpu.VMEM((VARS * TABLE + 8, LANES), F32)
        both = pltpu.VMEM((2, ROWS, LANES), F32)
        return call(
            functools.partial(local_kernel, sizes, last),
            state,
            [both] * 4 + [faces] * 5 + [pltpu.VMEM((32, LANES), I32)] + ([both] if last else []),
            20000,
            args,
        )

    r_a = lax.ppermute(g, AXES, pairs_a)
    part = local(False, fld, nb_v, ori_v, coef, dd)
    terms = shape(2 * ROWS, LANES, dtype=BF)
    scratch = [square, square, table, table, table]
    e1, q1, pb, unit = call(
        near_kernel,
        (terms, traces, traces, shape(16, LANES)),
        scratch + [table, pltpu.VMEM((80, LANES), F32)],
        10000,
        (part, g, r_a, info, meet, coef, hot, code),
    )
    r_b = lax.ppermute(pb, AXES, pairs_b)
    pairs = call(
        pair_kernel, shape(LANES, LANES, dtype=BF), [], 10000, (info, rows, meet, q1)
    )
    q, e = call(
        far_kernel,
        (traces, terms),
        scratch,
        10000,
        (g, q1, unit, r_b, info, rows, code, pairs, e1),
    )
    r_a = lax.ppermute(q, AXES, pairs_a)
    part = local(True, part, nb_v, ori_v, coef, dd, fld, e, ohs)
    return call(
        last_kernel,
        shape(VARS, NODES, EL),
        scratch + [pltpu.VMEM((VARS, NODES, EL), F32), pltpu.SemaphoreType.DMA((VARS,))],
        10000,
        (part, q, r_a, info, ohs, coef),
        out_hbm=True,
    )


def solution(mesh):
    sizes = tuple(mesh.shape[a] for a in AXES)
    in_specs = (P(None, None, AXES), P(AXES), P(), P(None, AXES), P(None, AXES))
    return jax.shard_map(
        functools.partial(per_device, sizes),
        mesh=mesh,
        in_specs=in_specs,
        out_specs=P(None, None, AXES),
        check_vma=False,
    )
```

```python
import functools

import jax
import jax.numpy as jnp
import numpy as np
from jax import lax
from jax.experimental import pallas as pl
from jax.experimental.pallas import tpu as pltpu
from jax.sharding import PartitionSpec as P

AXES = ("gx", "gy", "gz")
TIME_STEP = 0.03
LIFT = 6.0
VARS = 5
NODES = 64
EL = 256
LANES = 128
PITCH = 12
TABLE = 16 * PITCH
REMOTE = 32
FACES = 6
ROWS = VARS * NODES
BF = jnp.bfloat16
F32 = jnp.float32
I32 = jnp.int32


def gll_derivative():
    points = np.array([-1.0, -1.0 / np.sqrt(5.0), 1.0 / np.sqrt(5.0), 1.0])
    weights = np.array(
        [1.0 / np.prod([points[c] - points[p] for p in range(4) if p != c]) for c in range(4)]
    )
    matrix = np.zeros((4, 4))
    for row in range(4):
        for col in range(4):
            if row != col:
                matrix[row, col] = weights[col] / weights[row] / (points[row] - points[col])
        matrix[row, row] = -np.sum(matrix[row])
    return matrix


def node_derivatives():
    d, one = gll_derivative(), np.eye(4)
    parts = [
        np.kron(np.kron(d, one), one),
        np.kron(np.kron(one, d), one),
        np.kron(np.kron(one, one), d),
    ]
    return np.concatenate(parts, axis=1).astype(np.float32)


def iota(shape, dim):
    return lax.broadcasted_iota(I32, shape, dim)


def split(x):
    hi = x.astype(BF)
    return hi, (x - hi.astype(F32)).astype(BF)


def mm(a, b):
    return jnp.dot(a, b, preferred_element_type=F32)


def rows_at(lead, base, f, i=None):
    if f < 2:
        rows = pl.ds(base + 48 * f, 16)
    elif f < 4:
        rows = pl.ds(base + 12 * (f - 2) + 16 * i, 4)
    else:
        rows = pl.ds(base + 3 * (f - 4), 16, stride=4)
    return (rows, slice(None)) if lead is None else (lead, rows, slice(None))


def face_rows(ref, lead, v, f):
    if f in (2, 3):
        return jnp.concatenate([ref[rows_at(lead, v * NODES, f, i)] for i in range(4)], 0)
    return ref[rows_at(lead, v * NODES, f)]


def put_face_rows(across, lead, v, f, val):
    ref = across[f // 2]
    if f in (2, 3):
        for i in range(4):
            ref[rows_at(lead, v * NODES, f, i)] = val[4 * i : 4 * i + 4, :]
    else:
        ref[rows_at(lead, v * NODES, f)] = val


def rank_of(sizes):
    return (lax.axis_index("gx") * sizes[1] + lax.axis_index("gy")) * sizes[2] + lax.axis_index("gz")


def triangles(count):
    upper = jnp.where(iota((EL, EL), 0) <= iota((EL, EL), 1), 1.0, 0.0).astype(BF)
    r, c = iota((count, count), 0), iota((count, count), 1)
    lower = jnp.where((c < r) & ((c >> 3) == (r >> 3)), 1.0, 0.0).astype(BF)
    return upper, lower


def places(mask, upper, lower):
    inclusive = mm(mask.astype(BF), upper)
    total = jnp.sum(mask, 1, keepdims=True)
    total = jnp.broadcast_to(total, (mask.shape[0], LANES)).astype(BF)
    offset = mm(lower, total)[:, 0:1]
    return jnp.where(mask > 0.5, inclusive + offset - 1.0, -1.0)


def listed(place, values):
    slot = iota((REMOTE, EL), 0).astype(F32)
    accs = [jnp.zeros((REMOTE, EL), F32) for _ in values]
    for f in range(FACES):
        hit = place[f : f + 1, :] == slot
        accs = [jnp.where(hit, x[f : f + 1, :], acc) for x, acc in zip(values, accs)]
    return [jnp.sum(acc, 1, keepdims=True) for acc in accs]


def send_kernel(sizes, start_hbm, old, nb, ori, s_a, s_b, rows_ref, col_ref, old_v, nb_v, ori_v, edge, mk, start, sem):
    n = sizes[0] * sizes[1] * sizes[2]
    copies = [
        pltpu.make_async_copy(nb, nb_v, sem.at[0]),
        pltpu.make_async_copy(ori, ori_v, sem.at[1]),
        pltpu.make_async_copy(start_hbm, start, sem.at[2]),
        pltpu.make_async_copy(old, old_v, sem.at[3]),
    ]
    for copy in copies:
        copy.start()
    d = rank_of(sizes)
    even = (d & 1) == 0
    up = jnp.where(d + 1 == n, 0, d + 1) * EL
    down = jnp.where(d == 0, n - 1, d - 1) * EL
    mk[...] = jnp.zeros((16, EL), F32)
    upper, lower = triangles(16)
    copies[0].wait()
    nb = nb_v[...]
    rel = [nb - jnp.where(even, up, down), nb - jnp.where(even, down, up)]
    for k in range(2):
        mk[8 * k : 8 * k + FACES, :] = jnp.where((rel[k] >= 0) & (rel[k] < EL), 1.0, 0.0)
    place = places(mk[...], upper, lower)
    copies[1].wait()
    face = iota((FACES, EL), 0)
    own = (face * EL + iota((FACES, EL), 1) + 2048 * ori_v[...]).astype(F32)
    lists = []
    for k in range(2):
        lists.append(listed(place[8 * k : 8 * k + 8, :], [((face ^ 1) * EL + rel[k]).astype(F32), own]))
    col = jnp.concatenate([lists[0][0], lists[1][0], lists[0][1], lists[1][1]], 0)
    wide = jnp.broadcast_to(col, (LANES, LANES))
    row = jnp.transpose(wide)[0:8, :]
    turn = jnp.floor(row * (1.0 / 2048.0))
    code = row - 2048.0 * turn
    rows_ref[0:8, :] = code
    rows_ref[8:16, :] = turn
    col_ref[...] = wide[64:128, :]
    s_a[ROWS : ROWS + 8, :] = code
    s_a[ROWS + 8 : ROWS + 16, :] = turn

    copies[2].wait()
    o = start[d] - d * EL
    edge[0:4, :] = jnp.broadcast_to(o, (4, LANES))
    edge[4:8, :] = jnp.broadcast_to(start[d + 1] - d * EL, (4, LANES))
    first = EL - o
    q, rot = first >> 7, first & 127
    keep = iota((NODES, LANES), 1) < LANES - rot
    back = (LANES - rot) & 127
    t0 = pl.ds(pl.multiple_of(q * LANES, LANES), LANES)
    t1 = pl.ds(pl.multiple_of(jnp.minimum(q + 1, 3) * LANES, LANES), LANES)
    for copy in copies[3:]:
        copy.wait()

    def put(to_up, to_down):
        for v in range(VARS):
            rows = slice(v * NODES, v * NODES + NODES)
            to_up[rows, :] = jnp.where(
                keep, pltpu.roll(old_v[v, :, t0], back, 1), pltpu.roll(old_v[v, :, t1], back, 1)
            )
            to_down[rows, :] = pltpu.roll(old_v[v, :, 0:LANES], o & 127, 1)

    @pl.when(even)
    def _():
        put(s_a, s_b)

    @pl.when(jnp.logical_not(even))
    def _():
        put(s_b, s_a)


def own_kernel(
    sizes, start_hbm, old, col_ref, d_hbm, size_hbm, own, ohs, dd, coef, d_v, size_v, start, sem
):
    copies = [
        pltpu.make_async_copy(start_hbm, start, sem.at[2]),
        pltpu.make_async_copy(d_hbm, d_v, sem.at[0]),
        pltpu.make_async_copy(size_hbm, size_v, sem.at[1]),
    ]
    for copy in copies:
        copy.start()
    d = rank_of(sizes)
    copies[0].wait()
    s = d * EL - start[d]
    q, rot = s >> 7, s & 127
    keep = iota((NODES, LANES), 1) < LANES - rot
    back = (LANES - rot) & 127
    for v in range(VARS):
        rows = slice(v * NODES, v * NODES + NODES)
        t = [
            pltpu.roll(
                old[v, :, pl.ds(pl.multiple_of(jnp.maximum(q + i, 0) * LANES, LANES), LANES)], back, 1
            )
            for i in range(3)
        ]
        own[0, rows, :] = jnp.where(keep, t[0], t[1])
        own[1, rows, :] = jnp.where(keep, t[1], t[2])
    code = col_ref[...].astype(I32)
    lane = iota((64, LANES), 1)
    for h in range(2):
        hit = jnp.where((code & 255) == lane + h * LANES, 1.0, 0.0).astype(BF)
        ohs[0:64, h * LANES : h * LANES + LANES] = hit
        ohs[64:128, h * LANES : h * LANES + LANES] = jnp.zeros((64, LANES), BF)
    for copy in copies[1:]:
        copy.wait()
    dd[...] = jnp.concatenate(split(d_v[...]), 0)
    coef[...] = (TIME_STEP * 2.0) / size_v[...]


def chosen(gs, face, v):
    acc = face_rows(gs, None, v, 0)
    for f in range(1, FACES):
        acc = jnp.where(face == f, face_rows(gs, None, v, f), acc)
    return acc


def requested(fld, hot, face, gs, g):
    both = jnp.concatenate([fld[0], fld[1]], 1)
    out = mm(jnp.concatenate(split(both), 0), hot)
    gs[...] = out[0:ROWS, :] + out[ROWS : 2 * ROWS, :]
    for v in range(VARS):
        g[16 * v : 16 * v + 16, :] = chosen(gs, face, v)


def join_kernel(
    sizes, own, r_a, r_b, c_b, rows_ref, edge, col_ref, fld, hot_ref, code_ref, info, meet, g, gs
):
    even = (rank_of(sizes) & 1) == 0
    lane = iota((NODES, LANES), 1)
    below = lane < edge[0:1, :]
    above = lane + LANES >= edge[4:5, :]
    for v in range(VARS):
        rows = slice(v * NODES, v * NODES + NODES)
        a, b = r_a[rows, :], r_b[rows, :]
        fld[0, rows, :] = jnp.where(below, jnp.where(even, b, a), own[0, rows, :])
        fld[1, rows, :] = jnp.where(above, jnp.where(even, a, b), own[1, rows, :])
    lane8 = iota((8, LANES), 1)
    code = jnp.where(
        lane8 < 32,
        r_a[ROWS : ROWS + 8, :],
        jnp.where(lane8 < 64, c_b[0:8, :], rows_ref[0:8, :]),
    ).astype(I32)
    code_ref[...] = code
    lane16 = iota((16, LANES), 1)
    info[...] = jnp.where(
        lane16 < 96, pltpu.roll(rows_ref[...], 64, 1), c_b[...]
    ).astype(I32)
    spot = jnp.broadcast_to(code[0:1, :] & 255, (EL, LANES))
    hot = jnp.where(spot == iota((EL, LANES), 0), 1.0, 0.0).astype(BF)
    hot_ref[...] = hot
    face = jnp.broadcast_to(code[0:1, :] >> 8, (16, LANES))
    requested(fld, hot, face, gs, g)
    same = (col_ref[...].astype(I32) & 255) == jnp.broadcast_to(code[0:1, :] & 255, (64, LANES))
    meet[0:64, :] = jnp.where(same, 1.0, 0.0).astype(BF)
    meet[64:128, :] = jnp.zeros((64, LANES), BF)


def flux_parts(u):
    inv = pl.reciprocal(u[0])
    speeds = [u[i] * inv for i in range(1, 4)]
    p = 0.4 * (u[4] - 0.5 * (u[1] * speeds[0] + u[2] * speeds[1] + u[3] * speeds[2]))
    enthalpy = u[4] + p
    stress = {}
    for a in range(3):
        for b in range(a, 3):
            t = u[1 + a] * speeds[b]
            stress[a, b] = stress[b, a] = split(t + p if a == b else t)
    out = [[split(u[1 + a]) for a in range(3)]]
    out += [[stress[a, b] for a in range(3)] for b in range(3)]
    out.append([split(enthalpy * speeds[a]) for a in range(3)])
    return out


def directed(u, axis_is):
    inv = pl.reciprocal(u[0])
    p = 0.4 * u[4] - 0.2 * ((u[1] * u[1] + u[2] * u[2] + u[3] * u[3]) * inv)
    mom = jnp.where(axis_is[0], u[1], jnp.where(axis_is[1], u[2], u[3]))
    s = mom * inv
    t = 1.4 * (p * inv)
    return p, mom, s, jnp.abs(s) + t * lax.rsqrt(jnp.maximum(t, 1.2e-38))


def correction(inner, outer, axis_is, sign_scale, scale):
    pi, mi, si, ci = directed(inner, axis_is)
    po, mo, so, co = directed(outer, axis_is)
    lam = scale * jnp.maximum(ci, co)
    dp = po - pi
    along = (axis_is[0], axis_is[1], jnp.logical_not(axis_is[0] | axis_is[1]))
    flux = [mo - mi]
    flux += [
        (outer[i] * so - inner[i] * si) + jnp.where(along[i - 1], dp, 0.0) for i in range(1, 4)
    ]
    flux += [(outer[4] + po) * so - (inner[4] + pi) * si]
    return [sign_scale * flux[v] - lam * (outer[v] - inner[v]) for v in range(VARS)]


def turned(x, b0, b1, b2):
    x = [jnp.where(b1, x[4 * (3 - p) + q], x[4 * p + q]) for p in range(4) for q in range(4)]
    x = [jnp.where(b2, x[4 * p + 3 - q], x[4 * p + q]) for p in range(4) for q in range(4)]
    return [jnp.where(b0, x[4 * t + s], x[4 * s + t]) for s in range(4) for t in range(4)]


def local_kernel(sizes, last, fld, nb_ref, ori_ref, coef_ref, dd_ref, *rest):
    if last:
        old_fld, e, ohs, part, acc, ax, ay, az, xs, xg, xq, xo, xc, it, first = rest

        def put(h, v, new):
            first[h, v * NODES : v * NODES + NODES, :] = new

        added(fld, mm(e[...], ohs[...]), coef_ref, LIFT, put)
        fld = first
    else:
        part, acc, ax, ay, az, xs, xg, xq, xo, xc, it = rest
    for ref in (ax, ay, az):
        ref[...] = jnp.zeros((2, ROWS, LANES), F32)
    d = rank_of(sizes)
    dd = dd_ref[...]
    dh = dd[0:NODES, :]
    pieces = [[[], []] for _ in range(VARS)]
    for h in range(2):
        u = [fld[h, v * NODES : v * NODES + NODES, :] for v in range(VARS)]
        fl = flux_parts(u)
        for v in range(VARS):
            hl = fl[v]
            pieces[v][0].append(jnp.concatenate([x[0] for x in hl], 0))
            pieces[v][1].append(jnp.concatenate([x[1] for x in hl], 0))
    for v in range(VARS):
        hi = mm(dd, jnp.concatenate(pieces[v][0], 1))
        lo = mm(dh, jnp.concatenate(pieces[v][1], 1))
        vol = hi[0:NODES, :] + hi[NODES : 2 * NODES, :] + lo
        for h in range(2):
            acc[h, v * NODES : v * NODES + NODES, :] = vol[:, h * LANES : h * LANES + LANES]
    for v in range(VARS):
        for f in range(FACES):
            for h in range(2):
                t = face_rows(fld, h, v, f)
                b = v * TABLE
                xs[pl.ds(b + 2 * f + h, 16, stride=PITCH), :] = t
                xg[pl.ds(b + 2 * (f ^ 1) + h, 16, stride=PITCH), :] = t
                xq[pl.ds(b + 2 * (f ^ 1) + 1 - h, 16, stride=PITCH), :] = t
    it[...] = jnp.zeros((32, LANES), I32)
    for h in range(2):
        it[pl.ds(h, FACES, stride=2), :] = nb_ref[:, h * LANES : h * LANES + LANES]
        it[pl.ds(16 + h, FACES, stride=2), :] = ori_ref[:, h * LANES : h * LANES + LANES]
    t = it[0:16, :] - d * EL
    turn = it[16:32, :]
    row = iota((16, LANES), 0)
    local = (t >= 0) & (t < EL) & (row < 12)
    same = ((t >> 7) & 1) == (row & 1)
    idx = t & 127
    b0, b1, b2 = (turn & 1) != 0, (turn & 2) != 0, (turn & 4) != 0
    for v in range(VARS):
        got = []
        for m in range(16):
            rows = pl.ds(v * TABLE + m * PITCH, 16)
            ga = jnp.take_along_axis(xg[rows, :], idx, axis=1)
            gb = jnp.take_along_axis(xq[rows, :], idx, axis=1)
            got.append(jnp.where(same, ga, gb))
        for m, x in enumerate(turned(got, b0, b1, b2)):
            xo[pl.ds(v * TABLE + m * PITCH, 12), :] = x[0:12, :]
    axis_is = (row < 4, (row >= 4) & (row < 8))
    sign_scale = jnp.where((row & 2) != 0, 0.5 * LIFT, -0.5 * LIFT)
    for m in range(16):
        rows = [pl.ds(v * TABLE + m * PITCH, 16) for v in range(VARS)]
        inner, outer = [xs[r, :] for r in rows], [xo[r, :] for r in rows]
        cor = correction(inner, outer, axis_is, sign_scale, 0.5 * LIFT)
        for v in range(VARS):
            val = jnp.where(local, cor[v], 0.0)
            xc[pl.ds(v * TABLE + m * PITCH, 12), :] = val[0:12, :]
    for v in range(VARS):
        for f in range(FACES):
            for h in range(2):
                put_face_rows(
                    (ax, ay, az), h, v, f, xc[pl.ds(v * TABLE + 2 * f + h, 16, stride=PITCH), :]
                )
    for h in range(2):
        coef = coef_ref[0:1, h * LANES : h * LANES + LANES]
        for v in range(VARS):
            rows = slice(v * NODES, v * NODES + NODES)
            rate = acc[h, rows, :] + ax[h, rows, :] + ay[h, rows, :] + az[h, rows, :]
            new = fld[h, rows, :] - coef * rate
            if last:
                new = 0.5 * old_fld[h, rows, :] + 0.5 * new
            part[h, rows, :] = new


def face_terms(inner, outer, info, live, ro, y, ex, ey, ez):
    for v in range(VARS):
        ro[17 * v : 17 * v + 16, :] = outer[16 * v : 16 * v + 16, :]
    turn = info[8:16, :]
    x = [ro[pl.ds(m, 8, stride=17), :] for m in range(16)]
    for m, val in enumerate(turned(x, (turn & 1) != 0, (turn & 2) != 0, (turn & 4) != 0)):
        y[9 * m : 9 * m + 8, :] = val
    face = jnp.where(live, jnp.broadcast_to(info[0:1, :], (16, LANES)) >> 8, -1)
    axis_is = (face < 2, (face >= 2) & (face < 4))
    half_sign = jnp.where((face & 1) != 0, 0.5, -0.5)
    behind = [y[pl.ds(v, 16, stride=9), :] for v in range(VARS)]
    here = [inner[16 * v : 16 * v + 16, :] for v in range(VARS)]
    cor = correction(here, behind, axis_is, half_sign, 0.5)
    for ref in (ex, ey, ez):
        ref[...] = jnp.zeros((ROWS, LANES), F32)
    for v in range(VARS):
        for f in range(FACES):
            put_face_rows((ex, ey, ez), None, v, f, jnp.where(face == f, cor[v], 0.0))
    return jnp.concatenate(split(ex[...] + ey[...] + ez[...]), 0)


def added(part, spread, coef_ref, scale, put):
    for h in range(2):
        lanes = slice(h * LANES, h * LANES + LANES)
        coef = scale * coef_ref[0:1, lanes]
        for v in range(VARS):
            rows = slice(v * NODES, v * NODES + NODES)
            low = slice(ROWS + v * NODES, ROWS + v * NODES + NODES)
            put(h, v, part[h, rows, :] - coef * (spread[rows, lanes] + spread[low, lanes]))


def near_kernel(
    part, g, r_a, info, meet, coef_ref, hot_ref, code_ref, parts, q, pb, unit, ro, y, ex, ey, ez, gs, g1
):
    hot = hot_ref[...]
    asked = jnp.broadcast_to(code_ref[0:1, :] >> 8, (16, LANES))
    requested(part, hot, asked, gs, g1)
    ch, cl = split(jnp.broadcast_to(LIFT * coef_ref[0:1, :], (16, EL)))
    coef = mm(ch, hot) + mm(cl, hot)
    lane = iota((16, LANES), 1)
    terms = face_terms(pltpu.roll(g[...], 64, 1), r_a[...], info, lane < 32, ro, y, ex, ey, ez)
    parts[...] = terms
    change = mm(terms, meet[...])
    ex[...] = change[0:ROWS, :] + change[ROWS : 2 * ROWS, :]
    for v in range(VARS):
        rows = slice(16 * v, 16 * v + 16)
        new = g1[rows, :] - coef * chosen(ex, asked, v)
        q[rows, :] = new
        sent = jnp.where((lane >= 64) & (lane < 96), pltpu.roll(coef, 32, 1), g[rows, :])
        pb[rows, :] = jnp.where(lane < 32, pltpu.roll(new, 96, 1), sent)
    unit[...] = coef


def pair_kernel(info, rows_ref, meet, after, pairs):
    theirs = jnp.transpose(jnp.broadcast_to(info[0:1, :].astype(F32), (LANES, LANES))).astype(I32)
    mine = jnp.broadcast_to(rows_ref[0:1, :].astype(I32), (LANES, LANES))
    row, lane = iota((LANES, LANES), 0), iota((LANES, LANES), 1)
    to_b = (lane >= 32) & (lane < 64)
    on = ((theirs & 255) == (mine & 255)) & (row >= 96) & to_b
    kept = jnp.where(to_b, 0.0, meet[...].astype(F32))
    pairs[...] = jnp.where(on, 1.0, kept).astype(BF)


def far_kernel(g, q1, unit, r_b, info, rows_ref, code_ref, pairs, e1, q, e, ro, y, ex, ey, ez):
    lane = iota((80, LANES), 1)
    mine = pltpu.roll(g[...], 64, 1)
    got = r_b[...]
    lane16 = iota((16, LANES), 1)
    to_b = (lane16 >= 32) & (lane16 < 64)
    inner, outer = jnp.where(lane < 64, mine, got), jnp.where(lane < 64, got, mine)
    terms = face_terms(inner, outer, info, to_b | (lane16 >= 96), ro, y, ex, ey, ez)
    e[...] = e1[...] + terms
    change = mm(terms, pairs[...])
    ex[...] = change[0:ROWS, :] + change[ROWS : 2 * ROWS, :]
    code = jnp.where(to_b[0:1, :], rows_ref[0:1, :].astype(I32), code_ref[0:1, :])
    face = jnp.broadcast_to(code >> 8, (16, LANES))
    coef = jnp.where(to_b, pltpu.roll(r_b[0:16, :], 96, 1), unit[...])
    for v in range(VARS):
        rows = slice(16 * v, 16 * v + 16)
        base = jnp.where(to_b, pltpu.roll(r_b[rows, :], 32, 1), q1[rows, :])
        q[rows, :] = base - coef * chosen(ex, face, v)


def last_kernel(part, q, r_a, info, ohs, coef_ref, out_hbm, ro, y, ex, ey, ez, out, sem):
    lane = iota((80, LANES), 1)
    outer = jnp.where(lane < 32, r_a[...], q[...])
    live = iota((16, LANES), 1) < 64
    parts = face_terms(pltpu.roll(q[...], 64, 1), outer, info, live, ro, y, ex, ey, ez)
    spread = mm(parts, ohs[...])
    copies = []
    for v in range(VARS):
        for h in range(2):
            lanes = slice(h * LANES, h * LANES + LANES)
            rows = slice(v * NODES, v * NODES + NODES)
            low = slice(ROWS + v * NODES, ROWS + v * NODES + NODES)
            coef = (0.5 * LIFT) * coef_ref[0:1, lanes]
            out[v, :, lanes] = part[h, rows, :] - coef * (spread[rows, lanes] + spread[low, lanes])
        copies.append(pltpu.make_async_copy(out.at[v], out_hbm.at[v], sem.at[v]))
        copies[v].start()
    for copy in copies:
        copy.wait()


def call(body, out_shape, scratch, cost, args, hbm=(), out_hbm=False):
    spec = pl.BlockSpec(memory_space=pltpu.VMEM)
    specs = []
    for i, a in enumerate(args):
        if i in hbm:
            specs.append(pl.BlockSpec(memory_space=pltpu.HBM))
        elif a.dtype == I32 and a.ndim == 1:
            specs.append(pl.BlockSpec(memory_space=pltpu.SMEM))
        else:
            specs.append(spec)
    return pl.pallas_call(
        body,
        out_shape=out_shape,
        in_specs=specs,
        out_specs=pl.BlockSpec(memory_space=pltpu.HBM)
        if out_hbm
        else jax.tree.map(lambda _: spec, out_shape),
        scratch_shapes=scratch,
        cost_estimate=pl.CostEstimate(flops=cost, bytes_accessed=cost, transcendentals=0),
        compiler_params=pltpu.CompilerParams(vmem_limit_bytes=32 * 1024 * 1024),
    )(*[pltpu.with_memory_space_constraint(a, pltpu.HBM) if i in hbm else a for i, a in enumerate(args)])


def shape(*dims, dtype=F32):
    return jax.ShapeDtypeStruct(dims, dtype)


def per_device(sizes, old_state, element_size, old_start, neighbour, orientation):
    n = sizes[0] * sizes[1] * sizes[2]
    pairs_a = [(i, i ^ 1) for i in range(n)]
    pairs_b = [(i, (i + 1) % n if i % 2 else (i - 1) % n) for i in range(n)]

    size = element_size.reshape(1, EL)
    deriv = jnp.asarray(node_derivatives())
    s_a, s_b, rows, col, old_v, nb_v, ori_v, edge = call(
        functools.partial(send_kernel, sizes),
        (
            shape(ROWS + 16, LANES),
            shape(ROWS, LANES),
            shape(16, LANES),
            shape(64, LANES),
            shape(*old_state.shape),
            shape(FACES, EL, dtype=I32),
            shape(FACES, EL, dtype=I32),
            shape(8, LANES, dtype=I32),
        ),
        [
            pltpu.VMEM((16, EL), F32),
            pltpu.SMEM(old_start.shape, I32),
            pltpu.SemaphoreType.DMA((4,)),
        ],
        10000,
        (old_start, old_state, neighbour, orientation),
        hbm=(0, 1, 2, 3),
    )
    r_a = lax.ppermute(s_a, AXES, pairs_a)
    c_b = lax.ppermute(rows, AXES, pairs_b)
    r_b = lax.ppermute(s_b, AXES, pairs_b[1:-1])
    own, ohs, dd, coef = call(
        functools.partial(own_kernel, sizes),
        (
            shape(2, ROWS, LANES),
            shape(LANES, EL, dtype=BF),
            shape(2 * NODES, 3 * NODES, dtype=BF),
            shape(1, EL),
        ),
        [
            pltpu.VMEM((NODES, 3 * NODES), F32),
            pltpu.VMEM((1, EL), F32),
            pltpu.SMEM(old_start.shape, I32),
            pltpu.SemaphoreType.DMA((3,)),
        ],
        10000,
        (old_start, old_v, col, deriv, size),
        hbm=(0, 3, 4),
    )
    table = pltpu.VMEM((ROWS, LANES), F32)
    square = pltpu.VMEM((LANES + 24, LANES), F32)
    traces = shape(80, LANES)
    state = shape(2, ROWS, LANES)
    fld, hot, code, info, meet, g = call(
        functools.partial(join_kernel, sizes),
        (
            state,
            shape(EL, LANES, dtype=BF),
            shape(8, LANES, dtype=I32),
            shape(16, LANES, dtype=I32),
            shape(LANES, LANES, dtype=BF),
            traces,
        ),
        [table],
        10000,
        (own, r_a, r_b, c_b, rows, edge, col),
    )

    def local(last, *args):
        faces = pltpu.VMEM((VARS * TABLE + 8, LANES), F32)
        both = pltpu.VMEM((2, ROWS, LANES), F32)
        return call(
            functools.partial(local_kernel, sizes, last),
            state,
            [both] * 4 + [faces] * 5 + [pltpu.VMEM((32, LANES), I32)] + ([both] if last else []),
            20000,
            args,
        )

    r_a = lax.ppermute(g, AXES, pairs_a)
    part = local(False, fld, nb_v, ori_v, coef, dd)
    terms = shape(2 * ROWS, LANES, dtype=BF)
    scratch = [square, square, table, table, table]
    e1, q1, pb, unit = call(
        near_kernel,
        (terms, traces, traces, shape(16, LANES)),
        scratch + [table, pltpu.VMEM((80, LANES), F32)],
        10000,
        (part, g, r_a, info, meet, coef, hot, code),
    )
    r_b = lax.ppermute(pb, AXES, pairs_b)
    pairs = call(
        pair_kernel, shape(LANES, LANES, dtype=BF), [], 10000, (info, rows, meet, q1)
    )
    q, e = call(
        far_kernel,
        (traces, terms),
        scratch,
        10000,
        (g, q1, unit, r_b, info, rows, code, pairs, e1),
    )
    r_a = lax.ppermute(q, AXES, pairs_a)
    part = local(True, part, nb_v, ori_v, coef, dd, fld, e, ohs)
    return call(
        last_kernel,
        shape(VARS, NODES, EL),
        scratch + [pltpu.VMEM((VARS, NODES, EL), F32), pltpu.SemaphoreType.DMA((VARS,))],
        10000,
        (part, q, r_a, info, ohs, coef),
        out_hbm=True,
    )


def solution(mesh):
    sizes = tuple(mesh.shape[a] for a in AXES)
    in_specs = (P(None, None, AXES), P(AXES), P(), P(None, AXES), P(None, AXES))
    return jax.shard_map(
        functools.partial(per_device, sizes),
        mesh=mesh,
        in_specs=in_specs,
        out_specs=P(None, None, AXES),
        check_vma=False,
    )
```
